32 devices in a mesh: dp: 4 (over z), row: 2 (over core), col: 4 (over y, x).
Axes of the slice: x: 2, y: 2, z: 4, core: 2. Of those that a mesh axis runs over, the one named last changes fastest.
Arguments:
- block_input: bfloat16 [2048, 1024], P('dp', 'col'), may hold values from -6 to 6
- segments: int32 [2048], P('dp'), may hold values from 0 to 3, as said below
- positions: int32 [2048], P('dp'), may hold values from 0 to 1023, as said below
- attention_gain: float32 [1024], P('col'), may hold values from 0.25 to 1.75
- query_weight: bfloat16 [1024, 1024], P('col', 'row'), may hold values from -0.1875 to 0.1875
- key_weight: bfloat16 [1024, 512], P('col', 'row'), may hold values from -0.1875 to 0.1875
- value_weight: bfloat16 [1024, 512], P('col', 'row'), may hold values from -0.1875 to 0.1875
- query_gain: float32 [64], replicated, may hold values from 0.6 to 1.6
- key_gain: float32 [64], replicated, may hold values from 0.6 to 1.6
- output_weight: bfloat16 [1024, 1024], P('row', 'col'), may hold values from -0.75 to 0.75
- feedforward_gain: float32 [1024], P('col'), may hold values from 0.25 to 1.75
- gate_weight: bfloat16 [1024, 4608], P('col', 'row'), may hold values from -0.1875 to 0.1875
- up_weight: bfloat16 [1024, 4608], P('col', 'row'), may hold values from -0.1875 to 0.1875
- down_weight: bfloat16 [4608, 1024], P('row', 'col'), may hold values from -0.1875 to 0.1875
- cotangent: bfloat16 [2048, 1024], P('dp', 'col'), may hold values from -6 to 6
Outputs:
- block_output: bfloat16 [2048, 1024], P('dp', 'col')
- input_grad: float32 [2048, 1024], P('dp', 'col')
- attention_gain_grad: float32 [1024], P(('col', 'dp'))
- query_weight_grad: float32 [1024, 1024], P(('col', 'dp'), 'row')
- key_weight_grad: float32 [1024, 512], P(('col', 'dp'), 'row')
- value_weight_grad: float32 [1024, 512], P(('col', 'dp'), 'row')
- query_gain_grad: float32 [64], replicated
- key_gain_grad: float32 [64], replicated
- output_weight_grad: float32 [1024, 1024], P('row', ('col', 'dp'))
- feedforward_gain_grad: float32 [1024], P(('col', 'dp'))
- gate_weight_grad: float32 [1024, 4608], P(('col', 'dp'), 'row')
- up_weight_grad: float32 [1024, 4608], P(('col', 'dp'), 'row')
- down_weight_grad: float32 [4608, 1024], P('row', ('col', 'dp'))
The draws below stay inside these ranges and needn't reach their ends.
Inputs may be any that keep to these rules, and one draw needn't show every extreme that they name: `segments`: a document is a run of consecutive tokens that may run across sequences; whole documents have max(2, 200) to min(2000, 1024) tokens; the first document is cut at its start and may be shorter, the second has the most, the last may be cut, and a fourth document always begins; documents are numbered 0, 1, 2, 3, 0, 1, ... in order, so tokens of one sequence share a number exactly when they belong to one document. `positions`: the number of earlier tokens of the same document, counted across sequences and including tokens of a cut first document that lie before the first token.
All inputs are finite; a program needn't handle non-finite values.
Results may differ from the reference program's by a relative error of at most 0.017.
Values may be sent and summed in bfloat16 or wider, within the bound.
No kernel may reach another device: no remote copies, remote signals or barrier semaphores. Data moves between devices by JAX's collectives and lax.ppermute only.
A program may use at most 128 MiB of HBM per device.

```python
import jax
import jax.numpy as jnp
from jax import lax

D = 1024
HEADS = 16
KV = 8
HD = 64
FF = 4608
SEQ = 512
QW = 1024
KVW = 512
TOKENS = 2048


def document_layout(key):
    shortest = max(2, SEQ * 200 // 512)
    longest = min(SEQ * 2000 // 512, TOKENS // 2)
    number = TOKENS // shortest + 3
    lengths = jax.random.randint(jax.random.fold_in(key, 11), (number,), shortest, longest + 1)
    near_lengths = jax.random.randint(jax.random.fold_in(key, 17), (2,), shortest, 2 * shortest + 1)
    first_full = lengths[0]
    first_cap = TOKENS - longest - 4 * shortest - 1
    low_offset = jnp.maximum(first_full - first_cap, 0)
    offset = jax.random.randint(jax.random.fold_in(key, 13), (), low_offset, first_full)
    lengths = lengths.at[0].set(first_full - offset)
    lengths = lengths.at[1].set(longest)
    lengths = lengths.at[2].set(near_lengths[0])
    lengths = lengths.at[3].set(near_lengths[1])
    end_points = jnp.cumsum(lengths)
    starts = end_points - lengths
    token_index = jnp.arange(TOKENS)
    owner_index = jnp.sum((end_points[None, :] <= token_index[:, None]).astype(jnp.int32), axis=1)
    shifted = jnp.where(owner_index == 0, offset, 0)
    return ((owner_index % 4).astype(jnp.int32), (token_index - starts[owner_index] + shifted).astype(jnp.int32))


def draw_segments(key, part):
    return document_layout(key)[0]


def draw_positions(key, part):
    return document_layout(key)[1]


def with_spikes(entries, stream_key, source, target, parts, factor):
    owner, partner = [(jnp.arange(entries.shape[position]) // (entries.shape[position] // parts)).reshape([-1 if axis == position else 1 for axis in range(entries.ndim)]) for position in (source, target)]
    chosen = jax.random.permutation(stream_key, parts)[partner]
    strong = (owner == chosen) | (owner == (partner + parts // 2) % parts)
    return jnp.where(strong, factor * entries, entries)


def levels(stream_key, shape, shards, low, high):
    loudness, own = 1.0, jax.random.fold_in(stream_key, 6)
    for dim, blocks in shards:
        draws = jnp.exp(jax.random.uniform(jax.random.fold_in(own, dim), (blocks,), jnp.float32, low / len(shards), high / len(shards)))
        loudness = loudness * jnp.repeat(draws, shape[dim] // blocks).reshape([-1 if axis == dim else 1 for axis in range(len(shape))])
    return loudness


def noise(key, dims, deviation, bound, cuts=(), held_as=jnp.bfloat16):
    drawn = deviation * jax.random.normal(key, dims, jnp.float32)
    if cuts:
        drawn = drawn * levels(key, dims, cuts, -0.22, 0.18)
    return jnp.clip(drawn, -bound, bound).astype(held_as)


def bell_draw_with(stream_key, dims, scale, most, split, heavy, dtype=jnp.bfloat16):
    values = scale * jax.random.normal(stream_key, dims, jnp.float32)
    if split:
        values = values * levels(stream_key, dims, split, -0.22, 0.18)
    return jnp.clip(with_spikes(values, jax.random.fold_in(stream_key, 3), *heavy), -most, most).astype(dtype)


def setup_inputs(seed: int = 0) -> dict:
    seeds = jax.random.split(jax.random.key(seed), 16)
    return {
        "block_input": bell_draw_with(seeds[0], (TOKENS, D), 1.0, 6.0, ((0, 4), (1, 4)), (0, 1, 4, 2.0)),
        "segments": draw_segments(jax.random.fold_in(seeds[15], 71), 0),
        "positions": draw_positions(jax.random.fold_in(seeds[15], 71), 0),
        "attention_gain": jnp.clip(1.0 + 0.15 * jax.random.normal(seeds[3], (D,), jnp.float32), 0.25, 1.75),
        "query_weight": noise(seeds[4], (D, QW), D ** -0.5, 0.1875, ((0, 4), (1, 2))),
        "key_weight": noise(seeds[5], (D, KVW), D ** -0.5, 0.1875, ((0, 4), (1, 2))),
        "value_weight": noise(seeds[6], (D, KVW), D ** -0.5, 0.1875, ((0, 4), (1, 2))),
        "query_gain": jnp.clip(jax.random.uniform(seeds[7], (HD,), jnp.float32, 0.6, 1.6), 0.6, 1.6),
        "key_gain": jnp.clip(jax.random.uniform(seeds[8], (HD,), jnp.float32, 0.6, 1.6), 0.6, 1.6),
        "output_weight": noise(seeds[9], (QW, D), (QW // 16) ** -0.5, 0.75, ((0, 2), (1, 4))),
        "feedforward_gain": jnp.clip(1.0 + 0.15 * jax.random.normal(seeds[10], (D,), jnp.float32), 0.25, 1.75),
        "gate_weight": noise(seeds[11], (D, FF), D ** -0.5, 0.1875, ((0, 4), (1, 2))),
        "up_weight": noise(seeds[12], (D, FF), D ** -0.5, 0.1875, ((0, 4), (1, 2))),
        "down_weight": noise(seeds[13], (FF, D), (FF // 4) ** -0.5, 0.1875, ((0, 2), (1, 4))),
        "cotangent": bell_draw_with(seeds[14], (TOKENS, D), 1.0, 6.0, ((0, 4), (1, 4)), (0, 1, 4, 2.0)),
    }


EPSILON = 1e-05
THETA = 1000000.0
NEGATIVE = -1e+30

def rope_tables(places, head_size):
    half_size = head_size // 2
    frequency = THETA ** (-(jnp.arange(half_size).astype(jnp.float32) * 2.0 / head_size))
    angles = places.astype(jnp.float32)[:, None] * frequency[None, :]
    return (jnp.cos(angles), jnp.sin(angles))

def rotate(vectors, cosine, sine_part, direction):
    half_size = vectors.shape[-1] // 2
    first_half = vectors[..., :half_size]
    second_half = vectors[..., half_size:]
    cos_rows = cosine[:, None, :]
    sin_rows = direction * sine_part[:, None, :]
    return jnp.concatenate([first_half * cos_rows - second_half * sin_rows, second_half * cos_rows + first_half * sin_rows], axis=-1)

def head_norm(values, gain):
    scale_rows = lax.rsqrt(lax.optimization_barrier(jnp.mean(values * values, axis=-1, keepdims=True)) + EPSILON)
    normal = values * scale_rows
    return (normal * gain, normal, scale_rows)

def head_norm_back(upstream, normal, scale_rows, gain):
    weighted = upstream * gain
    gain_grad = lax.optimization_barrier(jnp.sum(upstream * normal, axis=(0, 1)))
    inner = lax.optimization_barrier(jnp.mean(weighted * normal, axis=-1, keepdims=True))
    return (scale_rows * (weighted - normal * inner), gain_grad)

def scores_of(grouped, key_rounded, segment_ids):
    head_size = grouped.shape[-1]
    raw = jnp.einsum('qkgd,skd->kgqs', grouped.astype(jnp.float32), key_rounded.astype(jnp.float32)) * head_size ** (-0.5)
    places = jnp.arange(grouped.shape[0])
    allowed = (places[None, :] <= places[:, None]) & (segment_ids[None, :] == segment_ids[:, None])
    return jnp.where(allowed[None, None], raw, NEGATIVE)

def attend(query_rounded, key_rounded, value_rounded, segment_ids):
    length, heads, head_size = query_rounded.shape
    kv_heads = key_rounded.shape[1]
    grouped = query_rounded.reshape(length, kv_heads, heads // kv_heads, head_size)
    scores = scores_of(grouped, key_rounded, segment_ids)
    top_score = lax.optimization_barrier(jnp.max(scores, axis=-1, keepdims=True))
    log_total = top_score + jnp.log(lax.optimization_barrier(jnp.sum(jnp.exp(scores - top_score), axis=-1, keepdims=True)))
    prob = jnp.exp(scores - log_total).astype(jnp.bfloat16)
    context = jnp.einsum('kgqs,skd->qkgd', prob.astype(jnp.float32), value_rounded.astype(jnp.float32))
    return (context.reshape(length, heads, head_size).astype(jnp.bfloat16), log_total[..., 0])

def attend_back(query_rounded, key_rounded, value_rounded, context, context_grad, log_total, segment_ids):
    length, heads, head_size = query_rounded.shape
    kv_heads = key_rounded.shape[1]
    group_size = heads // kv_heads
    grouped = query_rounded.reshape(length, kv_heads, group_size, head_size)
    scores = scores_of(grouped, key_rounded, segment_ids)
    prob_float = jnp.exp(scores - log_total[..., None])
    prob = prob_float.astype(jnp.bfloat16)
    grad_grouped = context_grad.reshape(length, kv_heads, group_size, head_size).astype(jnp.float32)
    value_grad = jnp.einsum('kgqs,qkgd->skd', prob.astype(jnp.float32), grad_grouped)
    prob_grad = jnp.einsum('qkgd,skd->kgqs', grad_grouped, value_rounded.astype(jnp.float32))
    context_grouped = context.reshape(length, kv_heads, group_size, head_size).astype(jnp.float32)
    delta_rows = lax.optimization_barrier(jnp.sum(grad_grouped * context_grouped, axis=-1)).transpose(1, 2, 0)
    score_grad = (prob_float * (prob_grad - delta_rows[..., None]) * head_size ** (-0.5)).astype(jnp.bfloat16)
    query_grad = jnp.einsum('kgqs,skd->qkgd', score_grad.astype(jnp.float32), key_rounded.astype(jnp.float32))
    key_grad = jnp.einsum('kgqs,qkgd->skd', score_grad.astype(jnp.float32), grouped.astype(jnp.float32))
    return (query_grad.reshape(length, heads, head_size), key_grad, value_grad)

def matmul(left, right):
    return jnp.dot(left, right, preferred_element_type=jnp.float32)

def reference(block_input, segments, positions, attention_gain, query_weight, key_weight, value_weight, query_gain, key_gain, output_weight, feedforward_gain, gate_weight, up_weight, down_weight, cotangent):
    number = block_input.shape[0] // SEQ
    width = block_input.shape[1]
    inputs = (block_input.reshape(number, SEQ, width), segments.reshape(number, SEQ), positions.reshape(number, SEQ), cotangent.reshape(number, SEQ, width))
    weights = (attention_gain, query_weight, key_weight, value_weight, query_gain, key_gain, output_weight, feedforward_gain, gate_weight, up_weight, down_weight)
    zero_grads = tuple((jnp.zeros(weight.shape, jnp.float32) for weight in weights))

    def one_sequence(totals, item):
        rows, segment_ids, places, upstream = item
        rows_float = rows.astype(jnp.float32)
        root_one = lax.rsqrt(lax.optimization_barrier(jnp.mean(rows_float * rows_float, axis=1, keepdims=True)) + EPSILON)
        normal_one = rows_float * root_one
        normed_one = (normal_one * attention_gain).astype(jnp.bfloat16)
        query_proj = matmul(normed_one, query_weight).reshape(SEQ, HEADS, HD)
        key_proj = matmul(normed_one, key_weight).reshape(SEQ, KV, HD)
        value_rounded = matmul(normed_one, value_weight).reshape(SEQ, KV, HD).astype(jnp.bfloat16)
        query_normed, query_hat, query_scale = head_norm(query_proj, query_gain)
        key_normed, key_hat, key_scale = head_norm(key_proj, key_gain)
        cosine, sine_part = rope_tables(places, HD)
        query_turned = rotate(query_normed, cosine, sine_part, 1.0).astype(jnp.bfloat16)
        key_turned = rotate(key_normed, cosine, sine_part, 1.0).astype(jnp.bfloat16)
        context, log_total = attend(query_turned, key_turned, value_rounded, segment_ids)
        context_flat = context.reshape(SEQ, QW)
        first_sum = rows_float + matmul(context_flat, output_weight)
        root_two = lax.rsqrt(lax.optimization_barrier(jnp.mean(first_sum * first_sum, axis=1, keepdims=True)) + EPSILON)
        normal_two = first_sum * root_two
        normed_two = (normal_two * feedforward_gain).astype(jnp.bfloat16)
        gate_pre = matmul(normed_two, gate_weight)
        up_pre = matmul(normed_two, up_weight)
        sigmoid_gate = jax.nn.sigmoid(gate_pre)
        silu_gate = gate_pre * sigmoid_gate
        hidden = (silu_gate * up_pre).astype(jnp.bfloat16)
        result = (first_sum + matmul(hidden, down_weight)).astype(jnp.bfloat16)
        upstream_float = upstream.astype(jnp.float32)
        down_grad = matmul(hidden.T, upstream)
        hidden_grad = matmul(upstream, down_weight.T)
        gate_grad = (hidden_grad * up_pre * sigmoid_gate * (1.0 + gate_pre * (1.0 - sigmoid_gate))).astype(jnp.bfloat16)
        up_grad = (hidden_grad * silu_gate).astype(jnp.bfloat16)
        gate_weight_grad = matmul(normed_two.T, gate_grad)
        up_weight_grad = matmul(normed_two.T, up_grad)
        normed_two_grad = matmul(gate_grad, gate_weight.T) + matmul(up_grad, up_weight.T)
        weighted_two = normed_two_grad * feedforward_gain
        feedforward_part = lax.optimization_barrier(jnp.sum(normed_two_grad * normal_two, axis=0))
        first_grad = upstream_float + root_two * (weighted_two - normal_two * lax.optimization_barrier(jnp.mean(weighted_two * normal_two, axis=1, keepdims=True)))
        first_rounded = first_grad.astype(jnp.bfloat16)
        output_weight_grad = matmul(context_flat.T, first_rounded)
        context_grad = matmul(first_rounded, output_weight.T).astype(jnp.bfloat16).reshape(SEQ, HEADS, HD)
        turned_query_grad, turned_key_grad, value_grad = attend_back(query_turned, key_turned, value_rounded, context, context_grad, log_total, segment_ids)
        normed_query_grad = rotate(turned_query_grad, cosine, sine_part, -1.0)
        normed_key_grad = rotate(turned_key_grad, cosine, sine_part, -1.0)
        query_grad, query_gain_part = head_norm_back(normed_query_grad, query_hat, query_scale, query_gain)
        key_grad, key_gain_part = head_norm_back(normed_key_grad, key_hat, key_scale, key_gain)
        query_rounded = query_grad.reshape(SEQ, QW).astype(jnp.bfloat16)
        key_rounded = key_grad.reshape(SEQ, KVW).astype(jnp.bfloat16)
        value_grad_rounded = value_grad.reshape(SEQ, KVW).astype(jnp.bfloat16)
        query_weight_grad = matmul(normed_one.T, query_rounded)
        key_weight_grad = matmul(normed_one.T, key_rounded)
        value_weight_grad = matmul(normed_one.T, value_grad_rounded)
        normed_one_grad = matmul(query_rounded, query_weight.T) + matmul(key_rounded, key_weight.T) + matmul(value_grad_rounded, value_weight.T)
        weighted_one = normed_one_grad * attention_gain
        attention_part = lax.optimization_barrier(jnp.sum(normed_one_grad * normal_one, axis=0))
        input_rows = first_grad + root_one * (weighted_one - normal_one * lax.optimization_barrier(jnp.mean(weighted_one * normal_one, axis=1, keepdims=True)))
        terms = (attention_part, query_weight_grad, key_weight_grad, value_weight_grad, query_gain_part, key_gain_part, output_weight_grad, feedforward_part, gate_weight_grad, up_weight_grad, down_grad)
        new_totals = tuple((total + term for total, term in zip(totals, terms)))
        return (new_totals, (result, input_rows))
    totals, (outputs, input_grads) = lax.scan(one_sequence, zero_grads, inputs)
    return (outputs.reshape(number * SEQ, width), input_grads.reshape(number * SEQ, width), totals[0], totals[1], totals[2], totals[3], totals[4], totals[5], totals[6], totals[7], totals[8], totals[9], totals[10])
```

```python
import jax
import jax.numpy as jnp
from jax import lax
from jax.sharding import PartitionSpec as P

EPSILON = 1e-05
THETA = 1000000.0
NEGATIVE = -1e30


F32 = jnp.float32
BF16 = jnp.bfloat16


def matmul(left, right):
    return jnp.dot(left, right, preferred_element_type=F32)


def matmul_nt(left, right):
    return lax.dot_general(left, right, (((1,), (1,)), ((), ())), preferred_element_type=F32)


def matmul_tn(left, right):
    return lax.dot_general(left, right, (((0,), (0,)), ((), ())), preferred_element_type=F32)


def flip(values, axis, distance):
    size = lax.axis_size(axis)
    return lax.ppermute(values, axis, [(i, i ^ distance) for i in range(size)])


def spread(values):
    return [values] + [flip(values, "col", k) for k in range(1, lax.axis_size("col"))]


def exchange(pieces):
    return [pieces[0]] + [flip(pieces[k], "col", k) for k in range(1, len(pieces))]


def total(parts):
    result = parts[0].astype(F32)
    for part in parts[1:]:
        result = result + part.astype(F32)
    return result


def after(values, gate):
    return lax.optimization_barrier((values, gate))[0]


def rope_tables(places, head_size):
    half_size = head_size // 2
    frequency = THETA ** (-(jnp.arange(half_size).astype(F32) * 2.0 / head_size))
    angles = places.astype(F32)[:, None] * frequency[None, :]
    return (jnp.cos(angles), jnp.sin(angles))


def rotate(vectors, cosine, sine_part, direction):
    half_size = vectors.shape[-1] // 2
    first_half = vectors[..., :half_size]
    second_half = vectors[..., half_size:]
    sin_rows = direction * sine_part
    return jnp.concatenate(
        [
            first_half * cosine - second_half * sin_rows,
            second_half * cosine + first_half * sin_rows,
        ],
        axis=-1,
    )


def head_norm(values, gain):
    scale_rows = lax.rsqrt(jnp.mean(values * values, axis=-1, keepdims=True) + EPSILON)
    normal = values * scale_rows
    return (normal * gain, normal, scale_rows)


def head_norm_back(upstream, normal, scale_rows, gain):
    weighted = upstream * gain
    gain_grad = jnp.sum(upstream * normal, axis=tuple(range(upstream.ndim - 1)))
    inner = jnp.mean(weighted * normal, axis=-1, keepdims=True)
    return (scale_rows * (weighted - normal * inner), gain_grad)


def body(
    block_input,
    segments,
    positions,
    attention_gain,
    query_weight,
    key_weight,
    value_weight,
    query_gain,
    key_gain,
    output_weight,
    feedforward_gain,
    gate_weight,
    up_weight,
    down_weight,
    cotangent,
):
    tokens = block_input.shape[0]
    part = block_input.shape[1]
    head = query_gain.shape[0]
    cols = lax.axis_size("col")
    planes = lax.axis_size("dp")
    width = part * cols
    half = tokens // 2
    row = lax.axis_index("row")
    col = lax.axis_index("col")
    plane = lax.axis_index("dp")
    kin = [col ^ k for k in range(cols)]

    def mine_first(values):
        return jnp.where(row == 0, values, jnp.roll(values, half, axis=0))

    def natural(values):
        return jnp.where(row == 0, values, jnp.roll(values, half, axis=0))

    def both_rows(values):
        return jnp.concatenate([values, flip(values, "row", 1)], axis=0)

    def swapped(values):
        return jnp.concatenate([values[half:], values[:half]], axis=0)

    def column_blocks(weight):
        size = weight.shape[1] // cols
        stacked = jnp.stack([weight[:, s * size : (s + 1) * size] for s in range(cols)])
        return [lax.dynamic_index_in_dim(stacked, kin[k], 0, keepdims=False) for k in range(cols)]

    def row_blocks(weight):
        size = weight.shape[0] // cols
        return [lax.dynamic_slice_in_dim(weight, kin[k] * size, size, 0) for k in range(cols)]

    def reordered(values, k):
        blocks = [values[:, j * part : (j + 1) * part] for j in range(cols)]
        return jnp.concatenate([blocks[k ^ j] for j in range(cols)], axis=1)

    mine = lax.dynamic_slice_in_dim(block_input, row * half, half, 0)
    input_mine = jnp.concatenate(spread(mine), axis=1)
    input_all = both_rows(input_mine)
    gains = jnp.concatenate(spread(jnp.stack([attention_gain, feedforward_gain])), axis=1)
    gain_one, gain_two = gains[0], gains[1]
    q_size, kv_size = query_weight.shape[1] // cols, key_weight.shape[1] // cols
    mixed = jnp.stack(
        [
            jnp.concatenate(
                [
                    query_weight[:, s * q_size : (s + 1) * q_size],
                    key_weight[:, s * kv_size : (s + 1) * kv_size],
                    value_weight[:, s * kv_size : (s + 1) * kv_size],
                ],
                axis=1,
            )
            for s in range(cols)
        ]
    )
    qkv_weight = jnp.concatenate(
        exchange(
            [lax.dynamic_index_in_dim(mixed, kin[k], 0, keepdims=False) for k in range(cols)]
        ),
        axis=0,
    )
    out_rows = row_blocks(after(output_weight, input_mine))
    out_near = jnp.concatenate(
        exchange(
            [jnp.concatenate([out_rows[k ^ j] for j in range(cols)], axis=0) for k in range(cols)]
        ),
        axis=1,
    )
    out_far = flip(out_near, "row", 1)
    later = after((gate_weight, up_weight, down_weight, cotangent), qkv_weight)
    gate_stored, up_stored, down_stored, cot_stored = later
    gate_mat = jnp.concatenate(exchange(column_blocks(gate_stored)), axis=0)
    up_mat = jnp.concatenate(exchange(column_blocks(up_stored)), axis=0)
    down_mat = jnp.concatenate(exchange(row_blocks(down_stored)), axis=1)
    cot_mine = lax.dynamic_slice_in_dim(cot_stored, row * half, half, 0)
    cot_all = both_rows(jnp.concatenate(spread(cot_mine), axis=1))

    segment_ids = mine_first(segments)
    places = mine_first(positions)
    index = mine_first(jnp.arange(tokens))

    input_float = input_all.astype(F32)
    root_one = lax.rsqrt(jnp.mean(input_float * input_float, axis=1, keepdims=True) + EPSILON)
    normal_one = input_float * root_one
    normed_one = (normal_one * gain_one).astype(BF16)
    qkv = matmul(normed_one, qkv_weight)
    group = q_size // head
    query_proj = jnp.stack([qkv[:, g * head : (g + 1) * head] for g in range(group)])
    key_proj = qkv[:, q_size : q_size + head]
    value_rounded = qkv[:, q_size + head :].astype(BF16)
    query_normed, query_hat, query_scale = head_norm(query_proj, query_gain)
    key_normed, key_hat, key_scale = head_norm(key_proj, key_gain)
    cosine, sine_part = rope_tables(places, head)
    query_turned = rotate(query_normed, cosine, sine_part, 1.0).astype(BF16)
    key_turned = rotate(key_normed, cosine, sine_part, 1.0).astype(BF16)
    allowed = (index[None, :] <= index[:, None]) & (segment_ids[None, :] == segment_ids[:, None])

    def scores_of():
        raw = jnp.einsum("gqd,kd->gqk", query_turned, key_turned, preferred_element_type=F32)
        return jnp.where(allowed[None], raw * head ** (-0.5), NEGATIVE)

    scores = scores_of()
    top_score = jnp.max(scores, axis=-1, keepdims=True)
    log_total = top_score + jnp.log(jnp.sum(jnp.exp(scores - top_score), axis=-1, keepdims=True))
    prob_float = jnp.exp(scores - log_total)
    prob = prob_float.astype(BF16)
    context_heads = jnp.einsum(
        "gqk,kd->gqd", prob, value_rounded, preferred_element_type=F32
    ).astype(BF16)
    context = jnp.concatenate([context_heads[g] for g in range(group)], axis=1)

    context_near = jnp.concatenate(spread(context), axis=1)
    context_far = swapped(flip(context_near, "row", 1))
    first_sum = input_float + matmul(context_near, out_near) + matmul(context_far, out_far)

    root_two = lax.rsqrt(jnp.mean(first_sum * first_sum, axis=1, keepdims=True) + EPSILON)
    normal_two = first_sum * root_two
    normed_two = (normal_two * gain_two).astype(BF16)
    gate_pre = matmul(normed_two, gate_mat)
    up_pre = matmul(normed_two, up_mat)
    sigmoid_gate = jax.nn.sigmoid(gate_pre)
    silu_gate = gate_pre * sigmoid_gate
    hidden = (silu_gate * up_pre).astype(BF16)
    hidden_grad = matmul_nt(cot_all, down_mat)
    gate_grad = (
        hidden_grad * up_pre * sigmoid_gate * (1.0 + gate_pre * (1.0 - sigmoid_gate))
    ).astype(BF16)
    up_grad = (hidden_grad * silu_gate).astype(BF16)
    two_part = (matmul_nt(gate_grad, gate_mat) + matmul_nt(up_grad, up_mat)).astype(BF16)

    two_half = two_part[:half].astype(F32) + flip(two_part[half:], "row", 1).astype(F32)
    share = half // cols
    two_half = two_half.astype(BF16)
    two_grad = total(
        exchange([reordered(block, k) for k, block in enumerate(row_blocks(two_half))])
    )
    own = [lax.dynamic_slice_in_dim(v, col * share, share, 0) for v in (normal_two, root_two, cot_all)]
    normal_own, root_own, cot_own = own
    weighted_two = two_grad * gain_two
    feedforward_part = jnp.sum(two_grad * normal_own, axis=0)
    inner_two = jnp.mean(weighted_two * normal_own, axis=1, keepdims=True)
    first_own = (
        cot_own.astype(F32) + root_own * (weighted_two - normal_own * inner_two)
    ).astype(BF16)
    first_parts = jnp.stack(exchange([reordered(first_own, k) for k in range(cols)]))
    first_half = jnp.concatenate(
        [lax.dynamic_index_in_dim(first_parts, kin[s], 0, keepdims=False) for s in range(cols)],
        axis=0,
    )
    first_rounded = both_rows(first_half)

    def summed(grad):
        rows = part // planes
        split = grad.astype(BF16).reshape(cols, planes, rows, grad.shape[1])
        if planes != 4:
            split = jnp.moveaxis(split, 1, 0)
            return lax.psum_scatter(split, "dp", scatter_dimension=0, tiled=True)[0]
        pieces = [
            lax.dynamic_index_in_dim(split, plane ^ m, 1, keepdims=False) for m in range(planes)
        ]
        return total([pieces[0]] + [flip(pieces[m], "dp", m) for m in range(1, planes)]).astype(
            BF16
        )

    def arranged(sums):
        parts = jnp.stack(exchange([sums[k] for k in range(cols)]))
        return [
            lax.dynamic_index_in_dim(parts, kin[s], 0, keepdims=False).astype(F32)
            for s in range(cols)
        ]

    down_share = jnp.concatenate(arranged(summed(matmul_tn(cot_all, hidden))), axis=1)
    gate_share = jnp.concatenate(arranged(summed(matmul_tn(normed_two, gate_grad))), axis=1)
    up_share = jnp.concatenate(arranged(summed(matmul_tn(normed_two, up_grad))), axis=1)

    result_part = matmul(hidden, down_mat).astype(BF16)
    result_half = (
        result_part[:half].astype(F32) + flip(result_part[half:], "row", 1).astype(F32)
    ).astype(BF16)
    result_mine = (
        first_sum[:half, :part]
        + total(exchange([result_half[:, k * part : (k + 1) * part] for k in range(cols)]))
    ).astype(BF16)
    block_output = natural(both_rows(result_mine))

    context_grad = matmul_nt(first_rounded, out_near[:q_size]).astype(BF16)
    grad_heads = jnp.stack([context_grad[:, g * head : (g + 1) * head] for g in range(group)])
    value_grad = jnp.einsum("gqk,gqd->kd", prob, grad_heads, preferred_element_type=F32)
    prob_grad = jnp.einsum("gqd,kd->gqk", grad_heads, value_rounded, preferred_element_type=F32)
    delta_rows = jnp.sum(
        grad_heads.astype(F32) * context_heads.astype(F32), axis=-1, keepdims=True
    )
    score_grad = (prob_float * (prob_grad - delta_rows) * head ** (-0.5)).astype(BF16)
    turned_query_grad = jnp.einsum(
        "gqk,kd->gqd", score_grad, key_turned, preferred_element_type=F32
    )
    turned_key_grad = jnp.einsum(
        "gqk,gqd->kd", score_grad, query_turned, preferred_element_type=F32
    )
    normed_query_grad = rotate(turned_query_grad, cosine, sine_part, -1.0)
    normed_key_grad = rotate(turned_key_grad, cosine, sine_part, -1.0)
    query_grad, query_gain_part = head_norm_back(
        normed_query_grad, query_hat, query_scale, query_gain
    )
    key_grad, key_gain_part = head_norm_back(normed_key_grad, key_hat, key_scale, key_gain)
    qkv_grad = jnp.concatenate(
        [query_grad[g] for g in range(group)] + [key_grad, value_grad], axis=1
    ).astype(BF16)
    one_part = matmul_nt(qkv_grad, qkv_weight)
    attention_part = jnp.sum(one_part * normal_one, axis=0)
    inner_part = jnp.sum(one_part * (normal_one * gain_one), axis=1) / width
    one_rounded = one_part.astype(BF16)
    one_half = (
        one_rounded[:half].astype(F32) + flip(one_rounded[half:], "row", 1).astype(F32)
    ).astype(BF16)
    inner_half = inner_part[:half] + flip(inner_part[half:], "row", 1)
    one_grad = total(exchange([one_half[:, k * part : (k + 1) * part] for k in range(cols)]))
    inner_one = total(spread(inner_half))[:, None]
    weighted_one = one_grad * gain_one[:part]
    input_mine_grad = first_rounded[:half, :part].astype(F32) + root_one[:half] * (
        weighted_one - normal_one[:half, :part] * inner_one
    )
    input_grad = natural(both_rows(input_mine_grad))

    mixed_grad = jnp.concatenate(
        [matmul_tn(normed_one, qkv_grad), matmul_tn(first_rounded, context)], axis=1
    )
    mixed_share = arranged(summed(mixed_grad))
    query_share = jnp.concatenate([v[:, :q_size] for v in mixed_share], axis=1)
    key_share = jnp.concatenate([v[:, q_size : q_size + head] for v in mixed_share], axis=1)
    value_share = jnp.concatenate(
        [v[:, q_size + head : q_size + 2 * head] for v in mixed_share], axis=1
    )
    output_share = jnp.concatenate([v[:, q_size + 2 * head :] for v in mixed_share], axis=1)

    gain_parts = jnp.stack([attention_part, feedforward_part]).reshape(2, cols, part)
    gain_parts = jnp.stack(
        [lax.dynamic_index_in_dim(gain_parts, kin[s], 1, keepdims=False) for s in range(cols)],
        axis=1,
    ).reshape(-1)
    sums = lax.psum(
        jnp.concatenate([gain_parts, query_gain_part, key_gain_part]), ("dp", "row", "col")
    )
    size = part // planes
    offset = col * part + plane * size
    attention_share = lax.dynamic_slice_in_dim(sums, offset, size, 0)
    feedforward_share = lax.dynamic_slice_in_dim(sums, width + offset, size, 0)
    query_gain_grad = sums[2 * width : 2 * width + head]
    key_gain_grad = sums[2 * width + head :]
    return (
        block_output,
        input_grad,
        attention_share,
        query_share,
        key_share,
        value_share,
        query_gain_grad,
        key_gain_grad,
        output_share.T,
        feedforward_share,
        gate_share,
        up_share,
        down_share.T,
    )


def solution(mesh):
    placed = (
        P("dp", "col"),
        P("dp"),
        P("dp"),
        P("col"),
        P("col", "row"),
        P("col", "row"),
        P("col", "row"),
        P(),
        P(),
        P("row", "col"),
        P("col"),
        P("col", "row"),
        P("col", "row"),
        P("row", "col"),
        P("dp", "col"),
    )
    return jax.shard_map(
        body,
        mesh=mesh,
        in_specs=placed,
        out_specs=(
            P("dp", "col"),
            P("dp", "col"),
            P(("col", "dp")),
            P(("col", "dp"), "row"),
            P(("col", "dp"), "row"),
            P(("col", "dp"), "row"),
            P(),
            P(),
            P("row", ("col", "dp")),
            P(("col", "dp")),
            P(("col", "dp"), "row"),
            P(("col", "dp"), "row"),
            P("row", ("col", "dp")),
        ),
        check_vma=False,
    )
```

```python
import jax
import jax.numpy as jnp
from jax import lax
from jax.experimental import pallas as pl
from jax.experimental.pallas import tpu as pltpu
from jax.sharding import PartitionSpec as P


EPSILON = 1e-05
THETA = 1000000.0
NEGATIVE = -1e30


F32 = jnp.float32
BF16 = jnp.bfloat16


def matmul(left, right):
    return jnp.dot(left, right, preferred_element_type=F32)


def matmul_nt(left, right):
    return lax.dot_general(left, right, (((1,), (1,)), ((), ())), preferred_element_type=F32)


def matmul_tn(left, right):
    return lax.dot_general(left, right, (((0,), (0,)), ((), ())), preferred_element_type=F32)


def flip(values, axis, distance):
    size = lax.axis_size(axis)
    return lax.ppermute(values, axis, [(i, i ^ distance) for i in range(size)])


def spread(values):
    return [values] + [flip(values, "col", k) for k in range(1, lax.axis_size("col"))]


def exchange(pieces):
    return [pieces[0]] + [flip(pieces[k], "col", k) for k in range(1, len(pieces))]


def total(parts):
    result = parts[0].astype(F32)
    for part in parts[1:]:
        result = result + part.astype(F32)
    return result


def kernel_call(kernel, outs, *args, scalars=None, scratch=()):
    specs = [pl.BlockSpec(memory_space=pltpu.VMEM)] * len(args)
    if scalars is not None:
        args = (scalars,) + args
        specs = [pl.BlockSpec(memory_space=pltpu.SMEM)] + specs
    return pl.pallas_call(
        kernel,
        out_shape=[jax.ShapeDtypeStruct(shape, dtype) for shape, dtype in outs],
        in_specs=specs,
        out_specs=[pl.BlockSpec(memory_space=pltpu.VMEM)] * len(outs),
        scratch_shapes=[pltpu.VMEM(shape, dtype) for shape, dtype in scratch],
        compiler_params=pltpu.CompilerParams(vmem_limit_bytes=48 * 1024 * 1024),
    )(*args)


def pack_one_kernel(where, x, gains, query, key, value, *outs):
    row, col = where[0], where[1]
    half = x.shape[0] // 2
    cols = len(outs)
    q_size, kv_size = query.shape[1] // cols, key.shape[1] // cols
    line = lax.broadcasted_iota(jnp.int32, (16, x.shape[1]), 0)
    rows = jnp.zeros((16, x.shape[1]), F32)
    for g in range(2):
        rest = gains[g : g + 1, :]
        for p in range(3):
            part = rest.astype(BF16).astype(F32)
            rows = jnp.where(line == 3 * g + p, part, rows)
            rest = rest - part
    mine = x[pl.ds(pl.multiple_of(row * half, half), half), :]
    for k, out in enumerate(outs):
        block = col ^ k
        out[:half, :] = mine
        out[half : half + 16, :] = rows.astype(BF16)
        out[half + 16 :, :q_size] = query[:, pl.ds(pl.multiple_of(block * q_size, q_size), q_size)]
        pair = pl.multiple_of((block >> 1) * (2 * kv_size), 2 * kv_size)
        odd = (block & 1) == 1
        both = []
        for weight in (key, value):
            two = weight[:, pl.ds(pair, 2 * kv_size)]
            both.append(jnp.where(odd, two[:, kv_size:], two[:, :kv_size]))
        out[half + 16 :, q_size:] = jnp.concatenate(both, axis=1)


def pack_two_kernel(where, weight, cot, *outs):
    row, col = where[0], where[1]
    half = cot.shape[0] // 2
    cols = len(outs)
    size = weight.shape[0] // cols
    for k, out in enumerate(outs):
        for j in range(cols):
            source = pl.multiple_of((col ^ (k ^ j)) * size, size)
            out[j * size : (j + 1) * size, :] = weight[pl.ds(source, size), :]
        out[cols * size :, :] = cot[pl.ds(pl.multiple_of(row * half, half), half), :]


def pack_gate_kernel(where, gate, up, *outs):
    col, odd_plane = where[1], (where[2] & 1) == 1
    cols = len(outs) - 1
    size = gate.shape[1] // cols

    def piece(weight, block):
        two = weight[:, pl.ds(pl.multiple_of((block >> 1) * (2 * size), 2 * size), 2 * size)]
        return jnp.where((block & 1) == 1, two[:, size:], two[:, :size])

    @pl.when(jnp.logical_not(odd_plane))
    def _():
        for k in range(cols):
            outs[k][...] = piece(gate, col ^ k)
        outs[cols][...] = piece(up, col)

    @pl.when(odd_plane)
    def _():
        for k in range(cols):
            outs[k][...] = piece(up, col ^ k)
        outs[cols][...] = piece(gate, col)


def join_kernel(first0, first1, first2, first3, ready, out):
    part = first0.shape[1]
    for k, piece in enumerate((first0, first1, first2, first3)):
        out[:, k * part : (k + 1) * part] = piece[...]


def forward_kernel(
    where, mine, other, context_near, context_far, joined, joined_far,
    near0, near1, near2, near3, far0, far1, far2, far3, first0, first1, first2, first3,
    normed_out, gate_out, up_out, hidden_out, own_out, share_out, sum_scratch,
):
    buffers = (first0, first1, first2, first3)
    half, part = mine.shape[0], near0.shape[0]
    size = context_near.shape[1]
    share = share_out.shape[0]
    top = mine[...].astype(F32) + matmul(context_near[:half, :], joined[:size, :])
    top = top + matmul(context_far[half:, :], joined_far[:size, :])
    low = other[...].astype(F32) + matmul(context_near[half:, :], joined[:size, :])
    low = low + matmul(context_far[:half, :], joined_far[:size, :])
    sum_scratch[...] = top
    own_out[...] = top[:, :part]
    share_out[...] = sum_scratch[pl.ds(pl.multiple_of(where[1] * share, share), share), :]
    gain = jnp.concatenate([gain_row(buffers, half + 3, k) for k in range(len(buffers))], axis=1)
    first_pre = second_pre = None
    for i, rows in enumerate((top, low)):
        root = lax.rsqrt(jnp.mean(rows * rows, axis=1, keepdims=True) + EPSILON)
        normed_out[i * half : (i + 1) * half, :] = (rows * root * gain).astype(BF16)
    for k, (near, far) in enumerate(
        ((near0, far0), (near1, far1), (near2, far2), (near3, far3))
    ):
        block = normed_out[:, k * part : (k + 1) * part]
        one, two = matmul(block, near[...]), matmul(block, far[...])
        first_pre = one if k == 0 else first_pre + one
        second_pre = two if k == 0 else second_pre + two
    even = (where[2] & 1) == 0
    gate_pre = jnp.where(even, first_pre, second_pre)
    up_pre = jnp.where(even, second_pre, first_pre)
    gate_out[...] = gate_pre
    up_out[...] = up_pre
    hidden_out[...] = (gate_pre * (1.0 / (1.0 + jnp.exp(-gate_pre))) * up_pre).astype(BF16)


def backward_kernel(
    where, joined, joined_far, gate_in, up_in, down0, down1, down2, down3,
    near0, near1, near2, near3, far0, far1, far2, far3,
    gate_grad_out, up_grad_out, mine_out, other_out,
):
    half, part = mine_out.shape[0], near0.shape[0]
    start = joined.shape[0] - half
    parts = []
    for rows in (joined, joined_far):
        grad = None
        for k, down in enumerate((down0, down1, down2, down3)):
            term = matmul_nt(rows[start:, k * part : (k + 1) * part], down[...])
            grad = term if k == 0 else grad + term
        parts.append(grad)
    hidden_grad = jnp.concatenate(parts, axis=0)
    gate_pre, up_pre = gate_in[...], up_in[...]
    sigmoid_gate = 1.0 / (1.0 + jnp.exp(-gate_pre))
    gate_grad = (
        hidden_grad * up_pre * sigmoid_gate * (1.0 + gate_pre * (1.0 - sigmoid_gate))
    ).astype(BF16)
    up_grad = (hidden_grad * (gate_pre * sigmoid_gate)).astype(BF16)
    gate_grad_out[...] = gate_grad
    up_grad_out[...] = up_grad
    even = (where[2] & 1) == 0
    near_grad = jnp.where(even, gate_grad, up_grad)
    far_grad = jnp.where(even, up_grad, gate_grad)
    for k, (near, far) in enumerate(
        ((near0, far0), (near1, far1), (near2, far2), (near3, far3))
    ):
        block = matmul_nt(near_grad, near[...]) + matmul_nt(far_grad, far[...])
        mine_out[:, k * part : (k + 1) * part] = block[:half].astype(BF16)
        other_out[:, k * part : (k + 1) * part] = block[half:].astype(BF16)


def result_kernel(hidden, down0, down1, down2, down3, mine_out, other_out):
    half, part = mine_out.shape[0], down0.shape[1]
    for k, down in enumerate((down0, down1, down2, down3)):
        block = matmul(hidden[...], down[...])
        mine_out[:, k * part : (k + 1) * part] = block[:half].astype(BF16)
        other_out[:, k * part : (k + 1) * part] = block[half:].astype(BF16)


def deal(where, scratch, k, send, keep, rows):
    for j in range(2):
        for out, m in ((send, 1 + 2 * j), (keep, 2 * j)):
            start = pl.multiple_of((where[2] ^ m) * rows, rows)
            out[j, k, :rows, :] = scratch[pl.ds(start, rows), :]


def weight_grad_kernel(
    where, joined, joined_far, hidden, normed, gate_grad, up_grad,
    down_send, gate_send, up_send, down_keep, gate_keep, up_keep, scratch,
):
    half = hidden.shape[0] // 2
    start = joined.shape[0] - half
    cols = down_send.shape[1]
    part = joined.shape[1] // cols
    rows = down_send.shape[2]
    for k in range(cols):
        span = slice(k * part, (k + 1) * part)
        grad = matmul_tn(joined[start:, span], hidden[:half, :])
        grad = grad + matmul_tn(joined_far[start:, span], hidden[half:, :])
        scratch[...] = grad.astype(BF16)
        deal(where, scratch, k, down_send, down_keep, rows)
    for upstream, send, keep in ((gate_grad, gate_send, gate_keep), (up_grad, up_send, up_keep)):
        for k in range(cols):
            span = slice(k * part, (k + 1) * part)
            scratch[...] = matmul_tn(normed[:, span], upstream[...]).astype(BF16)
            deal(where, scratch, k, send, keep, rows)


def pack_tokens_kernel(where, ours, came, out0, out1, out2, out3, scratch):
    outs = (out0, out1, out2, out3)
    share, part = out0.shape[0], out0.shape[1] // len(outs)
    scratch[...] = (ours[...].astype(F32) + came[...].astype(F32)).astype(BF16)
    for k, out in enumerate(outs):
        rows = pl.ds(pl.multiple_of((where[1] ^ k) * share, share), share)
        for j in range(len(outs)):
            source = k ^ j
            out[:, j * part : (j + 1) * part] = scratch[rows, source * part : (source + 1) * part]


def second_norm_kernel(
    where, came0, came1, came2, came3, sums, joined, first0, first1, first2, first3,
    out0, out1, out2, out3, gain_out,
):
    buffers = (first0, first1, first2, first3)
    outs = (out0, out1, out2, out3)
    share, part = out0.shape[0], out0.shape[1] // len(outs)
    half = share * len(outs)
    grad = came0[...].astype(F32) + came1[...].astype(F32)
    grad = grad + came2[...].astype(F32) + came3[...].astype(F32)
    gain = jnp.concatenate([gain_row(buffers, half + 3, k) for k in range(len(buffers))], axis=1)
    rows = sums[...]
    root = lax.rsqrt(jnp.mean(rows * rows, axis=1, keepdims=True) + EPSILON)
    normal = rows * root
    weighted = grad * gain
    gain_out[...] = jnp.sum(grad * normal, axis=0, keepdims=True)
    inner = jnp.mean(weighted * normal, axis=1, keepdims=True)
    start = pl.multiple_of(joined.shape[0] - half + where[1] * share, share)
    cot = joined[pl.ds(start, share), :].astype(F32)
    first = (cot + root * (weighted - normal * inner)).astype(BF16)
    for k, out in enumerate(outs):
        for j in range(len(outs)):
            source = k ^ j
            out[:, j * part : (j + 1) * part] = first[:, source * part : (source + 1) * part]


def join_tokens_kernel(where, came0, came1, came2, came3, out):
    share = came0.shape[0]
    for k, came in enumerate((came0, came1, came2, came3)):
        out[pl.ds(pl.multiple_of((where[1] ^ k) * share, share), share), :] = came[...]


def pack_features_kernel(ours, came, out0, out1, out2, out3):
    part = out0.shape[1]
    for k, out in enumerate((out0, out1, out2, out3)):
        span = slice(k * part, (k + 1) * part)
        out[...] = (ours[:, span].astype(F32) + came[:, span].astype(F32)).astype(BF16)


def pack_last_kernel(ours, came, inner, inner_came, out0, out1, out2, out3):
    half, part = ours.shape[0], out0.shape[1]
    line = lax.broadcasted_iota(jnp.int32, (16, part), 0)
    rows = jnp.zeros((16, part), F32)
    rest = inner[0:1, :half] + inner_came[0:1, :]
    for p in range(3):
        piece = rest.astype(BF16).astype(F32)
        rows = jnp.where(line == p, piece, rows)
        rest = rest - piece
    for k, out in enumerate((out0, out1, out2, out3)):
        span = slice(k * part, (k + 1) * part)
        out[:half, :] = (ours[:, span].astype(F32) + came[:, span].astype(F32)).astype(BF16)
        out[half:, :] = rows.astype(BF16)


def lane_is_first(size):
    return lax.broadcasted_iota(jnp.int32, (1, 2 * size), 1) < size


def head_scale(values, first):
    size = values.shape[1] // 2
    squares = values * values
    left = jnp.sum(jnp.where(first, squares, 0.0), axis=1, keepdims=True)
    right = jnp.sum(jnp.where(first, 0.0, squares), axis=1, keepdims=True)
    return lax.rsqrt(jnp.where(first, left, right) / size + EPSILON)


def turn(values, cosine, sine):
    width = values.shape[1]
    quarter = width // 4
    lane = lax.broadcasted_iota(jnp.int32, (1, width), 1)
    low = (lane & quarter) == 0
    other = jnp.where(
        low, pltpu.roll(values, width - quarter, 1), pltpu.roll(values, quarter, 1)
    )
    return values * cosine + other * sine


def root_and_input(mine, other):
    rows = jnp.concatenate([mine[...], other[...]], axis=0).astype(F32)
    mean = jnp.mean(rows * rows, axis=1, keepdims=True)
    return rows, lax.rsqrt(mean + EPSILON)


def gain_row(buffers, start, k):
    rows = buffers[k][start : start + 16, :].astype(F32)
    return rows[0:1] + rows[1:2] + rows[2:3]


def allowed_of(down, across):
    return (across[0:1, :] <= down[:, 0:1]) & (across[1:2, :] == down[:, 1:2])


def attend_kernel(
    mine, other, first0, first1, first2, first3, cosine, sine, gains, down, across,
    qkv_out, turned_out, context_out, log_out,
):
    buffers = (first0, first1, first2, first3)
    half, part = mine.shape[0], first0.shape[1]
    rows, root = root_and_input(mine, other)
    start = half + 16
    qkv = None
    for k, buffer in enumerate(buffers):
        block = rows[:, k * part : (k + 1) * part] * root * gain_row(buffers, half, k)
        term = matmul(block.astype(BF16), buffer[start:, :])
        qkv = term if qkv is None else qkv + term
    qkv_out[...] = qkv
    two = qkv.shape[1] // 2
    size = two // 2
    first = lane_is_first(size)
    query, pair = qkv[:, :two], qkv[:, two:]
    query_turned = turn(
        query * head_scale(query, first) * gains[0:1, :], cosine[...], sine[...]
    ).astype(BF16)
    key_turned = turn(pair * head_scale(pair, first) * gains[1:2, :], cosine[...], sine[...])
    pair_rounded = jnp.where(first, key_turned, pair).astype(BF16)
    turned_out[:, :two] = query_turned
    turned_out[:, two:] = pair_rounded
    key, value = pair_rounded[:, :size], pair_rounded[:, size:]
    allowed = allowed_of(down, across)
    contexts, logs = [], []
    for h in range(2):
        raw = matmul_nt(query_turned[:, h * size : (h + 1) * size], key)
        scores = jnp.where(allowed, raw * size ** (-0.5), NEGATIVE)
        top = jnp.max(scores, axis=1, keepdims=True)
        powers = jnp.exp(scores - top)
        sums = jnp.sum(powers, axis=1, keepdims=True)
        prob = (powers * (1.0 / sums)).astype(BF16)
        contexts.append(matmul(prob, value))
        logs.append(top + jnp.log(sums))
    context_out[...] = jnp.concatenate(contexts, axis=1).astype(BF16)
    log_out[...] = jnp.where(first, logs[0], logs[1])


def attend_back_kernel(
    where, mine, other, first0, first1, first2, first3, cosine, sine, gains, down, across,
    qkv_in, turned, context_in, logs, grad_mine, grad_other, out_weight,
    gain_in, one_mine, one_other, inner_out, mixed_send, mixed_keep, mixed,
):
    buffers = (first0, first1, first2, first3)
    half, part = mine.shape[0], first0.shape[1]
    two = context_in.shape[1]
    size = two // 2
    first = lane_is_first(size)
    upstream = jnp.concatenate([grad_mine[...], grad_other[...]], axis=0)
    context = context_in[...]
    context_grad = matmul_nt(upstream, out_weight[:two, :]).astype(BF16)
    key, value = turned[:, two : two + size], turned[:, two + size :]
    allowed = allowed_of(down, across)
    products = context_grad.astype(F32) * context.astype(F32)
    query_grads = []
    key_grad = value_grad = None
    for h in range(2):
        query = turned[:, h * size : (h + 1) * size]
        grad = context_grad[:, h * size : (h + 1) * size]
        raw = matmul_nt(query, key)
        scores = jnp.where(allowed, raw * size ** (-0.5), NEGATIVE)
        prob = jnp.exp(scores - logs[:, h * size : h * size + 1])
        delta = jnp.sum(
            jnp.where(first if h == 0 else jnp.logical_not(first), products, 0.0),
            axis=1,
            keepdims=True,
        )
        value_term = matmul_tn(prob.astype(BF16), grad)
        score_grad = (prob * (matmul_nt(grad, value) - delta) * size ** (-0.5)).astype(BF16)
        query_grads.append(matmul(score_grad, key))
        key_term = matmul_tn(score_grad, query)
        key_grad = key_term if h == 0 else key_grad + key_term
        value_grad = value_term if h == 0 else value_grad + value_term
    pieces, head_parts = [], []
    for i, grad in enumerate(
        (jnp.concatenate(query_grads, axis=1), jnp.concatenate([key_grad, value_grad], axis=1))
    ):
        normed = turn(grad, cosine[...], -sine[...])
        proj = qkv_in[:, i * two : (i + 1) * two]
        scale = head_scale(proj, first)
        hat = proj * scale
        weighted = normed * gains[i : i + 1, :]
        product = weighted * hat
        left = jnp.sum(jnp.where(first, product, 0.0), axis=1, keepdims=True)
        right = jnp.sum(jnp.where(first, 0.0, product), axis=1, keepdims=True)
        inner = jnp.where(first, left, right) / size
        result = scale * (weighted - hat * inner)
        pieces.append(result if i == 0 else jnp.where(first, result, grad))
        head_parts.append(jnp.sum(normed * hat, axis=0, keepdims=True))
    head_line = head_parts[0] + pltpu.roll(head_parts[0], size, 1)
    head_line = jnp.where(first, head_line, pltpu.roll(head_parts[1], size, 1))
    rows_here = mixed_send.shape[2] - 16
    line = lax.broadcasted_iota(jnp.int32, (16, part), 0)
    qkv_grad = jnp.concatenate(pieces, axis=1).astype(BF16)
    rows, root = root_and_input(mine, other)
    inner_sum = jnp.zeros((2 * half, 1), F32)
    for k, buffer in enumerate(buffers):
        span = slice(k * part, (k + 1) * part)
        gain = gain_row(buffers, half, k)
        hat = rows[:, span] * root
        grad = matmul_nt(qkv_grad, buffer[half + 16 :, :])
        product = grad * hat
        lines = jnp.where(line == 0, jnp.sum(product, axis=0, keepdims=True), 0.0)
        lines = jnp.where(line == 1, gain_in[:, span], lines).astype(BF16)
        inner_sum = inner_sum + jnp.sum(product * gain, axis=1, keepdims=True)
        one_mine[:, span] = grad[:half].astype(BF16)
        one_other[:, span] = grad[half:].astype(BF16)
        mixed[:, : 2 * two] = matmul_tn((hat * gain).astype(BF16), qkv_grad).astype(BF16)
        mixed[:, 2 * two :] = matmul_tn(upstream[:, span], context).astype(BF16)
        heads = jnp.broadcast_to(head_line, (16, two)).astype(BF16)
        if mixed_send.shape[0] == 2:
            deal(where, mixed, k, mixed_send, mixed_keep, rows_here)
            for out in (mixed_send, mixed_keep):
                for j in range(2):
                    out[j, k, rows_here:, : 2 * two] = lines
                    out[j, k, rows_here:, 2 * two :] = heads
        else:
            mixed_send[k, ...] = mixed[...]
            mixed_keep[k, :, : 2 * two] = lines
            mixed_keep[k, :, 2 * two :] = heads
    wide = jnp.broadcast_to(inner_sum / (part * len(buffers)), (2 * half, 128))
    inner_out[...] = jnp.transpose(wide)[:8, :]


def rope_tables(places, head_size):
    half_size = head_size // 2
    frequency = THETA ** (-(jnp.arange(half_size).astype(F32) * 2.0 / head_size))
    angles = places.astype(F32)[:, None] * frequency[None, :]
    return (jnp.cos(angles), jnp.sin(angles))


def body(
    block_input,
    segments,
    positions,
    attention_gain,
    query_weight,
    key_weight,
    value_weight,
    query_gain,
    key_gain,
    output_weight,
    feedforward_gain,
    gate_weight,
    up_weight,
    down_weight,
    cotangent,
):
    tokens = block_input.shape[0]
    part = block_input.shape[1]
    head = query_gain.shape[0]
    cols = lax.axis_size("col")
    planes = lax.axis_size("dp")
    width = part * cols
    half = tokens // 2
    row = lax.axis_index("row")
    col = lax.axis_index("col")
    plane = lax.axis_index("dp")
    kin = [col ^ k for k in range(cols)]

    def mine_first(values):
        return jnp.where(row == 0, values, jnp.roll(values, half, axis=0))

    def natural(values):
        return jnp.where(row == 0, values, jnp.roll(values, half, axis=0))

    def both_rows(values):
        return jnp.concatenate([values, flip(values, "row", 1)], axis=0)

    def chosen(blocks):
        stacked = jnp.stack(blocks)
        return [lax.dynamic_index_in_dim(stacked, kin[k], 0, keepdims=False) for k in range(cols)]

    def row_blocks(weight):
        size = weight.shape[0] // cols
        return [lax.dynamic_slice_in_dim(weight, kin[k] * size, size, 0) for k in range(cols)]

    q_size = query_weight.shape[1] // cols
    units = gate_weight.shape[1] // cols
    where = jnp.stack([row, col, plane]).astype(jnp.int32)
    shapes = [((half + 16 + part, part), BF16)] * cols
    first_in = exchange(
        kernel_call(
            pack_one_kernel,
            shapes,
            block_input,
            jnp.stack([attention_gain, feedforward_gain]),
            query_weight,
            key_weight,
            value_weight,
            scalars=where,
        ),
    )
    input_mine = jnp.concatenate([v[:half] for v in first_in], axis=1)
    gain_parts = jnp.concatenate([v[half : half + 16] for v in first_in], axis=1).astype(F32)
    gain_one = gain_parts[0] + gain_parts[1] + gain_parts[2]
    input_other = flip(input_mine, "row", 1)
    gate_in = kernel_call(
        pack_gate_kernel,
        [((part, units), BF16)] * (cols + 1),
        gate_weight,
        up_weight,
        scalars=where,
    )
    near_parts = exchange(gate_in[:cols])
    far_parts = [gate_in[cols]] + [flip(v, "dp", 1) for v in near_parts[1:]]
    second_parts = exchange(
        kernel_call(
            pack_two_kernel,
            [((output_weight.shape[0] + half, part), BF16)] * cols,
            output_weight,
            cotangent,
            scalars=where,
        ),
    )
    down_parts = exchange(row_blocks(down_weight))

    segment_ids = mine_first(segments)
    places = mine_first(positions)
    index = mine_first(jnp.arange(tokens))

    cosine, sine_part = rope_tables(places, head)
    group = q_size // head
    cos_lanes = jnp.concatenate([cosine] * (2 * group), axis=1)
    sin_lanes = jnp.concatenate([-sine_part, sine_part] * group, axis=1)
    head_gains = jnp.stack([jnp.tile(query_gain, group), jnp.tile(key_gain, group)])
    down = jnp.stack([index, segment_ids], axis=1)
    across = jnp.stack([index, segment_ids])
    common = (
        input_mine,
        input_other,
        *first_in,
        cos_lanes,
        sin_lanes,
        head_gains,
        down,
        across,
    )
    qkv, turned, context, logs = kernel_call(
        attend_kernel,
        [
            ((tokens, 2 * q_size), F32),
            ((tokens, 2 * q_size), BF16),
            ((tokens, q_size), BF16),
            ((tokens, q_size), F32),
        ],
        *common,
    )

    context_parts = spread(context)
    (second_in,) = kernel_call(
        join_kernel,
        [((output_weight.shape[0] + half, width), BF16)],
        *second_parts,
        context,
    )
    (context_near,) = kernel_call(
        join_kernel, [((tokens, output_weight.shape[0]), BF16)], *context_parts, context
    )
    second_far = flip(second_in, "row", 1)
    context_far = flip(context_near, "row", 1)

    share = half // cols
    normed_two, gate_pre, up_pre, hidden, first_block, first_share = kernel_call(
        forward_kernel,
        [
            ((tokens, width), BF16),
            ((tokens, units), F32),
            ((tokens, units), F32),
            ((tokens, units), BF16),
            ((half, part), F32),
            ((share, width), F32),
        ],
        input_mine,
        input_other,
        context_near,
        context_far,
        second_in,
        second_far,
        *near_parts,
        *far_parts,
        *first_in,
        scalars=where,
        scratch=[((half, width), F32)],
    )
    gate_grad, up_grad, two_mine, two_other = kernel_call(
        backward_kernel,
        [((tokens, units), BF16)] * 2 + [((half, width), BF16)] * 2,
        second_in,
        second_far,
        gate_pre,
        up_pre,
        *down_parts,
        *near_parts,
        *far_parts,
        scalars=where,
    )

    two_came = flip(two_other, "row", 1)
    two_pieces = kernel_call(
        pack_tokens_kernel,
        [((share, width), BF16)] * cols,
        two_mine,
        two_came,
        scalars=where,
        scratch=[((half, width), BF16)],
    )
    two_in = exchange(two_pieces)
    *first_pieces, feedforward_part = kernel_call(
        second_norm_kernel,
        [((share, width), BF16)] * cols + [((1, width), F32)],
        *two_in,
        first_share,
        second_in,
        *first_in,
        scalars=where,
    )
    (first_half,) = kernel_call(
        join_tokens_kernel,
        [((half, width), BF16)],
        *exchange(first_pieces),
        scalars=where,
    )
    first_other = flip(first_half, "row", 1)

    def summed(send, keep):
        came = flip(send, "dp", 1)
        rest = (keep[1].astype(F32) + came[1].astype(F32)).astype(BF16)
        far = flip(rest, "dp", 2)
        return total([keep[0], came[0], far]).astype(BF16)

    def scattered(split):
        return lax.psum_scatter(split, "dp", scatter_dimension=0, tiled=True)[0]

    def arranged(pieces):
        return [v.astype(F32) for v in chosen(exchange(pieces))]

    rows = part // planes
    if planes == 4:
        dealt = kernel_call(
            weight_grad_kernel,
            [((2, cols, rows, units), BF16)] * 6,
            second_in,
            second_far,
            hidden,
            normed_two,
            gate_grad,
            up_grad,
            scalars=where,
            scratch=[((part, units), BF16)],
        )
        sums = [summed(dealt[i], dealt[i + 3]) for i in range(3)]
    else:
        cot_all = jnp.concatenate([second_in[-half:], second_far[-half:]], axis=0)
        sums = [
            scattered(
                jnp.moveaxis(grad.astype(BF16).reshape(cols, planes, rows, units), 1, 0)
            )
            for grad in (
                matmul_tn(cot_all, hidden),
                matmul_tn(normed_two, gate_grad),
                matmul_tn(normed_two, up_grad),
            )
        ]
    shares = arranged([jnp.concatenate([v[k] for v in sums], axis=0) for k in range(cols)])
    down_share, gate_share, up_share = [
        jnp.concatenate([v[i * rows : (i + 1) * rows] for v in shares], axis=1) for i in range(3)
    ]

    result_mine, result_other = kernel_call(
        result_kernel, [((half, width), BF16)] * 2, hidden, *down_parts
    )
    result_came = flip(result_other, "row", 1)
    result_pieces = kernel_call(
        pack_features_kernel, [((half, part), BF16)] * cols, result_mine, result_came
    )
    result_in = exchange(result_pieces)
    result_mine = (first_block + total(result_in)).astype(BF16)
    block_output = natural(both_rows(result_mine))

    mixed_size = 3 * q_size
    if planes == 4:
        mixed_outs = [((2, cols, rows + 16, mixed_size), BF16)] * 2
    else:
        mixed_outs = [((cols, part, mixed_size), BF16), ((cols, 16, mixed_size), BF16)]
    one_mine, one_other, inner_part, mixed_first, mixed_second = kernel_call(
        attend_back_kernel,
        [((half, width), BF16), ((half, width), BF16), ((8, tokens), F32)] + mixed_outs,
        *common,
        qkv,
        turned,
        context,
        logs,
        first_half,
        first_other,
        second_in,
        feedforward_part,
        scalars=where,
        scratch=[((part, mixed_size), BF16)],
    )
    one_came = flip(one_other, "row", 1)
    inner_came = flip(inner_part[:, half:], "row", 1)
    one_pieces = kernel_call(
        pack_last_kernel,
        [((half + 16, part), BF16)] * cols,
        one_mine,
        one_came,
        inner_part,
        inner_came,
    )
    one_in = exchange(one_pieces)
    one_grad = total([v[:half] for v in one_in])
    inner_one = jnp.sum(total([v[half:] for v in one_in])[:3], axis=0)[:, None]
    weighted_one = one_grad * gain_one[:part]
    own_input = input_mine.astype(F32)
    root_one = lax.rsqrt(jnp.mean(own_input * own_input, axis=1, keepdims=True) + EPSILON)
    normal_one = own_input[:, :part] * root_one
    input_mine_grad = first_half[:, :part].astype(F32) + root_one * (
        weighted_one - normal_one * inner_one
    )
    input_grad = natural(both_rows(input_mine_grad))

    if planes == 4:
        mixed_sum = summed(mixed_first, mixed_second)
    else:
        lines = jnp.broadcast_to(mixed_second[:, None], (cols, planes, 16, mixed_size))
        blocks = mixed_first.reshape(cols, planes, rows, mixed_size)
        mixed_sum = scattered(jnp.moveaxis(jnp.concatenate([blocks, lines], axis=2), 1, 0))
    mixed_share = arranged([mixed_sum[k] for k in range(cols)])
    kv_start = q_size + head
    query_share = jnp.concatenate([v[:rows, :q_size] for v in mixed_share], axis=1)
    key_share = jnp.concatenate([v[:rows, q_size:kv_start] for v in mixed_share], axis=1)
    value_share = jnp.concatenate(
        [v[:rows, kv_start : kv_start + head] for v in mixed_share], axis=1
    )
    output_share = jnp.concatenate([v[:rows, kv_start + head :] for v in mixed_share], axis=1)
    gain_sums = total([v[rows : rows + 8] for v in mixed_share])
    gain_sums = gain_sums + flip(gain_sums, "row", 1)
    attention_share = lax.dynamic_slice_in_dim(gain_sums[0], plane * rows, rows, 0)
    feedforward_share = lax.dynamic_slice_in_dim(gain_sums[1], plane * rows, rows, 0)
    query_gain_grad = gain_sums[0, 2 * q_size : 2 * q_size + head]
    key_gain_grad = gain_sums[0, 2 * q_size + head :]
    return (
        block_output,
        input_grad,
        attention_share,
        query_share,
        key_share,
        value_share,
        query_gain_grad,
        key_gain_grad,
        output_share.T,
        feedforward_share,
        gate_share,
        up_share,
        down_share.T,
    )


def solution(mesh):
    placed = (
        P("dp", "col"),
        P("dp"),
        P("dp"),
        P("col"),
        P("col", "row"),
        P("col", "row"),
        P("col", "row"),
        P(),
        P(),
        P("row", "col"),
        P("col"),
        P("col", "row"),
        P("col", "row"),
        P("row", "col"),
        P("dp", "col"),
    )

    return jax.shard_map(
        body,
        mesh=mesh,
        in_specs=placed,
        out_specs=(
            P("dp", "col"),
            P("dp", "col"),
            P(("col", "dp")),
            P(("col", "dp"), "row"),
            P(("col", "dp"), "row"),
            P(("col", "dp"), "row"),
            P(),
            P(),
            P("row", ("col", "dp")),
            P(("col", "dp")),
            P(("col", "dp"), "row"),
            P(("col", "dp"), "row"),
            P("row", ("col", "dp")),
        ),
        check_vma=False,
    )
```

```python
import jax
import jax.numpy as jnp
from jax import lax
from jax.experimental import pallas as pl
from jax.experimental.pallas import tpu as pltpu
from jax.sharding import PartitionSpec as P


EPSILON = 1e-05
THETA = 1000000.0
NEGATIVE = -1e30


F32 = jnp.float32
BF16 = jnp.bfloat16


def matmul(left, right):
    return jnp.dot(left, right, preferred_element_type=F32)


def matmul_nt(left, right):
    return lax.dot_general(left, right, (((1,), (1,)), ((), ())), preferred_element_type=F32)


def matmul_tn(left, right):
    return lax.dot_general(left, right, (((0,), (0,)), ((), ())), preferred_element_type=F32)


def flip(values, axis, distance):
    size = lax.axis_size(axis)
    return lax.ppermute(values, axis, [(i, i ^ distance) for i in range(size)])


def spread(values):
    return [values] + [flip(values, "col", k) for k in range(1, lax.axis_size("col"))]


def exchange(pieces):
    return [pieces[0]] + [flip(pieces[k], "col", k) for k in range(1, len(pieces))]


def total(parts):
    result = parts[0].astype(F32)
    for part in parts[1:]:
        result = result + part.astype(F32)
    return result


def kernel_call(kernel, outs, *args, scalars=None, scratch=(), fetch=0):
    specs = [pl.BlockSpec(memory_space=pl.ANY)] * fetch
    specs = specs + [pl.BlockSpec(memory_space=pltpu.VMEM)] * (len(args) - fetch)
    scratch_shapes = [pltpu.VMEM(shape, dtype) for shape, dtype in scratch]
    if fetch:
        scratch_shapes = [pltpu.VMEM(v.shape, v.dtype) for v in args[:fetch]] + scratch_shapes
        scratch_shapes.append(pltpu.SemaphoreType.DMA((fetch,)))
    if scalars is not None:
        args = (scalars,) + args
        specs = [pl.BlockSpec(memory_space=pltpu.SMEM)] + specs
    return pl.pallas_call(
        kernel,
        out_shape=[jax.ShapeDtypeStruct(shape, dtype) for shape, dtype in outs],
        in_specs=specs,
        out_specs=[pl.BlockSpec(memory_space=pltpu.VMEM)] * len(outs),
        scratch_shapes=scratch_shapes,
        compiler_params=pltpu.CompilerParams(vmem_limit_bytes=48 * 1024 * 1024),
    )(*args)


def fetched(sources, targets, semaphores):
    copies = [
        pltpu.make_async_copy(source, target, semaphores.at[i])
        for i, (source, target) in enumerate(zip(sources, targets))
    ]
    for copy in copies:
        copy.start()
    for copy in copies:
        copy.wait()


def pack_one_kernel(
    where, x_in, query_in, key_in, value_in, gain_first, gain_second,
    out0, out1, out2, out3, x, query, key, value, semaphores,
):
    fetched((x_in, query_in, key_in, value_in), (x, query, key, value), semaphores)
    outs = (out0, out1, out2, out3)
    row, col = where[0], where[1]
    half = x.shape[0] // 2
    cols = len(outs)
    q_size, kv_size = query.shape[1] // cols, key.shape[1] // cols
    line = lax.broadcasted_iota(jnp.int32, (16, x.shape[1]), 0)
    rows = jnp.zeros((16, x.shape[1]), F32)
    for g, gain in enumerate((gain_first, gain_second)):
        rest = gain[...]
        for p in range(3):
            part = rest.astype(BF16).astype(F32)
            rows = jnp.where(line == 3 * g + p, part, rows)
            rest = rest - part
    mine = x[pl.ds(pl.multiple_of(row * half, half), half), :]
    for k, out in enumerate(outs):
        block = col ^ k
        out[:half, :] = mine
        out[half : half + 16, :] = rows.astype(BF16)
        out[half + 16 :, :q_size] = query[:, pl.ds(pl.multiple_of(block * q_size, q_size), q_size)]
        pair = pl.multiple_of((block >> 1) * (2 * kv_size), 2 * kv_size)
        odd = (block & 1) == 1
        both = []
        for weight in (key, value):
            two = weight[:, pl.ds(pair, 2 * kv_size)]
            both.append(jnp.where(odd, two[:, kv_size:], two[:, :kv_size]))
        out[half + 16 :, q_size:] = jnp.concatenate(both, axis=1)


def pack_two_kernel(where, weight_in, out0, out1, out2, out3, weight, semaphores):
    fetched((weight_in,), (weight,), semaphores)
    outs = (out0, out1, out2, out3)
    size = weight.shape[0] // len(outs)
    for k, out in enumerate(outs):
        for j in range(len(outs)):
            source = pl.multiple_of((where[1] ^ (k ^ j)) * size, size)
            out[j * size : (j + 1) * size, :] = weight[pl.ds(source, size), :]


def pack_three_kernel(where, down_in, cot_in, out0, out1, out2, out3, down, cot, semaphores):
    fetched((down_in, cot_in), (down, cot), semaphores)
    outs = (out0, out1, out2, out3)
    size, half = down.shape[0] // len(outs), cot.shape[0] // 2
    for k, out in enumerate(outs):
        out[:size, :] = down[pl.ds(pl.multiple_of((where[1] ^ k) * size, size), size), :]
        out[size:, :] = cot[pl.ds(pl.multiple_of(where[0] * half, half), half), :]


def pack_gate_kernel(
    where, gate_in, up_in, out0, out1, out2, out3, out4, gate, up, semaphores
):
    fetched((gate_in, up_in), (gate, up), semaphores)
    outs = (out0, out1, out2, out3, out4)
    col, odd_plane = where[1], (where[2] & 1) == 1
    cols = len(outs) - 1
    size = gate.shape[1] // cols

    def piece(weight, block):
        two = weight[:, pl.ds(pl.multiple_of((block >> 1) * (2 * size), 2 * size), 2 * size)]
        return jnp.where((block & 1) == 1, two[:, size:], two[:, :size])

    @pl.when(jnp.logical_not(odd_plane))
    def _():
        for k in range(cols):
            outs[k][...] = piece(gate, col ^ k)
        outs[cols][...] = piece(up, col)

    @pl.when(odd_plane)
    def _():
        for k in range(cols):
            outs[k][...] = piece(up, col ^ k)
        outs[cols][...] = piece(gate, col)


def join_kernel(first0, first1, first2, first3, out):
    part, size = first0.shape[1], out.shape[0]
    for k, piece in enumerate((first0, first1, first2, first3)):
        out[:, k * part : (k + 1) * part] = piece[piece.shape[0] - size :, :]


def forward_kernel(
    where, mine, other, context_near, context_far, joined, joined_far,
    near0, near1, near2, near3, far0, far1, far2, far3, first0, first1, first2, first3,
    normed_out, gate_out, up_out, hidden_out, own_out, share_out, sum_scratch,
):
    buffers = (first0, first1, first2, first3)
    half, part = mine.shape[0], near0.shape[0]
    size = context_near.shape[1]
    share = share_out.shape[0]
    top = mine[...].astype(F32) + matmul(context_near[:half, :], joined[:size, :])
    top = top + matmul(context_far[half:, :], joined_far[:size, :])
    low = other[...].astype(F32) + matmul(context_near[half:, :], joined[:size, :])
    low = low + matmul(context_far[:half, :], joined_far[:size, :])
    sum_scratch[...] = top
    own_out[...] = top[:, :part]
    share_out[...] = sum_scratch[pl.ds(pl.multiple_of(where[1] * share, share), share), :]
    gain = jnp.concatenate([gain_row(buffers, half + 3, k) for k in range(len(buffers))], axis=1)
    first_pre = second_pre = None
    for i, rows in enumerate((top, low)):
        root = lax.rsqrt(jnp.mean(rows * rows, axis=1, keepdims=True) + EPSILON)
        normed_out[i * half : (i + 1) * half, :] = (rows * root * gain).astype(BF16)
    for k, (near, far) in enumerate(
        ((near0, far0), (near1, far1), (near2, far2), (near3, far3))
    ):
        block = normed_out[:, k * part : (k + 1) * part]
        one, two = matmul(block, near[...]), matmul(block, far[...])
        first_pre = one if k == 0 else first_pre + one
        second_pre = two if k == 0 else second_pre + two
    even = (where[2] & 1) == 0
    gate_pre = jnp.where(even, first_pre, second_pre)
    up_pre = jnp.where(even, second_pre, first_pre)
    gate_out[...] = gate_pre
    up_out[...] = up_pre
    hidden_out[...] = (gate_pre * (1.0 / (1.0 + jnp.exp(-gate_pre))) * up_pre).astype(BF16)


def backward_kernel(
    where, cot_mine, cot_other, gate_in, up_in, down0, down1, down2, down3,
    near0, near1, near2, near3, far0, far1, far2, far3,
    gate_grad_out, up_grad_out, mine_out, other_out,
):
    half, part = mine_out.shape[0], near0.shape[0]
    size = gate_in.shape[1]
    parts = []
    for rows in (cot_mine, cot_other):
        grad = None
        for k, down in enumerate((down0, down1, down2, down3)):
            term = matmul_nt(rows[:, k * part : (k + 1) * part], down[:size, :])
            grad = term if k == 0 else grad + term
        parts.append(grad)
    hidden_grad = jnp.concatenate(parts, axis=0)
    gate_pre, up_pre = gate_in[...], up_in[...]
    sigmoid_gate = 1.0 / (1.0 + jnp.exp(-gate_pre))
    gate_grad = (
        hidden_grad * up_pre * sigmoid_gate * (1.0 + gate_pre * (1.0 - sigmoid_gate))
    ).astype(BF16)
    up_grad = (hidden_grad * (gate_pre * sigmoid_gate)).astype(BF16)
    gate_grad_out[...] = gate_grad
    up_grad_out[...] = up_grad
    even = (where[2] & 1) == 0
    near_grad = jnp.where(even, gate_grad, up_grad)
    far_grad = jnp.where(even, up_grad, gate_grad)
    for k, (near, far) in enumerate(
        ((near0, far0), (near1, far1), (near2, far2), (near3, far3))
    ):
        block = matmul_nt(near_grad, near[...]) + matmul_nt(far_grad, far[...])
        mine_out[:, k * part : (k + 1) * part] = block[:half].astype(BF16)
        other_out[:, k * part : (k + 1) * part] = block[half:].astype(BF16)


def result_kernel(hidden, down0, down1, down2, down3, mine_out, other_out):
    half, part = mine_out.shape[0], down0.shape[1]
    for k, down in enumerate((down0, down1, down2, down3)):
        block = matmul(hidden[...], down[: hidden.shape[1], :])
        mine_out[:, k * part : (k + 1) * part] = block[:half].astype(BF16)
        other_out[:, k * part : (k + 1) * part] = block[half:].astype(BF16)


def deal(where, scratch, k, send, keep, rows):
    for j in range(2):
        for out, m in ((send, 1 + 2 * j), (keep, 2 * j)):
            start = pl.multiple_of((where[2] ^ m) * rows, rows)
            out[j, k, :rows, :] = scratch[pl.ds(start, rows), :]


def weight_grad_kernel(
    where, cot_mine, cot_other, hidden, normed, gate_grad, up_grad,
    down_send, gate_send, up_send, down_keep, gate_keep, up_keep, scratch,
):
    half = hidden.shape[0] // 2
    cols = down_send.shape[1]
    part = cot_mine.shape[1] // cols
    rows = down_send.shape[2]
    for k in range(cols):
        span = slice(k * part, (k + 1) * part)
        grad = matmul_tn(cot_mine[:, span], hidden[:half, :])
        grad = grad + matmul_tn(cot_other[:, span], hidden[half:, :])
        scratch[...] = grad.astype(BF16)
        deal(where, scratch, k, down_send, down_keep, rows)
    for upstream, send, keep in ((gate_grad, gate_send, gate_keep), (up_grad, up_send, up_keep)):
        for k in range(cols):
            span = slice(k * part, (k + 1) * part)
            scratch[...] = matmul_tn(normed[:, span], upstream[...]).astype(BF16)
            deal(where, scratch, k, send, keep, rows)


def pack_tokens_kernel(where, ours, came, out0, out1, out2, out3, scratch):
    outs = (out0, out1, out2, out3)
    share, part = out0.shape[0], out0.shape[1] // len(outs)
    scratch[...] = (ours[...].astype(F32) + came[...].astype(F32)).astype(BF16)
    for k, out in enumerate(outs):
        rows = pl.ds(pl.multiple_of((where[1] ^ k) * share, share), share)
        for j in range(len(outs)):
            source = k ^ j
            out[:, j * part : (j + 1) * part] = scratch[rows, source * part : (source + 1) * part]


def second_norm_kernel(
    where, came0, came1, came2, came3, sums, cot_mine, first0, first1, first2, first3,
    out0, out1, out2, out3, gain_out,
):
    buffers = (first0, first1, first2, first3)
    outs = (out0, out1, out2, out3)
    share, part = out0.shape[0], out0.shape[1] // len(outs)
    half = share * len(outs)
    grad = came0[...].astype(F32) + came1[...].astype(F32)
    grad = grad + came2[...].astype(F32) + came3[...].astype(F32)
    gain = jnp.concatenate([gain_row(buffers, half + 3, k) for k in range(len(buffers))], axis=1)
    rows = sums[...]
    root = lax.rsqrt(jnp.mean(rows * rows, axis=1, keepdims=True) + EPSILON)
    normal = rows * root
    weighted = grad * gain
    gain_out[...] = jnp.sum(grad * normal, axis=0, keepdims=True)
    inner = jnp.mean(weighted * normal, axis=1, keepdims=True)
    cot = cot_mine[pl.ds(pl.multiple_of(where[1] * share, share), share), :].astype(F32)
    first = (cot + root * (weighted - normal * inner)).astype(BF16)
    for k, out in enumerate(outs):
        for j in range(len(outs)):
            source = k ^ j
            out[:, j * part : (j + 1) * part] = first[:, source * part : (source + 1) * part]


def join_tokens_kernel(where, came0, came1, came2, came3, out):
    share = came0.shape[0]
    for k, came in enumerate((came0, came1, came2, came3)):
        out[pl.ds(pl.multiple_of((where[1] ^ k) * share, share), share), :] = came[...]


def pack_features_kernel(ours, came, out0, out1, out2, out3):
    part = out0.shape[1]
    for k, out in enumerate((out0, out1, out2, out3)):
        span = slice(k * part, (k + 1) * part)
        out[...] = (ours[:, span].astype(F32) + came[:, span].astype(F32)).astype(BF16)


def pack_last_kernel(ours, came, inner, inner_came, out0, out1, out2, out3):
    half, part = ours.shape[0], out0.shape[1]
    line = lax.broadcasted_iota(jnp.int32, (16, part), 0)
    rows = jnp.zeros((16, part), F32)
    rest = inner[0:1, :half] + inner_came[0:1, :]
    for p in range(3):
        piece = rest.astype(BF16).astype(F32)
        rows = jnp.where(line == p, piece, rows)
        rest = rest - piece
    for k, out in enumerate((out0, out1, out2, out3)):
        span = slice(k * part, (k + 1) * part)
        out[:half, :] = (ours[:, span].astype(F32) + came[:, span].astype(F32)).astype(BF16)
        out[half:, :] = rows.astype(BF16)


def lane_is_first(size):
    return lax.broadcasted_iota(jnp.int32, (1, 2 * size), 1) < size


def head_scale(values, first):
    size = values.shape[1] // 2
    squares = values * values
    left = jnp.sum(jnp.where(first, squares, 0.0), axis=1, keepdims=True)
    right = jnp.sum(jnp.where(first, 0.0, squares), axis=1, keepdims=True)
    return lax.rsqrt(jnp.where(first, left, right) / size + EPSILON)


def turn(values, cosine, sine):
    width = values.shape[1]
    quarter = width // 4
    lane = lax.broadcasted_iota(jnp.int32, (1, width), 1)
    low = (lane & quarter) == 0
    other = jnp.where(
        low, pltpu.roll(values, width - quarter, 1), pltpu.roll(values, quarter, 1)
    )
    return values * cosine + other * sine


def root_and_input(mine, other):
    rows = jnp.concatenate([mine[...], other[...]], axis=0).astype(F32)
    mean = jnp.mean(rows * rows, axis=1, keepdims=True)
    return rows, lax.rsqrt(mean + EPSILON)


def gain_row(buffers, start, k):
    rows = buffers[k][start : start + 16, :].astype(F32)
    return rows[0:1] + rows[1:2] + rows[2:3]


def allowed_of(down, across):
    return (across[0:1, :] <= down[:, 0:1]) & (across[1:2, :] == down[:, 1:2])


def attend_kernel(
    mine, other, first0, first1, first2, first3, cosine, sine, gains, down, across,
    qkv_out, turned_out, context_out, log_out,
):
    buffers = (first0, first1, first2, first3)
    half, part = mine.shape[0], first0.shape[1]
    rows, root = root_and_input(mine, other)
    start = half + 16
    qkv = None
    for k, buffer in enumerate(buffers):
        block = rows[:, k * part : (k + 1) * part] * root * gain_row(buffers, half, k)
        term = matmul(block.astype(BF16), buffer[start:, :])
        qkv = term if qkv is None else qkv + term
    qkv_out[...] = qkv
    two = qkv.shape[1] // 2
    size = two // 2
    first = lane_is_first(size)
    query, pair = qkv[:, :two], qkv[:, two:]
    query_turned = turn(
        query * head_scale(query, first) * gains[0:1, :], cosine[...], sine[...]
    ).astype(BF16)
    key_turned = turn(pair * head_scale(pair, first) * gains[1:2, :], cosine[...], sine[...])
    pair_rounded = jnp.where(first, key_turned, pair).astype(BF16)
    turned_out[:, :two] = query_turned
    turned_out[:, two:] = pair_rounded
    key, value = pair_rounded[:, :size], pair_rounded[:, size:]
    allowed = allowed_of(down, across)
    contexts, logs = [], []
    for h in range(2):
        raw = matmul_nt(query_turned[:, h * size : (h + 1) * size], key)
        scores = jnp.where(allowed, raw * size ** (-0.5), NEGATIVE)
        top = jnp.max(scores, axis=1, keepdims=True)
        powers = jnp.exp(scores - top)
        sums = jnp.sum(powers, axis=1, keepdims=True)
        prob = (powers * (1.0 / sums)).astype(BF16)
        contexts.append(matmul(prob, value))
        logs.append(top + jnp.log(sums))
    context_out[...] = jnp.concatenate(contexts, axis=1).astype(BF16)
    log_out[...] = jnp.where(first, logs[0], logs[1])


def attend_back_kernel(
    where, mine, other, first0, first1, first2, first3, cosine, sine, gains, down, across,
    qkv_in, turned, context_in, logs, grad_mine, grad_other, out_weight,
    gain_in, one_mine, one_other, inner_out, mixed_send, mixed_keep, mixed,
):
    buffers = (first0, first1, first2, first3)
    half, part = mine.shape[0], first0.shape[1]
    two = context_in.shape[1]
    size = two // 2
    first = lane_is_first(size)
    upstream = jnp.concatenate([grad_mine[...], grad_other[...]], axis=0)
    context = context_in[...]
    context_grad = matmul_nt(upstream, out_weight[:two, :]).astype(BF16)
    key, value = turned[:, two : two + size], turned[:, two + size :]
    allowed = allowed_of(down, across)
    products = context_grad.astype(F32) * context.astype(F32)
    query_grads = []
    key_grad = value_grad = None
    for h in range(2):
        query = turned[:, h * size : (h + 1) * size]
        grad = context_grad[:, h * size : (h + 1) * size]
        raw = matmul_nt(query, key)
        scores = jnp.where(allowed, raw * size ** (-0.5), NEGATIVE)
        prob = jnp.exp(scores - logs[:, h * size : h * size + 1])
        delta = jnp.sum(
            jnp.where(first if h == 0 else jnp.logical_not(first), products, 0.0),
            axis=1,
            keepdims=True,
        )
        value_term = matmul_tn(prob.astype(BF16), grad)
        score_grad = (prob * (matmul_nt(grad, value) - delta) * size ** (-0.5)).astype(BF16)
        query_grads.append(matmul(score_grad, key))
        key_term = matmul_tn(score_grad, query)
        key_grad = key_term if h == 0 else key_grad + key_term
        value_grad = value_term if h == 0 else value_grad + value_term
    pieces, head_parts = [], []
    for i, grad in enumerate(
        (jnp.concatenate(query_grads, axis=1), jnp.concatenate([key_grad, value_grad], axis=1))
    ):
        normed = turn(grad, cosine[...], -sine[...])
        proj = qkv_in[:, i * two : (i + 1) * two]
        scale = head_scale(proj, first)
        hat = proj * scale
        weighted = normed * gains[i : i + 1, :]
        product = weighted * hat
        left = jnp.sum(jnp.where(first, product, 0.0), axis=1, keepdims=True)
        right = jnp.sum(jnp.where(first, 0.0, product), axis=1, keepdims=True)
        inner = jnp.where(first, left, right) / size
        result = scale * (weighted - hat * inner)
        pieces.append(result if i == 0 else jnp.where(first, result, grad))
        head_parts.append(jnp.sum(normed * hat, axis=0, keepdims=True))
    head_line = head_parts[0] + pltpu.roll(head_parts[0], size, 1)
    head_line = jnp.where(first, head_line, pltpu.roll(head_parts[1], size, 1))
    rows_here = mixed_send.shape[2] - 8
    line = lax.broadcasted_iota(jnp.int32, (8, part), 0)
    qkv_grad = jnp.concatenate(pieces, axis=1).astype(BF16)
    rows, root = root_and_input(mine, other)
    inner_sum = jnp.zeros((2 * half, 1), F32)
    for k, buffer in enumerate(buffers):
        span = slice(k * part, (k + 1) * part)
        gain = gain_row(buffers, half, k)
        hat = rows[:, span] * root
        grad = matmul_nt(qkv_grad, buffer[half + 16 :, :])
        product = grad * hat
        lines = jnp.where(line == 0, jnp.sum(product, axis=0, keepdims=True), 0.0)
        lines = jnp.where(line == 1, gain_in[:, span], lines).astype(BF16)
        inner_sum = inner_sum + jnp.sum(product * gain, axis=1, keepdims=True)
        one_mine[:, span] = grad[:half].astype(BF16)
        one_other[:, span] = grad[half:].astype(BF16)
        mixed[:, : 2 * two] = matmul_tn((hat * gain).astype(BF16), qkv_grad).astype(BF16)
        mixed[:, 2 * two :] = matmul_tn(upstream[:, span], context).astype(BF16)
        heads = jnp.broadcast_to(head_line, (8, two)).astype(BF16)
        if mixed_send.shape[0] == 2:
            deal(where, mixed, k, mixed_send, mixed_keep, rows_here)
            for out in (mixed_send, mixed_keep):
                for j in range(2):
                    out[j, k, rows_here:, : 2 * two] = lines
                    out[j, k, rows_here:, 2 * two :] = heads
        else:
            mixed_send[k, ...] = mixed[...]
            mixed_keep[k, :, : 2 * two] = lines
            mixed_keep[k, :, 2 * two :] = heads
    wide = jnp.broadcast_to(inner_sum / (part * len(buffers)), (2 * half, 128))
    inner_out[...] = jnp.transpose(wide)[:8, :]


def rope_tables(places, head_size):
    half_size = head_size // 2
    frequency = THETA ** (-(jnp.arange(half_size).astype(F32) * 2.0 / head_size))
    angles = places.astype(F32)[:, None] * frequency[None, :]
    return (jnp.cos(angles), jnp.sin(angles))


def body(
    block_input,
    segments,
    positions,
    attention_gain,
    query_weight,
    key_weight,
    value_weight,
    query_gain,
    key_gain,
    output_weight,
    feedforward_gain,
    gate_weight,
    up_weight,
    down_weight,
    cotangent,
):
    tokens = block_input.shape[0]
    part = block_input.shape[1]
    head = query_gain.shape[0]
    cols = lax.axis_size("col")
    planes = lax.axis_size("dp")
    width = part * cols
    half = tokens // 2
    row = lax.axis_index("row")
    col = lax.axis_index("col")
    plane = lax.axis_index("dp")
    kin = [col ^ k for k in range(cols)]

    def mine_first(values):
        return jnp.where(row == 0, values, jnp.roll(values, half, axis=0))

    def natural(values):
        return jnp.where(row == 0, values, jnp.roll(values, half, axis=0))

    def both_rows(values):
        return jnp.concatenate([values, flip(values, "row", 1)], axis=0)

    def chosen(blocks):
        stacked = jnp.stack(blocks)
        return [lax.dynamic_index_in_dim(stacked, kin[k], 0, keepdims=False) for k in range(cols)]

    q_size = query_weight.shape[1] // cols
    units = gate_weight.shape[1] // cols
    where = jnp.stack([row, col, plane]).astype(jnp.int32)
    shapes = [((half + 16 + part, part), BF16)] * cols
    first_in = exchange(
        kernel_call(
            pack_one_kernel,
            shapes,
            block_input,
            query_weight,
            key_weight,
            value_weight,
            attention_gain.reshape(1, part),
            feedforward_gain.reshape(1, part),
            scalars=where,
            fetch=4,
        ),
    )
    input_mine = jnp.concatenate([v[:half] for v in first_in], axis=1)
    gain_parts = jnp.concatenate([v[half : half + 16] for v in first_in], axis=1).astype(F32)
    gain_one = gain_parts[0] + gain_parts[1] + gain_parts[2]
    input_other = flip(input_mine, "row", 1)
    gate_in = kernel_call(
        pack_gate_kernel,
        [((part, units), BF16)] * (cols + 1),
        gate_weight,
        up_weight,
        scalars=where,
        fetch=2,
    )
    near_parts = exchange(gate_in[:cols])
    far_parts = [gate_in[cols]] + [flip(v, "dp", 1) for v in near_parts[1:]]
    inner_size = output_weight.shape[0]
    second_parts = exchange(
        kernel_call(
            pack_two_kernel,
            [((inner_size, part), BF16)] * cols,
            output_weight,
            scalars=where,
            fetch=1,
        ),
    )
    down_parts = exchange(
        kernel_call(
            pack_three_kernel,
            [((units + half, part), BF16)] * cols,
            down_weight,
            cotangent,
            scalars=where,
            fetch=2,
        ),
    )

    segment_ids = mine_first(segments)
    places = mine_first(positions)
    index = mine_first(jnp.arange(tokens))

    cosine, sine_part = rope_tables(places, head)
    group = q_size // head
    cos_lanes = jnp.concatenate([cosine] * (2 * group), axis=1)
    sin_lanes = jnp.concatenate([-sine_part, sine_part] * group, axis=1)
    head_gains = jnp.stack([jnp.tile(query_gain, group), jnp.tile(key_gain, group)])
    down = jnp.stack([index, segment_ids], axis=1)
    across = jnp.stack([index, segment_ids])
    common = (
        input_mine,
        input_other,
        *first_in,
        cos_lanes,
        sin_lanes,
        head_gains,
        down,
        across,
    )
    qkv, turned, context, logs = kernel_call(
        attend_kernel,
        [
            ((tokens, 2 * q_size), F32),
            ((tokens, 2 * q_size), BF16),
            ((tokens, q_size), BF16),
            ((tokens, q_size), F32),
        ],
        *common,
    )

    context_parts = spread(context)
    (context_near,) = kernel_call(join_kernel, [((tokens, inner_size), BF16)], *context_parts)
    context_far = flip(context_near, "row", 1)
    (second_in,) = kernel_call(join_kernel, [((inner_size, width), BF16)], *second_parts)
    second_far = flip(second_in, "row", 1)
    (cot_mine,) = kernel_call(join_kernel, [((half, width), BF16)], *down_parts)
    cot_other = flip(cot_mine, "row", 1)

    share = half // cols
    normed_two, gate_pre, up_pre, hidden, first_block, first_share = kernel_call(
        forward_kernel,
        [
            ((tokens, width), BF16),
            ((tokens, units), F32),
            ((tokens, units), F32),
            ((tokens, units), BF16),
            ((half, part), F32),
            ((share, width), F32),
        ],
        input_mine,
        input_other,
        context_near,
        context_far,
        second_in,
        second_far,
        *near_parts,
        *far_parts,
        *first_in,
        scalars=where,
        scratch=[((half, width), F32)],
    )
    gate_grad, up_grad, two_mine, two_other = kernel_call(
        backward_kernel,
        [((tokens, units), BF16)] * 2 + [((half, width), BF16)] * 2,
        cot_mine,
        cot_other,
        gate_pre,
        up_pre,
        *down_parts,
        *near_parts,
        *far_parts,
        scalars=where,
    )

    two_came = flip(two_other, "row", 1)
    two_pieces = kernel_call(
        pack_tokens_kernel,
        [((share, width), BF16)] * cols,
        two_mine,
        two_came,
        scalars=where,
        scratch=[((half, width), BF16)],
    )
    two_in = exchange(two_pieces)
    *first_pieces, feedforward_part = kernel_call(
        second_norm_kernel,
        [((share, width), BF16)] * cols + [((1, width), F32)],
        *two_in,
        first_share,
        cot_mine,
        *first_in,
        scalars=where,
    )
    (first_half,) = kernel_call(
        join_tokens_kernel,
        [((half, width), BF16)],
        *exchange(first_pieces),
        scalars=where,
    )
    first_other = flip(first_half, "row", 1)

    def summed(send, keep):
        came = flip(send, "dp", 1)
        rest = (keep[1].astype(F32) + came[1].astype(F32)).astype(BF16)
        far = flip(rest, "dp", 2)
        return total([keep[0], came[0], far]).astype(BF16)

    def scattered(split):
        return lax.psum_scatter(split, "dp", scatter_dimension=0, tiled=True)[0]

    def arranged(pieces):
        return [v.astype(F32) for v in chosen(exchange(pieces))]

    rows = part // planes
    if planes == 4:
        dealt = kernel_call(
            weight_grad_kernel,
            [((2, cols, rows, units), BF16)] * 6,
            cot_mine,
            cot_other,
            hidden,
            normed_two,
            gate_grad,
            up_grad,
            scalars=where,
            scratch=[((part, units), BF16)],
        )
        sums = [summed(dealt[i], dealt[i + 3]) for i in range(3)]
    else:
        cot_all = jnp.concatenate([cot_mine, cot_other], axis=0)
        sums = [
            scattered(
                jnp.moveaxis(grad.astype(BF16).reshape(cols, planes, rows, units), 1, 0)
            )
            for grad in (
                matmul_tn(cot_all, hidden),
                matmul_tn(normed_two, gate_grad),
                matmul_tn(normed_two, up_grad),
            )
        ]
    shares = arranged([jnp.concatenate([v[k] for v in sums], axis=0) for k in range(cols)])
    down_share, gate_share, up_share = [
        jnp.concatenate([v[i * rows : (i + 1) * rows] for v in shares], axis=1) for i in range(3)
    ]

    result_mine, result_other = kernel_call(
        result_kernel, [((half, width), BF16)] * 2, hidden, *down_parts
    )
    result_came = flip(result_other, "row", 1)
    result_pieces = kernel_call(
        pack_features_kernel, [((half, part), BF16)] * cols, result_mine, result_came
    )
    result_in = exchange(result_pieces)
    result_mine = (first_block + total(result_in)).astype(BF16)
    block_output = natural(both_rows(result_mine))

    mixed_size = 3 * q_size
    if planes == 4:
        mixed_outs = [((2, cols, rows + 8, mixed_size), BF16)] * 2
    else:
        mixed_outs = [((cols, part, mixed_size), BF16), ((cols, 8, mixed_size), BF16)]
    one_mine, one_other, inner_part, mixed_first, mixed_second = kernel_call(
        attend_back_kernel,
        [((half, width), BF16), ((half, width), BF16), ((8, tokens), F32)] + mixed_outs,
        *common,
        qkv,
        turned,
        context,
        logs,
        first_half,
        first_other,
        second_in,
        feedforward_part,
        scalars=where,
        scratch=[((part, mixed_size), BF16)],
    )
    one_came = flip(one_other, "row", 1)
    inner_came = flip(inner_part[:, half:], "row", 1)
    one_pieces = kernel_call(
        pack_last_kernel,
        [((half + 16, part), BF16)] * cols,
        one_mine,
        one_came,
        inner_part,
        inner_came,
    )
    one_in = exchange(one_pieces)
    one_grad = total([v[:half] for v in one_in])
    inner_one = jnp.sum(total([v[half:] for v in one_in])[:3], axis=0)[:, None]
    weighted_one = one_grad * gain_one[:part]
    own_input = input_mine.astype(F32)
    root_one = lax.rsqrt(jnp.mean(own_input * own_input, axis=1, keepdims=True) + EPSILON)
    normal_one = own_input[:, :part] * root_one
    input_mine_grad = first_half[:, :part].astype(F32) + root_one * (
        weighted_one - normal_one * inner_one
    )
    input_grad = natural(both_rows(input_mine_grad))

    if planes == 4:
        mixed_sum = summed(mixed_first, mixed_second)
    else:
        lines = jnp.broadcast_to(mixed_second[:, None], (cols, planes, 8, mixed_size))
        blocks = mixed_first.reshape(cols, planes, rows, mixed_size)
        mixed_sum = scattered(jnp.moveaxis(jnp.concatenate([blocks, lines], axis=2), 1, 0))
    mixed_share = arranged([mixed_sum[k] for k in range(cols)])
    kv_start = q_size + head
    query_share = jnp.concatenate([v[:rows, :q_size] for v in mixed_share], axis=1)
    key_share = jnp.concatenate([v[:rows, q_size:kv_start] for v in mixed_share], axis=1)
    value_share = jnp.concatenate(
        [v[:rows, kv_start : kv_start + head] for v in mixed_share], axis=1
    )
    output_share = jnp.concatenate([v[:rows, kv_start + head :] for v in mixed_share], axis=1)
    gain_sums = total([v[rows : rows + 8] for v in mixed_share])
    gain_sums = gain_sums + flip(gain_sums, "row", 1)
    attention_share = lax.dynamic_slice_in_dim(gain_sums[0], plane * rows, rows, 0)
    feedforward_share = lax.dynamic_slice_in_dim(gain_sums[1], plane * rows, rows, 0)
    query_gain_grad = gain_sums[0, 2 * q_size : 2 * q_size + head]
    key_gain_grad = gain_sums[0, 2 * q_size + head :]
    return (
        block_output,
        input_grad,
        attention_share,
        query_share,
        key_share,
        value_share,
        query_gain_grad,
        key_gain_grad,
        output_share.T,
        feedforward_share,
        gate_share,
        up_share,
        down_share.T,
    )


def solution(mesh):
    placed = (
        P("dp", "col"),
        P("dp"),
        P("dp"),
        P("col"),
        P("col", "row"),
        P("col", "row"),
        P("col", "row"),
        P(),
        P(),
        P("row", "col"),
        P("col"),
        P("col", "row"),
        P("col", "row"),
        P("row", "col"),
        P("dp", "col"),
    )


    return jax.shard_map(
        body,
        mesh=mesh,
        in_specs=placed,
        out_specs=(
            P("dp", "col"),
            P("dp", "col"),
            P(("col", "dp")),
            P(("col", "dp"), "row"),
            P(("col", "dp"), "row"),
            P(("col", "dp"), "row"),
            P(),
            P(),
            P("row", ("col", "dp")),
            P(("col", "dp")),
            P(("col", "dp"), "row"),
            P(("col", "dp"), "row"),
            P("row", ("col", "dp")),
        ),
        check_vma=False,
    )
```

```python
import jax
import jax.numpy as jnp
from jax import lax
from jax.experimental import pallas as pl
from jax.experimental.pallas import tpu as pltpu
from jax.sharding import PartitionSpec as P


EPSILON = 1e-05
THETA = 1000000.0
NEGATIVE = -1e30


F32 = jnp.float32
BF16 = jnp.bfloat16


def matmul(left, right):
    return jnp.dot(left, right, preferred_element_type=F32)


def matmul_nt(left, right):
    return lax.dot_general(left, right, (((1,), (1,)), ((), ())), preferred_element_type=F32)


def matmul_tn(left, right):
    return lax.dot_general(left, right, (((0,), (0,)), ((), ())), preferred_element_type=F32)


def flip(values, axis, distance):
    size = lax.axis_size(axis)
    return lax.ppermute(values, axis, [(i, i ^ distance) for i in range(size)])


def spread(values):
    return [values] + [flip(values, "col", k) for k in range(1, lax.axis_size("col"))]


def exchange(pieces):
    return [pieces[0]] + [flip(pieces[k], "col", k) for k in range(1, len(pieces))]


def total(parts):
    result = parts[0].astype(F32)
    for part in parts[1:]:
        result = result + part.astype(F32)
    return result


def kernel_call(kernel, outs, *args, scalars=None, scratch=(), fetch=0):
    specs = [pl.BlockSpec(memory_space=pltpu.HBM)] * fetch
    specs = specs + [pl.BlockSpec(memory_space=pltpu.VMEM)] * (len(args) - fetch)
    scratch_shapes = [pltpu.VMEM(shape, dtype) for shape, dtype in scratch]
    if fetch:
        scratch_shapes = [pltpu.VMEM(v.shape, v.dtype) for v in args[:fetch]] + scratch_shapes
        scratch_shapes.append(pltpu.SemaphoreType.DMA((fetch,)))
    if scalars is not None:
        args = (scalars,) + args
        specs = [pl.BlockSpec(memory_space=pltpu.SMEM)] + specs
    return pl.pallas_call(
        kernel,
        out_shape=[jax.ShapeDtypeStruct(shape, dtype) for shape, dtype in outs],
        in_specs=specs,
        out_specs=[pl.BlockSpec(memory_space=pltpu.VMEM)] * len(outs),
        scratch_shapes=scratch_shapes,
        compiler_params=pltpu.CompilerParams(vmem_limit_bytes=48 * 1024 * 1024),
    )(*args)


def fetched(sources, targets, semaphores):
    copies = [
        pltpu.make_async_copy(source, target, semaphores.at[i])
        for i, (source, target) in enumerate(zip(sources, targets))
    ]
    for copy in copies:
        copy.start()
    for copy in copies:
        copy.wait()


def pack_one_kernel(
    where, x_in, query_in, key_in, value_in, gain_first, gain_second,
    out0, out1, out2, out3, x, query, key, value, semaphores,
):
    fetched((x_in, query_in, key_in, value_in), (x, query, key, value), semaphores)
    outs = (out0, out1, out2, out3)
    row, col = where[0], where[1]
    half = x.shape[0] // 2
    cols = len(outs)
    q_size, kv_size = query.shape[1] // cols, key.shape[1] // cols
    line = lax.broadcasted_iota(jnp.int32, (16, x.shape[1]), 0)
    rows = jnp.zeros((16, x.shape[1]), F32)
    for g, gain in enumerate((gain_first, gain_second)):
        rest = gain[...]
        for p in range(3):
            part = rest.astype(BF16).astype(F32)
            rows = jnp.where(line == 3 * g + p, part, rows)
            rest = rest - part
    mine = x[pl.ds(pl.multiple_of(row * half, half), half), :]
    for k, out in enumerate(outs):
        block = col ^ k
        out[:half, :] = mine
        out[half : half + 16, :] = rows.astype(BF16)
        out[half + 16 :, :q_size] = query[:, pl.ds(pl.multiple_of(block * q_size, q_size), q_size)]
        pair = pl.multiple_of((block >> 1) * (2 * kv_size), 2 * kv_size)
        odd = (block & 1) == 1
        both = []
        for weight in (key, value):
            two = weight[:, pl.ds(pair, 2 * kv_size)]
            both.append(jnp.where(odd, two[:, kv_size:], two[:, :kv_size]))
        out[half + 16 :, q_size:] = jnp.concatenate(both, axis=1)


def pack_two_kernel(
    where, weight_in, cot_in, out0, out1, out2, out3, weight, cot, semaphores
):
    fetched((weight_in, cot_in), (weight, cot), semaphores)
    outs = (out0, out1, out2, out3)
    size, half = weight.shape[0] // len(outs), cot.shape[0] // 2
    for k, out in enumerate(outs):
        out[:half, :] = cot[pl.ds(pl.multiple_of(where[0] * half, half), half), :]
        for j in range(len(outs)):
            source = pl.multiple_of((where[1] ^ (k ^ j)) * size, size)
            out[half + j * size : half + (j + 1) * size, :] = weight[pl.ds(source, size), :]


def pack_three_kernel(where, down_in, out0, out1, out2, out3, down, semaphores):
    fetched((down_in,), (down,), semaphores)
    outs = (out0, out1, out2, out3)
    size = down.shape[0] // len(outs)
    for k, out in enumerate(outs):
        out[...] = down[pl.ds(pl.multiple_of((where[1] ^ k) * size, size), size), :]


def pack_gate_kernel(
    where, gate_in, up_in, out0, out1, out2, out3, out4, gate, up, semaphores
):
    fetched((gate_in, up_in), (gate, up), semaphores)
    outs = (out0, out1, out2, out3, out4)
    col, odd_plane = where[1], (where[2] & 1) == 1
    cols = len(outs) - 1
    size = gate.shape[1] // cols

    def piece(weight, block):
        two = weight[:, pl.ds(pl.multiple_of((block >> 1) * (2 * size), 2 * size), 2 * size)]
        return jnp.where((block & 1) == 1, two[:, size:], two[:, :size])

    @pl.when(jnp.logical_not(odd_plane))
    def _():
        for k in range(cols):
            outs[k][...] = piece(gate, col ^ k)
        outs[cols][...] = piece(up, col)

    @pl.when(odd_plane)
    def _():
        for k in range(cols):
            outs[k][...] = piece(up, col ^ k)
        outs[cols][...] = piece(gate, col)


def join_kernel(first0, first1, first2, first3, out):
    part, size = first0.shape[1], out.shape[0]
    for k, piece in enumerate((first0, first1, first2, first3)):
        out[:, k * part : (k + 1) * part] = piece[piece.shape[0] - size :, :]


def project_kernel(
    where, mine, other, context_near, context_far, joined, joined_far,
    first0, first1, first2, first3, normed_out, own_out, share_out, sum_scratch,
):
    buffers = (first0, first1, first2, first3)
    half, part = mine.shape[0], first0.shape[1]
    share = share_out.shape[0]
    top = mine[...].astype(F32) + matmul(context_near[:half, :], joined[...])
    top = top + matmul(context_far[half:, :], joined_far[...])
    low = other[...].astype(F32) + matmul(context_near[half:, :], joined[...])
    low = low + matmul(context_far[:half, :], joined_far[...])
    sum_scratch[...] = top
    own_out[...] = top[:, :part]
    share_out[...] = sum_scratch[pl.ds(pl.multiple_of(where[1] * share, share), share), :]
    gain = jnp.concatenate([gain_row(buffers, half + 3, k) for k in range(len(buffers))], axis=1)
    for i, rows in enumerate((top, low)):
        root = lax.rsqrt(jnp.mean(rows * rows, axis=1, keepdims=True) + EPSILON)
        normed_out[i * half : (i + 1) * half, :] = (rows * root * gain).astype(BF16)


def hidden_kernel(
    where, normed, near0, near1, near2, near3, far0, far1, far2, far3,
    gate_out, up_out, hidden_out,
):
    part = near0.shape[0]
    first_pre = second_pre = None
    for k, (near, far) in enumerate(
        ((near0, far0), (near1, far1), (near2, far2), (near3, far3))
    ):
        block = normed[:, k * part : (k + 1) * part]
        one, two = matmul(block, near[...]), matmul(block, far[...])
        first_pre = one if k == 0 else first_pre + one
        second_pre = two if k == 0 else second_pre + two
    even = (where[2] & 1) == 0
    gate_pre = jnp.where(even, first_pre, second_pre)
    up_pre = jnp.where(even, second_pre, first_pre)
    gate_out[...] = gate_pre
    up_out[...] = up_pre
    hidden_out[...] = (gate_pre * (1.0 / (1.0 + jnp.exp(-gate_pre))) * up_pre).astype(BF16)


def backward_kernel(
    where, cot_mine, cot_other, gate_in, up_in, down0, down1, down2, down3,
    near0, near1, near2, near3, far0, far1, far2, far3,
    gate_grad_out, up_grad_out, mine_out, other_out,
):
    half, part = mine_out.shape[0], near0.shape[0]
    size = gate_in.shape[1]
    parts = []
    for rows in (cot_mine, cot_other):
        grad = None
        for k, down in enumerate((down0, down1, down2, down3)):
            term = matmul_nt(rows[:, k * part : (k + 1) * part], down[:size, :])
            grad = term if k == 0 else grad + term
        parts.append(grad)
    hidden_grad = jnp.concatenate(parts, axis=0)
    gate_pre, up_pre = gate_in[...], up_in[...]
    sigmoid_gate = 1.0 / (1.0 + jnp.exp(-gate_pre))
    gate_grad = (
        hidden_grad * up_pre * sigmoid_gate * (1.0 + gate_pre * (1.0 - sigmoid_gate))
    ).astype(BF16)
    up_grad = (hidden_grad * (gate_pre * sigmoid_gate)).astype(BF16)
    gate_grad_out[...] = gate_grad
    up_grad_out[...] = up_grad
    even = (where[2] & 1) == 0
    near_grad = jnp.where(even, gate_grad, up_grad)
    far_grad = jnp.where(even, up_grad, gate_grad)
    for k, (near, far) in enumerate(
        ((near0, far0), (near1, far1), (near2, far2), (near3, far3))
    ):
        block = matmul_nt(near_grad, near[...]) + matmul_nt(far_grad, far[...])
        mine_out[:, k * part : (k + 1) * part] = block[:half].astype(BF16)
        other_out[:, k * part : (k + 1) * part] = block[half:].astype(BF16)


def result_kernel(hidden, down0, down1, down2, down3, mine_out, other_out):
    half, part = mine_out.shape[0], down0.shape[1]
    for k, down in enumerate((down0, down1, down2, down3)):
        block = matmul(hidden[...], down[: hidden.shape[1], :])
        mine_out[:, k * part : (k + 1) * part] = block[:half].astype(BF16)
        other_out[:, k * part : (k + 1) * part] = block[half:].astype(BF16)


def deal(where, scratch, k, send, keep, rows):
    for j in range(2):
        for out, m in ((send, 1 + 2 * j), (keep, 2 * j)):
            start = pl.multiple_of((where[2] ^ m) * rows, rows)
            out[j, k, :rows, :] = scratch[pl.ds(start, rows), :]


def down_grad_kernel(where, cot_mine, cot_other, hidden, send, keep, scratch):
    half = hidden.shape[0] // 2
    cols, rows = send.shape[1], send.shape[2]
    part = cot_mine.shape[1] // cols
    for k in range(cols):
        span = slice(k * part, (k + 1) * part)
        grad = matmul_tn(cot_mine[:, span], hidden[:half, :])
        grad = grad + matmul_tn(cot_other[:, span], hidden[half:, :])
        scratch[...] = grad.astype(BF16)
        deal(where, scratch, k, send, keep, rows)


def weight_grad_kernel(
    where, normed, gate_grad, up_grad, gate_send, gate_keep, up_send, up_keep, scratch
):
    cols, rows = gate_send.shape[1], gate_send.shape[2]
    part = normed.shape[1] // cols
    for upstream, send, keep in ((gate_grad, gate_send, gate_keep), (up_grad, up_send, up_keep)):
        for k in range(cols):
            span = slice(k * part, (k + 1) * part)
            scratch[...] = matmul_tn(normed[:, span], upstream[...]).astype(BF16)
            deal(where, scratch, k, send, keep, rows)


def pack_tokens_kernel(where, ours, came, out0, out1, out2, out3, scratch):
    outs = (out0, out1, out2, out3)
    share, part = out0.shape[0], out0.shape[1] // len(outs)
    scratch[...] = (ours[...].astype(F32) + came[...].astype(F32)).astype(BF16)
    for k, out in enumerate(outs):
        rows = pl.ds(pl.multiple_of((where[1] ^ k) * share, share), share)
        for j in range(len(outs)):
            source = k ^ j
            out[:, j * part : (j + 1) * part] = scratch[rows, source * part : (source + 1) * part]


def second_norm_kernel(
    where, came0, came1, came2, came3, sums, cot_mine, first0, first1, first2, first3,
    out0, out1, out2, out3, gain_out,
):
    buffers = (first0, first1, first2, first3)
    outs = (out0, out1, out2, out3)
    share, part = out0.shape[0], out0.shape[1] // len(outs)
    half = share * len(outs)
    grad = came0[...].astype(F32) + came1[...].astype(F32)
    grad = grad + came2[...].astype(F32) + came3[...].astype(F32)
    gain = jnp.concatenate([gain_row(buffers, half + 3, k) for k in range(len(buffers))], axis=1)
    rows = sums[...]
    root = lax.rsqrt(jnp.mean(rows * rows, axis=1, keepdims=True) + EPSILON)
    normal = rows * root
    weighted = grad * gain
    gain_out[...] = jnp.sum(grad * normal, axis=0, keepdims=True)
    inner = jnp.mean(weighted * normal, axis=1, keepdims=True)
    cot = cot_mine[pl.ds(pl.multiple_of(where[1] * share, share), share), :].astype(F32)
    first = (cot + root * (weighted - normal * inner)).astype(BF16)
    for k, out in enumerate(outs):
        for j in range(len(outs)):
            source = k ^ j
            out[:, j * part : (j + 1) * part] = first[:, source * part : (source + 1) * part]


def join_tokens_kernel(where, came0, came1, came2, came3, out):
    share = came0.shape[0]
    for k, came in enumerate((came0, came1, came2, came3)):
        out[pl.ds(pl.multiple_of((where[1] ^ k) * share, share), share), :] = came[...]


def pack_features_kernel(ours, came, out0, out1, out2, out3):
    part = out0.shape[1]
    for k, out in enumerate((out0, out1, out2, out3)):
        span = slice(k * part, (k + 1) * part)
        out[...] = (ours[:, span].astype(F32) + came[:, span].astype(F32)).astype(BF16)


def pack_last_kernel(ours, came, inner, inner_came, out0, out1, out2, out3):
    half, part = ours.shape[0], out0.shape[1]
    line = lax.broadcasted_iota(jnp.int32, (16, part), 0)
    rows = jnp.zeros((16, part), F32)
    rest = inner[0:1, :half] + inner_came[0:1, :]
    for p in range(3):
        piece = rest.astype(BF16).astype(F32)
        rows = jnp.where(line == p, piece, rows)
        rest = rest - piece
    for k, out in enumerate((out0, out1, out2, out3)):
        span = slice(k * part, (k + 1) * part)
        out[:half, :] = (ours[:, span].astype(F32) + came[:, span].astype(F32)).astype(BF16)
        out[half:, :] = rows.astype(BF16)


def join_first_kernel(first0, first1, first2, first3, out):
    part, size = first0.shape[1], out.shape[0]
    for k, piece in enumerate((first0, first1, first2, first3)):
        out[:, k * part : (k + 1) * part] = piece[:size, :]


def in_chip_order(where, pieces):
    odd, high = (where[1] & 1) == 1, (where[1] & 2) == 2
    ordered = []
    for s in range(4):
        low_pair = jnp.where(odd, pieces[s ^ 1], pieces[s])
        high_pair = jnp.where(odd, pieces[s ^ 3], pieces[s ^ 2])
        ordered.append(jnp.where(high, high_pair, low_pair))
    return ordered


def unpack_feed_kernel(where, came0, came1, came2, came3, down_out, gate_out, up_out):
    rows = gate_out.shape[0]
    pieces = in_chip_order(where, [v[...] for v in (came0, came1, came2, came3)])
    for i, out in enumerate((down_out, gate_out, up_out)):
        span = slice(i * rows, (i + 1) * rows)
        out[...] = jnp.concatenate([v[span].astype(F32) for v in pieces], axis=1)


def unpack_mixed_kernel(
    where, came0, came1, came2, came3, query_out, key_out, value_out, output_out, gain_out
):
    rows = query_out.shape[0]
    pieces = in_chip_order(where, [v[...] for v in (came0, came1, came2, came3)])
    two = query_out.shape[1] // len(pieces)
    size = two // 2
    pieces = [v.astype(F32) for v in pieces]
    for out, start, wide in (
        (query_out, 0, two), (key_out, two, size), (value_out, two + size, size),
        (output_out, 2 * two, two),
    ):
        out[...] = jnp.concatenate([v[:rows, start : start + wide] for v in pieces], axis=1)
    gain_out[...] = pieces[0][rows:] + pieces[1][rows:] + pieces[2][rows:] + pieces[3][rows:]


def lane_is_first(size):
    return lax.broadcasted_iota(jnp.int32, (1, 2 * size), 1) < size


def head_scale(values, first):
    size = values.shape[1] // 2
    squares = values * values
    left = jnp.sum(jnp.where(first, squares, 0.0), axis=1, keepdims=True)
    right = jnp.sum(jnp.where(first, 0.0, squares), axis=1, keepdims=True)
    return lax.rsqrt(jnp.where(first, left, right) / size + EPSILON)


def turn(values, cosine, sine):
    width = values.shape[1]
    quarter = width // 4
    lane = lax.broadcasted_iota(jnp.int32, (1, width), 1)
    low = (lane & quarter) == 0
    other = jnp.where(
        low, pltpu.roll(values, width - quarter, 1), pltpu.roll(values, quarter, 1)
    )
    return values * cosine + other * sine


def root_and_input(mine, other):
    rows = jnp.concatenate([mine[...], other[...]], axis=0).astype(F32)
    mean = jnp.mean(rows * rows, axis=1, keepdims=True)
    return rows, lax.rsqrt(mean + EPSILON)


def gain_row(buffers, start, k):
    rows = buffers[k][start : start + 16, :].astype(F32)
    return rows[0:1] + rows[1:2] + rows[2:3]


def allowed_of(down, across):
    return (across[0:1, :] <= down[:, 0:1]) & (across[1:2, :] == down[:, 1:2])


def attend_kernel(
    mine, other, first0, first1, first2, first3, cosine, sine, gains, down, across,
    qkv_out, turned_out, context_out, log_out,
):
    buffers = (first0, first1, first2, first3)
    half, part = mine.shape[0], first0.shape[1]
    rows, root = root_and_input(mine, other)
    start = half + 16
    qkv = None
    for k, buffer in enumerate(buffers):
        block = rows[:, k * part : (k + 1) * part] * root * gain_row(buffers, half, k)
        term = matmul(block.astype(BF16), buffer[start:, :])
        qkv = term if qkv is None else qkv + term
    qkv_out[...] = qkv
    two = qkv.shape[1] // 2
    size = two // 2
    first = lane_is_first(size)
    query, pair = qkv[:, :two], qkv[:, two:]
    query_turned = turn(
        query * head_scale(query, first) * gains[0:1, :], cosine[...], sine[...]
    ).astype(BF16)
    key_turned = turn(pair * head_scale(pair, first) * gains[1:2, :], cosine[...], sine[...])
    pair_rounded = jnp.where(first, key_turned, pair).astype(BF16)
    turned_out[:, :two] = query_turned
    turned_out[:, two:] = pair_rounded
    key, value = pair_rounded[:, :size], pair_rounded[:, size:]
    allowed = allowed_of(down, across)
    contexts, logs = [], []
    for h in range(2):
        raw = matmul_nt(query_turned[:, h * size : (h + 1) * size], key)
        scores = jnp.where(allowed, raw * size ** (-0.5), NEGATIVE)
        top = jnp.max(scores, axis=1, keepdims=True)
        powers = jnp.exp(scores - top)
        sums = jnp.sum(powers, axis=1, keepdims=True)
        prob = (powers * (1.0 / sums)).astype(BF16)
        contexts.append(matmul(prob, value))
        logs.append(top + jnp.log(sums))
    context_out[...] = jnp.concatenate(contexts, axis=1).astype(BF16)
    log_out[...] = jnp.where(first, logs[0], logs[1])


def attend_back_kernel(
    where, mine, other, first0, first1, first2, first3, cosine, sine, gains, down, across,
    qkv_in, turned, context_in, logs, grad_mine, grad_other, out_weight,
    gain_in, one_mine, one_other, inner_out, mixed_send, mixed_keep, mixed,
):
    buffers = (first0, first1, first2, first3)
    half, part = mine.shape[0], first0.shape[1]
    two = context_in.shape[1]
    size = two // 2
    first = lane_is_first(size)
    upstream = jnp.concatenate([grad_mine[...], grad_other[...]], axis=0)
    context = context_in[...]
    context_grad = matmul_nt(upstream, out_weight[:two, :]).astype(BF16)
    key, value = turned[:, two : two + size], turned[:, two + size :]
    allowed = allowed_of(down, across)
    products = context_grad.astype(F32) * context.astype(F32)
    query_grads = []
    key_grad = value_grad = None
    for h in range(2):
        query = turned[:, h * size : (h + 1) * size]
        grad = context_grad[:, h * size : (h + 1) * size]
        raw = matmul_nt(query, key)
        scores = jnp.where(allowed, raw * size ** (-0.5), NEGATIVE)
        prob = jnp.exp(scores - logs[:, h * size : h * size + 1])
        delta = jnp.sum(
            jnp.where(first if h == 0 else jnp.logical_not(first), products, 0.0),
            axis=1,
            keepdims=True,
        )
        value_term = matmul_tn(prob.astype(BF16), grad)
        score_grad = (prob * (matmul_nt(grad, value) - delta) * size ** (-0.5)).astype(BF16)
        query_grads.append(matmul(score_grad, key))
        key_term = matmul_tn(score_grad, query)
        key_grad = key_term if h == 0 else key_grad + key_term
        value_grad = value_term if h == 0 else value_grad + value_term
    pieces, head_parts = [], []
    for i, grad in enumerate(
        (jnp.concatenate(query_grads, axis=1), jnp.concatenate([key_grad, value_grad], axis=1))
    ):
        normed = turn(grad, cosine[...], -sine[...])
        proj = qkv_in[:, i * two : (i + 1) * two]
        scale = head_scale(proj, first)
        hat = proj * scale
        weighted = normed * gains[i : i + 1, :]
        product = weighted * hat
        left = jnp.sum(jnp.where(first, product, 0.0), axis=1, keepdims=True)
        right = jnp.sum(jnp.where(first, 0.0, product), axis=1, keepdims=True)
        inner = jnp.where(first, left, right) / size
        result = scale * (weighted - hat * inner)
        pieces.append(result if i == 0 else jnp.where(first, result, grad))
        head_parts.append(jnp.sum(normed * hat, axis=0, keepdims=True))
    head_line = head_parts[0] + pltpu.roll(head_parts[0], size, 1)
    head_line = jnp.where(first, head_line, pltpu.roll(head_parts[1], size, 1))
    rows_here = mixed_send.shape[2] - 8
    line = lax.broadcasted_iota(jnp.int32, (8, part), 0)
    qkv_grad = jnp.concatenate(pieces, axis=1).astype(BF16)
    rows, root = root_and_input(mine, other)
    inner_sum = jnp.zeros((2 * half, 1), F32)
    for k, buffer in enumerate(buffers):
        span = slice(k * part, (k + 1) * part)
        gain = gain_row(buffers, half, k)
        hat = rows[:, span] * root
        grad = matmul_nt(qkv_grad, buffer[half + 16 :, :])
        product = grad * hat
        lines = jnp.where(line == 0, jnp.sum(product, axis=0, keepdims=True), 0.0)
        lines = jnp.where(line == 1, gain_in[:, span], lines).astype(BF16)
        inner_sum = inner_sum + jnp.sum(product * gain, axis=1, keepdims=True)
        one_mine[:, span] = grad[:half].astype(BF16)
        one_other[:, span] = grad[half:].astype(BF16)
        mixed[:, : 2 * two] = matmul_tn((hat * gain).astype(BF16), qkv_grad).astype(BF16)
        mixed[:, 2 * two :] = matmul_tn(upstream[:, span], context).astype(BF16)
        heads = jnp.broadcast_to(head_line, (8, two)).astype(BF16)
        if mixed_send.shape[0] == 2:
            deal(where, mixed, k, mixed_send, mixed_keep, rows_here)
            for out in (mixed_send, mixed_keep):
                for j in range(2):
                    out[j, k, rows_here:, : 2 * two] = lines
                    out[j, k, rows_here:, 2 * two :] = heads
        else:
            mixed_send[k, ...] = mixed[...]
            mixed_keep[k, :, : 2 * two] = lines
            mixed_keep[k, :, 2 * two :] = heads
    wide = jnp.broadcast_to(inner_sum / (part * len(buffers)), (2 * half, 128))
    inner_out[...] = jnp.transpose(wide)[:8, :]


def rope_tables(places, head_size):
    half_size = head_size // 2
    frequency = THETA ** (-(jnp.arange(half_size).astype(F32) * 2.0 / head_size))
    angles = places.astype(F32)[:, None] * frequency[None, :]
    return (jnp.cos(angles), jnp.sin(angles))


def body(
    block_input,
    segments,
    positions,
    attention_gain,
    query_weight,
    key_weight,
    value_weight,
    query_gain,
    key_gain,
    output_weight,
    feedforward_gain,
    gate_weight,
    up_weight,
    down_weight,
    cotangent,
):
    tokens = block_input.shape[0]
    part = block_input.shape[1]
    head = query_gain.shape[0]
    cols = lax.axis_size("col")
    planes = lax.axis_size("dp")
    width = part * cols
    half = tokens // 2
    row = lax.axis_index("row")
    col = lax.axis_index("col")
    plane = lax.axis_index("dp")

    def mine_first(values):
        return jnp.where(row == 0, values, jnp.roll(values, half, axis=0))

    def natural(values):
        return jnp.where(row == 0, values, jnp.roll(values, half, axis=0))

    def both_rows(values):
        return jnp.concatenate([values, flip(values, "row", 1)], axis=0)

    q_size = query_weight.shape[1] // cols
    units = gate_weight.shape[1] // cols
    where = jnp.stack([row, col, plane]).astype(jnp.int32)
    shapes = [((half + 16 + part, part), BF16)] * cols
    first_in = exchange(
        kernel_call(
            pack_one_kernel,
            shapes,
            block_input,
            query_weight,
            key_weight,
            value_weight,
            attention_gain.reshape(1, part),
            feedforward_gain.reshape(1, part),
            scalars=where,
            fetch=4,
        ),
    )
    (input_mine,) = kernel_call(join_first_kernel, [((half, width), BF16)], *first_in)
    gain_parts = jnp.concatenate([v[half : half + 16] for v in first_in], axis=1).astype(F32)
    gain_one = gain_parts[0] + gain_parts[1] + gain_parts[2]
    input_other = flip(input_mine, "row", 1)
    gate_in = kernel_call(
        pack_gate_kernel,
        [((part, units), BF16)] * (cols + 1),
        gate_weight,
        up_weight,
        scalars=where,
        fetch=2,
    )
    near_parts = exchange(gate_in[:cols])
    far_parts = [gate_in[cols]] + [flip(v, "dp", 1) for v in near_parts[1:]]
    inner_size = output_weight.shape[0]
    two_out = kernel_call(
        pack_two_kernel,
        [((half + inner_size, part), BF16)] * cols,
        output_weight,
        cotangent,
        scalars=where,
        fetch=2,
    )
    second_parts = exchange(two_out)
    three_out = kernel_call(
        pack_three_kernel,
        [((units, part), BF16)] * cols,
        down_weight,
        scalars=where,
        fetch=1,
    )
    down_parts = exchange(three_out)

    group = q_size // head
    segment_ids = mine_first(segments)
    places = mine_first(positions)
    index = mine_first(jnp.arange(tokens))

    cosine, sine_part = rope_tables(places, head)
    cos_lanes = jnp.concatenate([cosine] * (2 * group), axis=1)
    sin_lanes = jnp.concatenate([-sine_part, sine_part] * group, axis=1)
    head_gains = jnp.stack([jnp.tile(query_gain, group), jnp.tile(key_gain, group)])
    down = jnp.stack([index, segment_ids], axis=1)
    across = jnp.stack([index, segment_ids])
    common = (
        input_mine,
        input_other,
        *first_in,
        cos_lanes,
        sin_lanes,
        head_gains,
        down,
        across,
    )
    qkv, turned, context, logs = kernel_call(
        attend_kernel,
        [
            ((tokens, 2 * q_size), F32),
            ((tokens, 2 * q_size), BF16),
            ((tokens, q_size), BF16),
            ((tokens, q_size), F32),
        ],
        *common,
    )

    context_parts = spread(context)
    (context_near,) = kernel_call(join_kernel, [((tokens, inner_size), BF16)], *context_parts)
    context_far = flip(context_near, "row", 1)
    (second_in,) = kernel_call(join_kernel, [((inner_size, width), BF16)], *second_parts)
    second_far = flip(second_in, "row", 1)
    (cot_mine,) = kernel_call(join_first_kernel, [((half, width), BF16)], *second_parts)
    cot_other = flip(cot_mine, "row", 1)

    share = half // cols
    normed_two, first_block, first_share = kernel_call(
        project_kernel,
        [((tokens, width), BF16), ((half, part), F32), ((share, width), F32)],
        input_mine,
        input_other,
        context_near,
        context_far,
        second_in,
        second_far,
        *first_in,
        scalars=where,
        scratch=[((half, width), F32)],
    )
    gate_pre, up_pre, hidden = kernel_call(
        hidden_kernel,
        [((tokens, units), F32), ((tokens, units), F32), ((tokens, units), BF16)],
        normed_two,
        *near_parts,
        *far_parts,
        scalars=where,
    )
    rows = part // planes
    if planes == 4:
        down_dealt = kernel_call(
            down_grad_kernel,
            [((2, cols, rows, units), BF16)] * 2,
            cot_mine,
            cot_other,
            hidden,
            scalars=where,
            scratch=[((part, units), BF16)],
        )
    gate_grad, up_grad, two_mine, two_other = kernel_call(
        backward_kernel,
        [((tokens, units), BF16)] * 2 + [((half, width), BF16)] * 2,
        cot_mine,
        cot_other,
        gate_pre,
        up_pre,
        *down_parts,
        *near_parts,
        *far_parts,
        scalars=where,
    )

    two_came = flip(two_other, "row", 1)
    two_pieces = kernel_call(
        pack_tokens_kernel,
        [((share, width), BF16)] * cols,
        two_mine,
        two_came,
        scalars=where,
        scratch=[((half, width), BF16)],
    )
    two_in = exchange(two_pieces)
    *first_pieces, feedforward_part = kernel_call(
        second_norm_kernel,
        [((share, width), BF16)] * cols + [((1, width), F32)],
        *two_in,
        first_share,
        cot_mine,
        *first_in,
        scalars=where,
    )
    first_back = exchange(first_pieces)
    (first_half,) = kernel_call(
        join_tokens_kernel, [((half, width), BF16)], *first_back, scalars=where
    )
    first_other = flip(first_half, "row", 1)

    def summed(send, keep):
        came = flip(send, "dp", 1)
        rest = (keep[1].astype(F32) + came[1].astype(F32)).astype(BF16)
        far = flip(rest, "dp", 2)
        return total([keep[0], came[0], far]).astype(BF16)

    def scattered(split):
        return lax.psum_scatter(split, "dp", scatter_dimension=0, tiled=True)[0]

    if planes == 4:
        dealt = kernel_call(
            weight_grad_kernel,
            [((2, cols, rows, units), BF16)] * 4,
            normed_two,
            gate_grad,
            up_grad,
            scalars=where,
            scratch=[((part, units), BF16)],
        )
        dealt = list(down_dealt) + list(dealt)
        sums = [summed(dealt[2 * i], dealt[2 * i + 1]) for i in range(3)]
    else:
        cot_all = jnp.concatenate([cot_mine, cot_other], axis=0)
        sums = [
            scattered(
                jnp.moveaxis(grad.astype(BF16).reshape(cols, planes, rows, units), 1, 0)
            )
            for grad in (
                matmul_tn(cot_all, hidden),
                matmul_tn(normed_two, gate_grad),
                matmul_tn(normed_two, up_grad),
            )
        ]
    feed_in = exchange([jnp.concatenate([v[k] for v in sums], axis=0) for k in range(cols)])
    down_share, gate_share, up_share = kernel_call(
        unpack_feed_kernel, [((rows, cols * units), F32)] * 3, *feed_in, scalars=where
    )

    result_mine, result_other = kernel_call(
        result_kernel, [((half, width), BF16)] * 2, hidden, *down_parts
    )
    result_came = flip(result_other, "row", 1)
    result_pieces = kernel_call(
        pack_features_kernel, [((half, part), BF16)] * cols, result_mine, result_came
    )
    result_in = exchange(result_pieces)
    result_mine = (first_block + total(result_in)).astype(BF16)
    block_output = natural(both_rows(result_mine))

    mixed_size = 3 * q_size
    if planes == 4:
        mixed_outs = [((2, cols, rows + 8, mixed_size), BF16)] * 2
    else:
        mixed_outs = [((cols, part, mixed_size), BF16), ((cols, 8, mixed_size), BF16)]
    one_mine, one_other, inner_part, mixed_first, mixed_second = kernel_call(
        attend_back_kernel,
        [((half, width), BF16), ((half, width), BF16), ((8, tokens), F32)] + mixed_outs,
        *common,
        qkv,
        turned,
        context,
        logs,
        first_half,
        first_other,
        second_in,
        feedforward_part,
        scalars=where,
        scratch=[((part, mixed_size), BF16)],
    )
    one_came = flip(one_other, "row", 1)
    inner_came = flip(inner_part[:, half:], "row", 1)
    one_pieces = kernel_call(
        pack_last_kernel,
        [((half + 16, part), BF16)] * cols,
        one_mine,
        one_came,
        inner_part,
        inner_came,
    )
    one_in = exchange(one_pieces)
    one_grad = total([v[:half] for v in one_in])
    inner_one = jnp.sum(total([v[half:] for v in one_in])[:3], axis=0)[:, None]
    weighted_one = one_grad * gain_one[:part]
    own_input = input_mine.astype(F32)
    root_one = lax.rsqrt(jnp.mean(own_input * own_input, axis=1, keepdims=True) + EPSILON)
    normal_one = own_input[:, :part] * root_one
    input_mine_grad = first_half[:, :part].astype(F32) + root_one * (
        weighted_one - normal_one * inner_one
    )
    input_grad = natural(both_rows(input_mine_grad))

    if planes == 4:
        mixed_sum = summed(mixed_first, mixed_second)
    else:
        lines = jnp.broadcast_to(mixed_second[:, None], (cols, planes, 8, mixed_size))
        blocks = mixed_first.reshape(cols, planes, rows, mixed_size)
        mixed_sum = scattered(jnp.moveaxis(jnp.concatenate([blocks, lines], axis=2), 1, 0))
    mixed_in = exchange([mixed_sum[k] for k in range(cols)])
    query_share, key_share, value_share, output_share, gain_sums = kernel_call(
        unpack_mixed_kernel,
        [
            ((rows, cols * q_size), F32),
            ((rows, cols * head), F32),
            ((rows, cols * head), F32),
            ((rows, cols * q_size), F32),
            ((8, mixed_size), F32),
        ],
        *mixed_in,
        scalars=where,
    )
    gain_sums = gain_sums + flip(gain_sums, "row", 1)
    attention_share = lax.dynamic_slice_in_dim(gain_sums[0], plane * rows, rows, 0)
    feedforward_share = lax.dynamic_slice_in_dim(gain_sums[1], plane * rows, rows, 0)
    query_gain_grad = gain_sums[0, 2 * q_size : 2 * q_size + head]
    key_gain_grad = gain_sums[0, 2 * q_size + head :]
    return (
        block_output,
        input_grad,
        attention_share,
        query_share,
        key_share,
        value_share,
        query_gain_grad,
        key_gain_grad,
        output_share.T,
        feedforward_share,
        gate_share,
        up_share,
        down_share.T,
    )


def solution(mesh):
    placed = (
        P("dp", "col"),
        P("dp"),
        P("dp"),
        P("col"),
        P("col", "row"),
        P("col", "row"),
        P("col", "row"),
        P(),
        P(),
        P("row", "col"),
        P("col"),
        P("col", "row"),
        P("col", "row"),
        P("row", "col"),
        P("dp", "col"),
    )


    return jax.shard_map(
        body,
        mesh=mesh,
        in_specs=placed,
        out_specs=(
            P("dp", "col"),
            P("dp", "col"),
            P(("col", "dp")),
            P(("col", "dp"), "row"),
            P(("col", "dp"), "row"),
            P(("col", "dp"), "row"),
            P(),
            P(),
            P("row", ("col", "dp")),
            P(("col", "dp")),
            P(("col", "dp"), "row"),
            P(("col", "dp"), "row"),
            P("row", ("col", "dp")),
        ),
        check_vma=False,
    )
```

```python
import jax
import jax.numpy as jnp
from jax import lax
from jax.experimental import pallas as pl
from jax.experimental.pallas import tpu as pltpu
from jax.sharding import PartitionSpec as P


EPSILON = 1e-05
THETA = 1000000.0
NEGATIVE = -1e30


F32 = jnp.float32
BF16 = jnp.bfloat16


def matmul(left, right):
    return jnp.dot(left, right, preferred_element_type=F32)


def matmul_nt(left, right):
    return lax.dot_general(left, right, (((1,), (1,)), ((), ())), preferred_element_type=F32)


def matmul_tn(left, right):
    return lax.dot_general(left, right, (((0,), (0,)), ((), ())), preferred_element_type=F32)


def flip(values, axis, distance):
    size = lax.axis_size(axis)
    return lax.ppermute(values, axis, [(i, i ^ distance) for i in range(size)])


def spread(values):
    return [values] + [flip(values, "col", k) for k in range(1, lax.axis_size("col"))]


def exchange(pieces):
    return [pieces[0]] + [flip(pieces[k], "col", k) for k in range(1, len(pieces))]


def total(parts):
    result = parts[0].astype(F32)
    for part in parts[1:]:
        result = result + part.astype(F32)
    return result


def kernel_call(kernel, outs, *args, scalars=None, scratch=(), fetch=0, room=8):
    specs = [pl.BlockSpec(memory_space=pltpu.HBM)] * fetch
    specs = specs + [pl.BlockSpec(memory_space=pltpu.VMEM)] * (len(args) - fetch)
    scratch_shapes = [pltpu.VMEM(shape, dtype) for shape, dtype in scratch]
    if fetch:
        scratch_shapes = [pltpu.VMEM(v.shape, v.dtype) for v in args[:fetch]] + scratch_shapes
        scratch_shapes.append(pltpu.SemaphoreType.DMA((fetch,)))
    if scalars is not None:
        args = (scalars,) + args
        specs = [pl.BlockSpec(memory_space=pltpu.SMEM)] + specs
    return pl.pallas_call(
        kernel,
        out_shape=[jax.ShapeDtypeStruct(shape, dtype) for shape, dtype in outs],
        in_specs=specs,
        out_specs=[pl.BlockSpec(memory_space=pltpu.VMEM)] * len(outs),
        scratch_shapes=scratch_shapes,
        compiler_params=pltpu.CompilerParams(vmem_limit_bytes=room * 1024 * 1024),
    )(*args)


def fetched(sources, targets, semaphores):
    copies = [
        pltpu.make_async_copy(source, target, semaphores.at[i])
        for i, (source, target) in enumerate(zip(sources, targets))
    ]
    for copy in copies:
        copy.start()
    for copy in copies:
        copy.wait()


def pack_one_kernel(
    where, x_in, query_in, key_in, value_in, gain_first, gain_second,
    out0, out1, out2, out3, x, query, key, value, semaphores,
):
    fetched((x_in, query_in, key_in, value_in), (x, query, key, value), semaphores)
    outs = (out0, out1, out2, out3)
    row, col = where[0], where[1]
    half = x.shape[0] // 2
    cols = len(outs)
    q_size, kv_size = query.shape[1] // cols, key.shape[1] // cols
    line = lax.broadcasted_iota(jnp.int32, (16, x.shape[1]), 0)
    rows = jnp.zeros((16, x.shape[1]), F32)
    for g, gain in enumerate((gain_first, gain_second)):
        rest = gain[...]
        for p in range(3):
            part = rest.astype(BF16).astype(F32)
            rows = jnp.where(line == 3 * g + p, part, rows)
            rest = rest - part
    mine = x[pl.ds(pl.multiple_of(row * half, half), half), :]
    for k, out in enumerate(outs):
        block = col ^ k
        out[:half, :] = mine
        out[half : half + 16, :] = rows.astype(BF16)
        out[half + 16 :, :q_size] = query[:, pl.ds(pl.multiple_of(block * q_size, q_size), q_size)]
        pair = pl.multiple_of((block >> 1) * (2 * kv_size), 2 * kv_size)
        odd = (block & 1) == 1
        both = []
        for weight in (key, value):
            two = weight[:, pl.ds(pair, 2 * kv_size)]
            both.append(jnp.where(odd, two[:, kv_size:], two[:, :kv_size]))
        out[half + 16 :, q_size:] = jnp.concatenate(both, axis=1)


def pack_two_kernel(
    where, weight_in, cot_in, out0, out1, out2, out3, weight, cot, semaphores
):
    fetched((weight_in, cot_in), (weight, cot), semaphores)
    outs = (out0, out1, out2, out3)
    size, half = weight.shape[0] // len(outs), cot.shape[0] // 2
    for k, out in enumerate(outs):
        out[:half, :] = cot[pl.ds(pl.multiple_of(where[0] * half, half), half), :]
        for j in range(len(outs)):
            source = pl.multiple_of((where[1] ^ (k ^ j)) * size, size)
            out[half + j * size : half + (j + 1) * size, :] = weight[pl.ds(source, size), :]


def pack_three_kernel(where, down_in, out0, out1, out2, out3, down, semaphores):
    fetched((down_in,), (down,), semaphores)
    outs = (out0, out1, out2, out3)
    size = down.shape[0] // len(outs)
    for k, out in enumerate(outs):
        out[...] = down[pl.ds(pl.multiple_of((where[1] ^ k) * size, size), size), :]


def pack_gate_kernel(
    where, gate_in, up_in, out0, out1, out2, out3, out4, gate, up, semaphores
):
    fetched((gate_in, up_in), (gate, up), semaphores)
    outs = (out0, out1, out2, out3, out4)
    col, odd_plane = where[1], (where[2] & 1) == 1
    cols = len(outs) - 1
    size = gate.shape[1] // cols

    def piece(weight, block):
        two = weight[:, pl.ds(pl.multiple_of((block >> 1) * (2 * size), 2 * size), 2 * size)]
        return jnp.where((block & 1) == 1, two[:, size:], two[:, :size])

    @pl.when(jnp.logical_not(odd_plane))
    def _():
        for k in range(cols):
            outs[k][...] = piece(gate, col ^ k)
        outs[cols][...] = piece(up, col)

    @pl.when(odd_plane)
    def _():
        for k in range(cols):
            outs[k][...] = piece(up, col ^ k)
        outs[cols][...] = piece(gate, col)


def join_kernel(first0, first1, first2, first3, out):
    part, size = first0.shape[1], out.shape[0]
    for k, piece in enumerate((first0, first1, first2, first3)):
        out[:, k * part : (k + 1) * part] = piece[piece.shape[0] - size :, :]


def project_kernel(
    where, mine, other, context_near, context_far, joined, joined_far,
    first0, first1, first2, first3, normed_out, own_out, share_out, sum_scratch,
):
    buffers = (first0, first1, first2, first3)
    half, part = mine.shape[0], first0.shape[1]
    share = share_out.shape[0]
    top = mine[...].astype(F32) + matmul(context_near[:half, :], joined[...])
    top = top + matmul(context_far[half:, :], joined_far[...])
    low = other[...].astype(F32) + matmul(context_near[half:, :], joined[...])
    low = low + matmul(context_far[:half, :], joined_far[...])
    sum_scratch[...] = top
    own_out[...] = top[:, :part]
    share_out[...] = sum_scratch[pl.ds(pl.multiple_of(where[1] * share, share), share), :]
    gain = jnp.concatenate([gain_row(buffers, half + 3, k) for k in range(len(buffers))], axis=1)
    for i, rows in enumerate((top, low)):
        root = lax.rsqrt(jnp.mean(rows * rows, axis=1, keepdims=True) + EPSILON)
        normed_out[i * half : (i + 1) * half, :] = (rows * root * gain).astype(BF16)


def hidden_kernel(
    where, normed, near0, near1, near2, near3, far0, far1, far2, far3,
    gate_out, up_out, hidden_out,
):
    part = near0.shape[0]
    first_pre = second_pre = None
    for k, (near, far) in enumerate(
        ((near0, far0), (near1, far1), (near2, far2), (near3, far3))
    ):
        block = normed[:, k * part : (k + 1) * part]
        one, two = matmul(block, near[...]), matmul(block, far[...])
        first_pre = one if k == 0 else first_pre + one
        second_pre = two if k == 0 else second_pre + two
    even = (where[2] & 1) == 0
    gate_pre = jnp.where(even, first_pre, second_pre)
    up_pre = jnp.where(even, second_pre, first_pre)
    gate_out[...] = gate_pre
    up_out[...] = up_pre
    hidden_out[...] = (gate_pre * (1.0 / (1.0 + jnp.exp(-gate_pre))) * up_pre).astype(BF16)


def backward_kernel(
    where, cot_mine, cot_other, gate_in, up_in, down0, down1, down2, down3,
    near0, near1, near2, near3, far0, far1, far2, far3,
    gate_grad_out, up_grad_out, mine_out, other_out,
):
    half, part = mine_out.shape[0], near0.shape[0]
    size = gate_in.shape[1]
    parts = []
    for rows in (cot_mine, cot_other):
        grad = None
        for k, down in enumerate((down0, down1, down2, down3)):
            term = matmul_nt(rows[:, k * part : (k + 1) * part], down[:size, :])
            grad = term if k == 0 else grad + term
        parts.append(grad)
    hidden_grad = jnp.concatenate(parts, axis=0)
    gate_pre, up_pre = gate_in[...], up_in[...]
    sigmoid_gate = 1.0 / (1.0 + jnp.exp(-gate_pre))
    gate_grad = (
        hidden_grad * up_pre * sigmoid_gate * (1.0 + gate_pre * (1.0 - sigmoid_gate))
    ).astype(BF16)
    up_grad = (hidden_grad * (gate_pre * sigmoid_gate)).astype(BF16)
    gate_grad_out[...] = gate_grad
    up_grad_out[...] = up_grad
    even = (where[2] & 1) == 0
    near_grad = jnp.where(even, gate_grad, up_grad)
    far_grad = jnp.where(even, up_grad, gate_grad)
    for k, (near, far) in enumerate(
        ((near0, far0), (near1, far1), (near2, far2), (near3, far3))
    ):
        block = matmul_nt(near_grad, near[...]) + matmul_nt(far_grad, far[...])
        mine_out[:, k * part : (k + 1) * part] = block[:half].astype(BF16)
        other_out[:, k * part : (k + 1) * part] = block[half:].astype(BF16)


def result_kernel(hidden, down0, down1, down2, down3, mine_out, other_out):
    half, part = mine_out.shape[0], down0.shape[1]
    for k, down in enumerate((down0, down1, down2, down3)):
        block = matmul(hidden[...], down[: hidden.shape[1], :])
        mine_out[:, k * part : (k + 1) * part] = block[:half].astype(BF16)
        other_out[:, k * part : (k + 1) * part] = block[half:].astype(BF16)


def deal(where, scratch, k, send, keep, rows):
    for j in range(2):
        for out, m in ((send, 1 + 2 * j), (keep, 2 * j)):
            start = pl.multiple_of((where[2] ^ m) * rows, rows)
            out[j, k, :rows, :] = scratch[pl.ds(start, rows), :]


def down_grad_kernel(where, cot_mine, cot_other, hidden, send, keep, scratch):
    half = hidden.shape[0] // 2
    cols, rows = send.shape[1], send.shape[2]
    part = cot_mine.shape[1] // cols
    for k in range(cols):
        span = slice(k * part, (k + 1) * part)
        grad = matmul_tn(cot_mine[:, span], hidden[:half, :])
        grad = grad + matmul_tn(cot_other[:, span], hidden[half:, :])
        scratch[...] = grad.astype(BF16)
        deal(where, scratch, k, send, keep, rows)


def weight_grad_kernel(
    where, normed, gate_grad, up_grad, gate_send, gate_keep, up_send, up_keep, scratch
):
    cols, rows = gate_send.shape[1], gate_send.shape[2]
    part = normed.shape[1] // cols
    for upstream, send, keep in ((gate_grad, gate_send, gate_keep), (up_grad, up_send, up_keep)):
        for k in range(cols):
            span = slice(k * part, (k + 1) * part)
            scratch[...] = matmul_tn(normed[:, span], upstream[...]).astype(BF16)
            deal(where, scratch, k, send, keep, rows)


def pack_tokens_kernel(where, ours, came, out0, out1, out2, out3, scratch):
    outs = (out0, out1, out2, out3)
    share, part = out0.shape[0], out0.shape[1] // len(outs)
    scratch[...] = (ours[...].astype(F32) + came[...].astype(F32)).astype(BF16)
    for k, out in enumerate(outs):
        rows = pl.ds(pl.multiple_of((where[1] ^ k) * share, share), share)
        for j in range(len(outs)):
            source = k ^ j
            out[:, j * part : (j + 1) * part] = scratch[rows, source * part : (source + 1) * part]


def second_norm_kernel(
    where, came0, came1, came2, came3, sums, cot_mine, first0, first1, first2, first3,
    out0, out1, out2, out3, gain_out,
):
    buffers = (first0, first1, first2, first3)
    outs = (out0, out1, out2, out3)
    share, part = out0.shape[0], out0.shape[1] // len(outs)
    half = share * len(outs)
    grad = came0[...].astype(F32) + came1[...].astype(F32)
    grad = grad + came2[...].astype(F32) + came3[...].astype(F32)
    gain = jnp.concatenate([gain_row(buffers, half + 3, k) for k in range(len(buffers))], axis=1)
    rows = sums[...]
    root = lax.rsqrt(jnp.mean(rows * rows, axis=1, keepdims=True) + EPSILON)
    normal = rows * root
    weighted = grad * gain
    gain_out[...] = jnp.sum(grad * normal, axis=0, keepdims=True)
    inner = jnp.mean(weighted * normal, axis=1, keepdims=True)
    cot = cot_mine[pl.ds(pl.multiple_of(where[1] * share, share), share), :].astype(F32)
    first = (cot + root * (weighted - normal * inner)).astype(BF16)
    for k, out in enumerate(outs):
        for j in range(len(outs)):
            source = k ^ j
            out[:, j * part : (j + 1) * part] = first[:, source * part : (source + 1) * part]


def join_tokens_kernel(where, came0, came1, came2, came3, out):
    share = came0.shape[0]
    for k, came in enumerate((came0, came1, came2, came3)):
        out[pl.ds(pl.multiple_of((where[1] ^ k) * share, share), share), :] = came[...]


def pack_features_kernel(ours, came, out0, out1, out2, out3):
    part = out0.shape[1]
    for k, out in enumerate((out0, out1, out2, out3)):
        span = slice(k * part, (k + 1) * part)
        out[...] = (ours[:, span].astype(F32) + came[:, span].astype(F32)).astype(BF16)


def pack_last_kernel(ours, came, inner, inner_came, out0, out1, out2, out3):
    half, part = ours.shape[0], out0.shape[1]
    line = lax.broadcasted_iota(jnp.int32, (16, part), 0)
    rows = jnp.zeros((16, part), F32)
    rest = inner[0:1, :half] + inner_came[0:1, :]
    for p in range(3):
        piece = rest.astype(BF16).astype(F32)
        rows = jnp.where(line == p, piece, rows)
        rest = rest - piece
    for k, out in enumerate((out0, out1, out2, out3)):
        span = slice(k * part, (k + 1) * part)
        out[:half, :] = (ours[:, span].astype(F32) + came[:, span].astype(F32)).astype(BF16)
        out[half:, :] = rows.astype(BF16)


def join_first_kernel(first0, first1, first2, first3, out):
    part, size = first0.shape[1], out.shape[0]
    for k, piece in enumerate((first0, first1, first2, first3)):
        out[:, k * part : (k + 1) * part] = piece[:size, :]


def in_chip_order(where, pieces):
    odd, high = (where[1] & 1) == 1, (where[1] & 2) == 2
    ordered = []
    for s in range(4):
        low_pair = jnp.where(odd, pieces[s ^ 1], pieces[s])
        high_pair = jnp.where(odd, pieces[s ^ 3], pieces[s ^ 2])
        ordered.append(jnp.where(high, high_pair, low_pair))
    return ordered


def unpack_feed_kernel(where, came0, came1, came2, came3, down_out, gate_out, up_out):
    rows = gate_out.shape[0]
    pieces = in_chip_order(where, [v[...] for v in (came0, came1, came2, came3)])
    for i, out in enumerate((down_out, gate_out, up_out)):
        span = slice(i * rows, (i + 1) * rows)
        out[...] = jnp.concatenate([v[span].astype(F32) for v in pieces], axis=1)


def unpack_mixed_kernel(
    where, came0, came1, came2, came3, query_out, key_out, value_out, output_out, gain_out
):
    rows = query_out.shape[0]
    pieces = in_chip_order(where, [v[...] for v in (came0, came1, came2, came3)])
    two = query_out.shape[1] // len(pieces)
    size = two // 2
    pieces = [v.astype(F32) for v in pieces]
    for out, start, wide in (
        (query_out, 0, two), (key_out, two, size), (value_out, two + size, size),
        (output_out, 2 * two, two),
    ):
        out[...] = jnp.concatenate([v[:rows, start : start + wide] for v in pieces], axis=1)
    gain_out[...] = pieces[0][rows:] + pieces[1][rows:] + pieces[2][rows:] + pieces[3][rows:]


def lane_is_first(size):
    return lax.broadcasted_iota(jnp.int32, (1, 2 * size), 1) < size


def head_scale(values, first):
    size = values.shape[1] // 2
    squares = values * values
    left = jnp.sum(jnp.where(first, squares, 0.0), axis=1, keepdims=True)
    right = jnp.sum(jnp.where(first, 0.0, squares), axis=1, keepdims=True)
    return lax.rsqrt(jnp.where(first, left, right) / size + EPSILON)


def turn(values, cosine, sine):
    width = values.shape[1]
    quarter = width // 4
    lane = lax.broadcasted_iota(jnp.int32, (1, width), 1)
    low = (lane & quarter) == 0
    other = jnp.where(
        low, pltpu.roll(values, width - quarter, 1), pltpu.roll(values, quarter, 1)
    )
    return values * cosine + other * sine


def root_and_input(mine, other):
    rows = jnp.concatenate([mine[...], other[...]], axis=0).astype(F32)
    mean = jnp.mean(rows * rows, axis=1, keepdims=True)
    return rows, lax.rsqrt(mean + EPSILON)


def gain_row(buffers, start, k):
    rows = buffers[k][start : start + 16, :].astype(F32)
    return rows[0:1] + rows[1:2] + rows[2:3]


def allowed_of(down, across):
    return (across[0:1, :] <= down[:, 0:1]) & (across[1:2, :] == down[:, 1:2])


def attend_kernel(
    mine, other, first0, first1, first2, first3, cosine, sine, gains, down, across,
    qkv_out, turned_out, context_out, log_out,
):
    buffers = (first0, first1, first2, first3)
    half, part = mine.shape[0], first0.shape[1]
    rows, root = root_and_input(mine, other)
    start = half + 16
    qkv = None
    for k, buffer in enumerate(buffers):
        block = rows[:, k * part : (k + 1) * part] * root * gain_row(buffers, half, k)
        term = matmul(block.astype(BF16), buffer[start:, :])
        qkv = term if qkv is None else qkv + term
    qkv_out[...] = qkv
    two = qkv.shape[1] // 2
    size = two // 2
    first = lane_is_first(size)
    query, pair = qkv[:, :two], qkv[:, two:]
    query_turned = turn(
        query * head_scale(query, first) * gains[0:1, :], cosine[...], sine[...]
    ).astype(BF16)
    key_turned = turn(pair * head_scale(pair, first) * gains[1:2, :], cosine[...], sine[...])
    pair_rounded = jnp.where(first, key_turned, pair).astype(BF16)
    turned_out[:, :two] = query_turned
    turned_out[:, two:] = pair_rounded
    key, value = pair_rounded[:, :size], pair_rounded[:, size:]
    allowed = allowed_of(down, across)
    contexts, logs = [], []
    for h in range(2):
        raw = matmul_nt(query_turned[:, h * size : (h + 1) * size], key)
        scores = jnp.where(allowed, raw * size ** (-0.5), NEGATIVE)
        top = jnp.max(scores, axis=1, keepdims=True)
        powers = jnp.exp(scores - top)
        sums = jnp.sum(powers, axis=1, keepdims=True)
        prob = (powers * (1.0 / sums)).astype(BF16)
        contexts.append(matmul(prob, value))
        logs.append(top + jnp.log(sums))
    context_out[...] = jnp.concatenate(contexts, axis=1).astype(BF16)
    log_out[...] = jnp.where(first, logs[0], logs[1])


def attend_back_kernel(
    where, mine, other, first0, first1, first2, first3, cosine, sine, gains, down, across,
    qkv_in, turned, context_in, logs, grad_mine, grad_other, out_weight,
    gain_in, one_mine, one_other, inner_out, mixed_send, mixed_keep, mixed,
):
    buffers = (first0, first1, first2, first3)
    half, part = mine.shape[0], first0.shape[1]
    two = context_in.shape[1]
    size = two // 2
    first = lane_is_first(size)
    upstream = jnp.concatenate([grad_mine[...], grad_other[...]], axis=0)
    context = context_in[...]
    context_grad = matmul_nt(upstream, out_weight[:two, :]).astype(BF16)
    key, value = turned[:, two : two + size], turned[:, two + size :]
    allowed = allowed_of(down, across)
    products = context_grad.astype(F32) * context.astype(F32)
    query_grads = []
    key_grad = value_grad = None
    for h in range(2):
        query = turned[:, h * size : (h + 1) * size]
        grad = context_grad[:, h * size : (h + 1) * size]
        raw = matmul_nt(query, key)
        scores = jnp.where(allowed, raw * size ** (-0.5), NEGATIVE)
        prob = jnp.exp(scores - logs[:, h * size : h * size + 1])
        delta = jnp.sum(
            jnp.where(first if h == 0 else jnp.logical_not(first), products, 0.0),
            axis=1,
            keepdims=True,
        )
        value_term = matmul_tn(prob.astype(BF16), grad)
        score_grad = (prob * (matmul_nt(grad, value) - delta) * size ** (-0.5)).astype(BF16)
        query_grads.append(matmul(score_grad, key))
        key_term = matmul_tn(score_grad, query)
        key_grad = key_term if h == 0 else key_grad + key_term
        value_grad = value_term if h == 0 else value_grad + value_term
    pieces, head_parts = [], []
    for i, grad in enumerate(
        (jnp.concatenate(query_grads, axis=1), jnp.concatenate([key_grad, value_grad], axis=1))
    ):
        normed = turn(grad, cosine[...], -sine[...])
        proj = qkv_in[:, i * two : (i + 1) * two]
        scale = head_scale(proj, first)
        hat = proj * scale
        weighted = normed * gains[i : i + 1, :]
        product = weighted * hat
        left = jnp.sum(jnp.where(first, product, 0.0), axis=1, keepdims=True)
        right = jnp.sum(jnp.where(first, 0.0, product), axis=1, keepdims=True)
        inner = jnp.where(first, left, right) / size
        result = scale * (weighted - hat * inner)
        pieces.append(result if i == 0 else jnp.where(first, result, grad))
        head_parts.append(jnp.sum(normed * hat, axis=0, keepdims=True))
    head_line = head_parts[0] + pltpu.roll(head_parts[0], size, 1)
    head_line = jnp.where(first, head_line, pltpu.roll(head_parts[1], size, 1))
    rows_here = mixed_send.shape[2] - 8
    line = lax.broadcasted_iota(jnp.int32, (8, part), 0)
    qkv_grad = jnp.concatenate(pieces, axis=1).astype(BF16)
    rows, root = root_and_input(mine, other)
    inner_sum = jnp.zeros((2 * half, 1), F32)
    for k, buffer in enumerate(buffers):
        span = slice(k * part, (k + 1) * part)
        gain = gain_row(buffers, half, k)
        hat = rows[:, span] * root
        grad = matmul_nt(qkv_grad, buffer[half + 16 :, :])
        product = grad * hat
        lines = jnp.where(line == 0, jnp.sum(product, axis=0, keepdims=True), 0.0)
        lines = jnp.where(line == 1, gain_in[:, span], lines).astype(BF16)
        inner_sum = inner_sum + jnp.sum(product * gain, axis=1, keepdims=True)
        one_mine[:, span] = grad[:half].astype(BF16)
        one_other[:, span] = grad[half:].astype(BF16)
        mixed[:, : 2 * two] = matmul_tn((hat * gain).astype(BF16), qkv_grad).astype(BF16)
        mixed[:, 2 * two :] = matmul_tn(upstream[:, span], context).astype(BF16)
        heads = jnp.broadcast_to(head_line, (8, two)).astype(BF16)
        if mixed_send.shape[0] == 2:
            deal(where, mixed, k, mixed_send, mixed_keep, rows_here)
            for out in (mixed_send, mixed_keep):
                for j in range(2):
                    out[j, k, rows_here:, : 2 * two] = lines
                    out[j, k, rows_here:, 2 * two :] = heads
        else:
            mixed_send[k, ...] = mixed[...]
            mixed_keep[k, :, : 2 * two] = lines
            mixed_keep[k, :, 2 * two :] = heads
    wide = jnp.broadcast_to(inner_sum / (part * len(buffers)), (2 * half, 128))
    inner_out[...] = jnp.transpose(wide)[:8, :]


def rope_tables(places, head_size):
    half_size = head_size // 2
    frequency = THETA ** (-(jnp.arange(half_size).astype(F32) * 2.0 / head_size))
    angles = places.astype(F32)[:, None] * frequency[None, :]
    return (jnp.cos(angles), jnp.sin(angles))


def body(
    block_input,
    segments,
    positions,
    attention_gain,
    query_weight,
    key_weight,
    value_weight,
    query_gain,
    key_gain,
    output_weight,
    feedforward_gain,
    gate_weight,
    up_weight,
    down_weight,
    cotangent,
):
    tokens = block_input.shape[0]
    part = block_input.shape[1]
    head = query_gain.shape[0]
    cols = lax.axis_size("col")
    planes = lax.axis_size("dp")
    width = part * cols
    half = tokens // 2
    row = lax.axis_index("row")
    col = lax.axis_index("col")
    plane = lax.axis_index("dp")

    def mine_first(values):
        return jnp.where(row == 0, values, jnp.roll(values, half, axis=0))

    def natural(values):
        return jnp.where(row == 0, values, jnp.roll(values, half, axis=0))

    def both_rows(values):
        return jnp.concatenate([values, flip(values, "row", 1)], axis=0)

    q_size = query_weight.shape[1] // cols
    units = gate_weight.shape[1] // cols
    where = jnp.stack([row, col, plane]).astype(jnp.int32)
    shapes = [((half + 16 + part, part), BF16)] * cols
    first_in = exchange(
        kernel_call(
            pack_one_kernel,
            shapes,
            block_input,
            query_weight,
            key_weight,
            value_weight,
            attention_gain.reshape(1, part),
            feedforward_gain.reshape(1, part),
            scalars=where,
            fetch=4, room=60),
    )
    (input_mine,) = kernel_call(join_first_kernel, [((half, width), BF16)], *first_in, room=10)
    gain_parts = jnp.concatenate([v[half : half + 16] for v in first_in], axis=1).astype(F32)
    gain_one = gain_parts[0] + gain_parts[1] + gain_parts[2]
    input_other = flip(input_mine, "row", 1)
    gate_in = kernel_call(
        pack_gate_kernel,
        [((part, units), BF16)] * (cols + 1),
        gate_weight,
        up_weight,
        scalars=where,
        fetch=2, room=12)
    near_parts = exchange(gate_in[:cols])
    far_parts = [gate_in[cols]] + [flip(v, "dp", 1) for v in near_parts[1:]]
    inner_size = output_weight.shape[0]
    two_out = kernel_call(
        pack_two_kernel,
        [((half + inner_size, part), BF16)] * cols,
        output_weight,
        cotangent,
        scalars=where,
        fetch=2,
    )
    second_parts = exchange(two_out)
    three_out = kernel_call(
        pack_three_kernel,
        [((units, part), BF16)] * cols,
        down_weight,
        scalars=where,
        fetch=1,
    )
    down_parts = exchange(three_out)

    group = q_size // head
    segment_ids = mine_first(segments)
    places = mine_first(positions)
    index = mine_first(jnp.arange(tokens))

    cosine, sine_part = rope_tables(places, head)
    cos_lanes = jnp.concatenate([cosine] * (2 * group), axis=1)
    sin_lanes = jnp.concatenate([-sine_part, sine_part] * group, axis=1)
    head_gains = jnp.stack([jnp.tile(query_gain, group), jnp.tile(key_gain, group)])
    down = jnp.stack([index, segment_ids], axis=1)
    across = jnp.stack([index, segment_ids])
    common = (
        input_mine,
        input_other,
        *first_in,
        cos_lanes,
        sin_lanes,
        head_gains,
        down,
        across,
    )
    qkv, turned, context, logs = kernel_call(
        attend_kernel,
        [
            ((tokens, 2 * q_size), F32),
            ((tokens, 2 * q_size), BF16),
            ((tokens, q_size), BF16),
            ((tokens, q_size), F32),
        ],
        *common, room=26)

    context_parts = spread(context)
    (context_near,) = kernel_call(join_kernel, [((tokens, inner_size), BF16)], *context_parts, room=10)
    context_far = flip(context_near, "row", 1)
    (second_in,) = kernel_call(join_kernel, [((inner_size, width), BF16)], *second_parts, room=10)
    second_far = flip(second_in, "row", 1)
    (cot_mine,) = kernel_call(join_first_kernel, [((half, width), BF16)], *second_parts, room=10)
    cot_other = flip(cot_mine, "row", 1)

    share = half // cols
    normed_two, first_block, first_share = kernel_call(
        project_kernel,
        [((tokens, width), BF16), ((half, part), F32), ((share, width), F32)],
        input_mine,
        input_other,
        context_near,
        context_far,
        second_in,
        second_far,
        *first_in,
        scalars=where,
        scratch=[((half, width), F32)], room=24)
    gate_pre, up_pre, hidden = kernel_call(
        hidden_kernel,
        [((tokens, units), F32), ((tokens, units), F32), ((tokens, units), BF16)],
        normed_two,
        *near_parts,
        *far_parts,
        scalars=where, room=24)
    rows = part // planes
    if planes == 4:
        down_dealt = kernel_call(
            down_grad_kernel,
            [((2, cols, rows, units), BF16)] * 2,
            cot_mine,
            cot_other,
            hidden,
            scalars=where,
            scratch=[((part, units), BF16)], room=14)
    gate_grad, up_grad, two_mine, two_other = kernel_call(
        backward_kernel,
        [((tokens, units), BF16)] * 2 + [((half, width), BF16)] * 2,
        cot_mine,
        cot_other,
        gate_pre,
        up_pre,
        *down_parts,
        *near_parts,
        *far_parts,
        scalars=where, room=30)

    two_came = flip(two_other, "row", 1)
    two_pieces = kernel_call(
        pack_tokens_kernel,
        [((share, width), BF16)] * cols,
        two_mine,
        two_came,
        scalars=where,
        scratch=[((half, width), BF16)],
    )
    two_in = exchange(two_pieces)
    *first_pieces, feedforward_part = kernel_call(
        second_norm_kernel,
        [((share, width), BF16)] * cols + [((1, width), F32)],
        *two_in,
        first_share,
        cot_mine,
        *first_in,
        scalars=where,
    )
    first_back = exchange(first_pieces)
    (first_half,) = kernel_call(
        join_tokens_kernel, [((half, width), BF16)], *first_back, scalars=where
    )
    first_other = flip(first_half, "row", 1)

    def summed(send, keep):
        came = flip(send, "dp", 1)
        rest = (keep[1].astype(F32) + came[1].astype(F32)).astype(BF16)
        far = flip(rest, "dp", 2)
        return total([keep[0], came[0], far]).astype(BF16)

    def scattered(split):
        return lax.psum_scatter(split, "dp", scatter_dimension=0, tiled=True)[0]

    if planes == 4:
        dealt = kernel_call(
            weight_grad_kernel,
            [((2, cols, rows, units), BF16)] * 4,
            normed_two,
            gate_grad,
            up_grad,
            scalars=where,
            scratch=[((part, units), BF16)], room=20)
        dealt = list(down_dealt) + list(dealt)
        sums = [summed(dealt[2 * i], dealt[2 * i + 1]) for i in range(3)]
    else:
        cot_all = jnp.concatenate([cot_mine, cot_other], axis=0)
        sums = [
            scattered(
                jnp.moveaxis(grad.astype(BF16).reshape(cols, planes, rows, units), 1, 0)
            )
            for grad in (
                matmul_tn(cot_all, hidden),
                matmul_tn(normed_two, gate_grad),
                matmul_tn(normed_two, up_grad),
            )
        ]
    feed_in = exchange([jnp.concatenate([v[k] for v in sums], axis=0) for k in range(cols)])
    down_share, gate_share, up_share = kernel_call(
        unpack_feed_kernel, [((rows, cols * units), F32)] * 3, *feed_in, scalars=where, room=12)

    result_mine, result_other = kernel_call(
        result_kernel, [((half, width), BF16)] * 2, hidden, *down_parts, room=12)
    result_came = flip(result_other, "row", 1)
    result_pieces = kernel_call(
        pack_features_kernel, [((half, part), BF16)] * cols, result_mine, result_came
    )
    result_in = exchange(result_pieces)
    result_mine = (first_block + total(result_in)).astype(BF16)
    block_output = natural(both_rows(result_mine))

    mixed_size = 3 * q_size
    if planes == 4:
        mixed_outs = [((2, cols, rows + 8, mixed_size), BF16)] * 2
    else:
        mixed_outs = [((cols, part, mixed_size), BF16), ((cols, 8, mixed_size), BF16)]
    one_mine, one_other, inner_part, mixed_first, mixed_second = kernel_call(
        attend_back_kernel,
        [((half, width), BF16), ((half, width), BF16), ((8, tokens), F32)] + mixed_outs,
        *common,
        qkv,
        turned,
        context,
        logs,
        first_half,
        first_other,
        second_in,
        feedforward_part,
        scalars=where,
        scratch=[((part, mixed_size), BF16)], room=34)
    one_came = flip(one_other, "row", 1)
    inner_came = flip(inner_part[:, half:], "row", 1)
    one_pieces = kernel_call(
        pack_last_kernel,
        [((half + 16, part), BF16)] * cols,
        one_mine,
        one_came,
        inner_part,
        inner_came, room=10)
    one_in = exchange(one_pieces)
    one_grad = total([v[:half] for v in one_in])
    inner_one = jnp.sum(total([v[half:] for v in one_in])[:3], axis=0)[:, None]
    weighted_one = one_grad * gain_one[:part]
    own_input = input_mine.astype(F32)
    root_one = lax.rsqrt(jnp.mean(own_input * own_input, axis=1, keepdims=True) + EPSILON)
    normal_one = own_input[:, :part] * root_one
    input_mine_grad = first_half[:, :part].astype(F32) + root_one * (
        weighted_one - normal_one * inner_one
    )
    input_grad = natural(both_rows(input_mine_grad))

    if planes == 4:
        mixed_sum = summed(mixed_first, mixed_second)
    else:
        lines = jnp.broadcast_to(mixed_second[:, None], (cols, planes, 8, mixed_size))
        blocks = mixed_first.reshape(cols, planes, rows, mixed_size)
        mixed_sum = scattered(jnp.moveaxis(jnp.concatenate([blocks, lines], axis=2), 1, 0))
    mixed_in = exchange([mixed_sum[k] for k in range(cols)])
    query_share, key_share, value_share, output_share, gain_sums = kernel_call(
        unpack_mixed_kernel,
        [
            ((rows, cols * q_size), F32),
            ((rows, cols * head), F32),
            ((rows, cols * head), F32),
            ((rows, cols * q_size), F32),
            ((8, mixed_size), F32),
        ],
        *mixed_in,
        scalars=where,
    )
    gain_sums = gain_sums + flip(gain_sums, "row", 1)
    attention_share = lax.dynamic_slice_in_dim(gain_sums[0], plane * rows, rows, 0)
    feedforward_share = lax.dynamic_slice_in_dim(gain_sums[1], plane * rows, rows, 0)
    query_gain_grad = gain_sums[0, 2 * q_size : 2 * q_size + head]
    key_gain_grad = gain_sums[0, 2 * q_size + head :]
    return (
        block_output,
        input_grad,
        attention_share,
        query_share,
        key_share,
        value_share,
        query_gain_grad,
        key_gain_grad,
        output_share.T,
        feedforward_share,
        gate_share,
        up_share,
        down_share.T,
    )


def solution(mesh):
    placed = (
        P("dp", "col"),
        P("dp"),
        P("dp"),
        P("col"),
        P("col", "row"),
        P("col", "row"),
        P("col", "row"),
        P(),
        P(),
        P("row", "col"),
        P("col"),
        P("col", "row"),
        P("col", "row"),
        P("row", "col"),
        P("dp", "col"),
    )


    return jax.shard_map(
        body,
        mesh=mesh,
        in_specs=placed,
        out_specs=(
            P("dp", "col"),
            P("dp", "col"),
            P(("col", "dp")),
            P(("col", "dp"), "row"),
            P(("col", "dp"), "row"),
            P(("col", "dp"), "row"),
            P(),
            P(),
            P("row", ("col", "dp")),
            P(("col", "dp")),
            P(("col", "dp"), "row"),
            P(("col", "dp"), "row"),
            P("row", ("col", "dp")),
        ),
        check_vma=False,
    )
```

```python
import jax
import jax.numpy as jnp
from jax import lax
from jax.experimental import pallas as pl
from jax.experimental.pallas import tpu as pltpu
from jax.sharding import PartitionSpec as P


EPSILON = 1e-05
THETA = 1000000.0
NEGATIVE = -1e30


F32 = jnp.float32
BF16 = jnp.bfloat16


def matmul(left, right):
    return jnp.dot(left, right, preferred_element_type=F32)


def matmul_nt(left, right):
    return lax.dot_general(left, right, (((1,), (1,)), ((), ())), preferred_element_type=F32)


def matmul_tn(left, right):
    return lax.dot_general(left, right, (((0,), (0,)), ((), ())), preferred_element_type=F32)


def flip(values, axis, distance):
    size = lax.axis_size(axis)
    return lax.ppermute(values, axis, [(i, i ^ distance) for i in range(size)])


def spread(values):
    return [values] + [flip(values, "col", k) for k in range(1, lax.axis_size("col"))]


def exchange(pieces):
    return [pieces[0]] + [flip(pieces[k], "col", k) for k in range(1, len(pieces))]


def total(parts):
    result = parts[0].astype(F32)
    for part in parts[1:]:
        result = result + part.astype(F32)
    return result


def kernel_call(kernel, outs, *args, scalars=None, scratch=(), fetch=0, room=8):
    specs = [pl.BlockSpec(memory_space=pltpu.HBM)] * fetch
    specs = specs + [pl.BlockSpec(memory_space=pltpu.VMEM)] * (len(args) - fetch)
    scratch_shapes = [pltpu.VMEM(shape, dtype) for shape, dtype in scratch]
    if fetch:
        scratch_shapes = [pltpu.VMEM(v.shape, v.dtype) for v in args[:fetch]] + scratch_shapes
        scratch_shapes.append(pltpu.SemaphoreType.DMA((fetch,)))
    if scalars is not None:
        args = (scalars,) + args
        specs = [pl.BlockSpec(memory_space=pltpu.SMEM)] + specs
    return pl.pallas_call(
        kernel,
        out_shape=[jax.ShapeDtypeStruct(shape, dtype) for shape, dtype in outs],
        in_specs=specs,
        out_specs=[pl.BlockSpec(memory_space=pltpu.VMEM)] * len(outs),
        scratch_shapes=scratch_shapes,
        compiler_params=pltpu.CompilerParams(vmem_limit_bytes=room * 1024 * 1024),
    )(*args)


def fetched(sources, targets, semaphores):
    copies = [
        pltpu.make_async_copy(source, target, semaphores.at[i])
        for i, (source, target) in enumerate(zip(sources, targets))
    ]
    for copy in copies:
        copy.start()
    for copy in copies:
        copy.wait()


def pack_one_kernel(
    where, x_in, query_in, key_in, value_in, gain_first, gain_second,
    out0, out1, out2, out3, x, query, key, value, semaphores,
):
    fetched((x_in, query_in, key_in, value_in), (x, query, key, value), semaphores)
    outs = (out0, out1, out2, out3)
    row, col = where[0], where[1]
    half = x.shape[0] // 2
    cols = len(outs)
    q_size, kv_size = query.shape[1] // cols, key.shape[1] // cols
    line = lax.broadcasted_iota(jnp.int32, (16, x.shape[1]), 0)
    rows = jnp.zeros((16, x.shape[1]), F32)
    for g, gain in enumerate((gain_first, gain_second)):
        rest = gain[...]
        for p in range(3):
            part = rest.astype(BF16).astype(F32)
            rows = jnp.where(line == 3 * g + p, part, rows)
            rest = rest - part
    mine = x[pl.ds(pl.multiple_of(row * half, half), half), :]
    for k, out in enumerate(outs):
        block = col ^ k
        out[:half, :] = mine
        out[half : half + 16, :] = rows.astype(BF16)
        out[half + 16 :, :q_size] = query[:, pl.ds(pl.multiple_of(block * q_size, q_size), q_size)]
        pair = pl.multiple_of((block >> 1) * (2 * kv_size), 2 * kv_size)
        odd = (block & 1) == 1
        both = []
        for weight in (key, value):
            two = weight[:, pl.ds(pair, 2 * kv_size)]
            both.append(jnp.where(odd, two[:, kv_size:], two[:, :kv_size]))
        out[half + 16 :, q_size:] = jnp.concatenate(both, axis=1)


def pack_two_kernel(
    where, weight_in, cot_in, out0, out1, out2, out3, weight, cot, semaphores
):
    fetched((weight_in, cot_in), (weight, cot), semaphores)
    outs = (out0, out1, out2, out3)
    size, half = weight.shape[0] // len(outs), cot.shape[0] // 2
    for k, out in enumerate(outs):
        out[:half, :] = cot[pl.ds(pl.multiple_of(where[0] * half, half), half), :]
        for j in range(len(outs)):
            source = pl.multiple_of((where[1] ^ (k ^ j)) * size, size)
            out[half + j * size : half + (j + 1) * size, :] = weight[pl.ds(source, size), :]


def pack_three_kernel(where, down_in, out0, out1, out2, out3, down, semaphores):
    fetched((down_in,), (down,), semaphores)
    outs = (out0, out1, out2, out3)
    size = down.shape[0] // len(outs)
    for k, out in enumerate(outs):
        out[...] = down[pl.ds(pl.multiple_of((where[1] ^ k) * size, size), size), :]


def pack_gate_kernel(
    where, gate_in, up_in, out0, out1, out2, out3, out4, gate, up, semaphores
):
    fetched((gate_in, up_in), (gate, up), semaphores)
    outs = (out0, out1, out2, out3, out4)
    col, odd_plane = where[1], (where[2] & 1) == 1
    cols = len(outs) - 1
    size = gate.shape[1] // cols

    def piece(weight, block):
        two = weight[:, pl.ds(pl.multiple_of((block >> 1) * (2 * size), 2 * size), 2 * size)]
        return jnp.where((block & 1) == 1, two[:, size:], two[:, :size])

    @pl.when(jnp.logical_not(odd_plane))
    def _():
        for k in range(cols):
            outs[k][...] = piece(gate, col ^ k)
        outs[cols][...] = piece(up, col)

    @pl.when(odd_plane)
    def _():
        for k in range(cols):
            outs[k][...] = piece(up, col ^ k)
        outs[cols][...] = piece(gate, col)


def join_kernel(first0, first1, first2, first3, out):
    part, size = first0.shape[1], out.shape[0]
    for k, piece in enumerate((first0, first1, first2, first3)):
        out[:, k * part : (k + 1) * part] = piece[piece.shape[0] - size :, :]


def project_kernel(
    where, mine, other, context_near, context_far, joined, joined_far,
    first0, first1, first2, first3, normed_out, own_out, share_out, sum_scratch,
):
    buffers = (first0, first1, first2, first3)
    half, part = mine.shape[0], first0.shape[1]
    share = share_out.shape[0]
    top = mine[...].astype(F32) + matmul(context_near[:half, :], joined[...])
    top = top + matmul(context_far[half:, :], joined_far[...])
    low = other[...].astype(F32) + matmul(context_near[half:, :], joined[...])
    low = low + matmul(context_far[:half, :], joined_far[...])
    sum_scratch[...] = top
    own_out[...] = top[:, :part]
    share_out[...] = sum_scratch[pl.ds(pl.multiple_of(where[1] * share, share), share), :]
    gain = jnp.concatenate([gain_row(buffers, half + 3, k) for k in range(len(buffers))], axis=1)
    for i, rows in enumerate((top, low)):
        root = lax.rsqrt(jnp.mean(rows * rows, axis=1, keepdims=True) + EPSILON)
        normed_out[i * half : (i + 1) * half, :] = (rows * root * gain).astype(BF16)


def hidden_kernel(
    where, normed, near0, near1, near2, near3, far0, far1, far2, far3,
    gate_out, up_out, hidden_out,
):
    part = near0.shape[0]
    first_pre = second_pre = None
    for k, (near, far) in enumerate(
        ((near0, far0), (near1, far1), (near2, far2), (near3, far3))
    ):
        block = normed[:, k * part : (k + 1) * part]
        one, two = matmul(block, near[...]), matmul(block, far[...])
        first_pre = one if k == 0 else first_pre + one
        second_pre = two if k == 0 else second_pre + two
    even = (where[2] & 1) == 0
    gate_pre = jnp.where(even, first_pre, second_pre)
    up_pre = jnp.where(even, second_pre, first_pre)
    gate_out[...] = gate_pre
    up_out[...] = up_pre
    hidden_out[...] = (gate_pre * (1.0 / (1.0 + jnp.exp(-gate_pre))) * up_pre).astype(BF16)


def backward_kernel(
    where, cot_mine, cot_other, gate_in, up_in, down0, down1, down2, down3,
    near0, near1, near2, near3, far0, far1, far2, far3,
    gate_grad_out, up_grad_out, mine_out, other_out,
):
    half, part = mine_out.shape[0], near0.shape[0]
    size = gate_in.shape[1]
    parts = []
    for rows in (cot_mine, cot_other):
        grad = None
        for k, down in enumerate((down0, down1, down2, down3)):
            term = matmul_nt(rows[:, k * part : (k + 1) * part], down[:size, :])
            grad = term if k == 0 else grad + term
        parts.append(grad)
    hidden_grad = jnp.concatenate(parts, axis=0)
    gate_pre, up_pre = gate_in[...], up_in[...]
    sigmoid_gate = 1.0 / (1.0 + jnp.exp(-gate_pre))
    gate_grad = (
        hidden_grad * up_pre * sigmoid_gate * (1.0 + gate_pre * (1.0 - sigmoid_gate))
    ).astype(BF16)
    up_grad = (hidden_grad * (gate_pre * sigmoid_gate)).astype(BF16)
    gate_grad_out[...] = gate_grad
    up_grad_out[...] = up_grad
    even = (where[2] & 1) == 0
    near_grad = jnp.where(even, gate_grad, up_grad)
    far_grad = jnp.where(even, up_grad, gate_grad)
    for k, (near, far) in enumerate(
        ((near0, far0), (near1, far1), (near2, far2), (near3, far3))
    ):
        block = matmul_nt(near_grad, near[...]) + matmul_nt(far_grad, far[...])
        mine_out[:, k * part : (k + 1) * part] = block[:half].astype(BF16)
        other_out[:, k * part : (k + 1) * part] = block[half:].astype(BF16)


def result_kernel(hidden, down0, down1, down2, down3, mine_out, other_out):
    half, part = mine_out.shape[0], down0.shape[1]
    for k, down in enumerate((down0, down1, down2, down3)):
        block = matmul(hidden[...], down[: hidden.shape[1], :])
        mine_out[:, k * part : (k + 1) * part] = block[:half].astype(BF16)
        other_out[:, k * part : (k + 1) * part] = block[half:].astype(BF16)


def deal(where, scratch, k, send, keep, rows):
    for j in range(2):
        for out, m in ((send, 1 + 2 * j), (keep, 2 * j)):
            start = pl.multiple_of((where[2] ^ m) * rows, rows)
            out[j, k, :rows, :] = scratch[pl.ds(start, rows), :]


def down_grad_kernel(where, cot_mine, cot_other, hidden, send, keep, scratch):
    half = hidden.shape[0] // 2
    cols, rows = send.shape[1], send.shape[2]
    part = cot_mine.shape[1] // cols
    for k in range(cols):
        span = slice(k * part, (k + 1) * part)
        grad = matmul_tn(cot_mine[:, span], hidden[:half, :])
        grad = grad + matmul_tn(cot_other[:, span], hidden[half:, :])
        scratch[...] = grad.astype(BF16)
        deal(where, scratch, k, send, keep, rows)


def weight_grad_kernel(
    where, normed, gate_grad, up_grad, gate_send, gate_keep, up_send, up_keep, scratch
):
    cols, rows = gate_send.shape[1], gate_send.shape[2]
    part = normed.shape[1] // cols
    for upstream, send, keep in ((gate_grad, gate_send, gate_keep), (up_grad, up_send, up_keep)):
        for k in range(cols):
            span = slice(k * part, (k + 1) * part)
            scratch[...] = matmul_tn(normed[:, span], upstream[...]).astype(BF16)
            deal(where, scratch, k, send, keep, rows)


def pack_tokens_kernel(where, ours, came, out0, out1, out2, out3, scratch):
    outs = (out0, out1, out2, out3)
    share, part = out0.shape[0], out0.shape[1] // len(outs)
    scratch[...] = (ours[...].astype(F32) + came[...].astype(F32)).astype(BF16)
    for k, out in enumerate(outs):
        rows = pl.ds(pl.multiple_of((where[1] ^ k) * share, share), share)
        for j in range(len(outs)):
            source = k ^ j
            out[:, j * part : (j + 1) * part] = scratch[rows, source * part : (source + 1) * part]


def second_norm_kernel(
    where, came0, came1, came2, came3, sums, cot_mine, first0, first1, first2, first3,
    out0, out1, out2, out3, gain_out,
):
    buffers = (first0, first1, first2, first3)
    outs = (out0, out1, out2, out3)
    share, part = out0.shape[0], out0.shape[1] // len(outs)
    half = share * len(outs)
    grad = came0[...].astype(F32) + came1[...].astype(F32)
    grad = grad + came2[...].astype(F32) + came3[...].astype(F32)
    gain = jnp.concatenate([gain_row(buffers, half + 3, k) for k in range(len(buffers))], axis=1)
    rows = sums[...]
    root = lax.rsqrt(jnp.mean(rows * rows, axis=1, keepdims=True) + EPSILON)
    normal = rows * root
    weighted = grad * gain
    gain_out[...] = jnp.sum(grad * normal, axis=0, keepdims=True)
    inner = jnp.mean(weighted * normal, axis=1, keepdims=True)
    cot = cot_mine[pl.ds(pl.multiple_of(where[1] * share, share), share), :].astype(F32)
    first = (cot + root * (weighted - normal * inner)).astype(BF16)
    for k, out in enumerate(outs):
        for j in range(len(outs)):
            source = k ^ j
            out[:, j * part : (j + 1) * part] = first[:, source * part : (source + 1) * part]


def join_tokens_kernel(where, came0, came1, came2, came3, out):
    share = came0.shape[0]
    for k, came in enumerate((came0, came1, came2, came3)):
        out[pl.ds(pl.multiple_of((where[1] ^ k) * share, share), share), :] = came[...]


def pack_features_kernel(ours, came, out0, out1, out2, out3):
    part = out0.shape[1]
    for k, out in enumerate((out0, out1, out2, out3)):
        span = slice(k * part, (k + 1) * part)
        out[...] = (ours[:, span].astype(F32) + came[:, span].astype(F32)).astype(BF16)


def pack_last_kernel(ours, came, inner, inner_came, out0, out1, out2, out3):
    half, part = ours.shape[0], out0.shape[1]
    line = lax.broadcasted_iota(jnp.int32, (16, part), 0)
    rows = jnp.zeros((16, part), F32)
    rest = inner[0:1, :half] + inner_came[0:1, :]
    for p in range(3):
        piece = rest.astype(BF16).astype(F32)
        rows = jnp.where(line == p, piece, rows)
        rest = rest - piece
    for k, out in enumerate((out0, out1, out2, out3)):
        span = slice(k * part, (k + 1) * part)
        out[:half, :] = (ours[:, span].astype(F32) + came[:, span].astype(F32)).astype(BF16)
        out[half:, :] = rows.astype(BF16)


def join_first_kernel(first0, first1, first2, first3, out):
    part, size = first0.shape[1], out.shape[0]
    for k, piece in enumerate((first0, first1, first2, first3)):
        out[:, k * part : (k + 1) * part] = piece[:size, :]


def in_chip_order(where, pieces):
    odd, high = (where[1] & 1) == 1, (where[1] & 2) == 2
    ordered = []
    for s in range(4):
        low_pair = jnp.where(odd, pieces[s ^ 1], pieces[s])
        high_pair = jnp.where(odd, pieces[s ^ 3], pieces[s ^ 2])
        ordered.append(jnp.where(high, high_pair, low_pair))
    return ordered


def plane_sum(keep, came, far, k):
    return keep[0, k].astype(F32) + came[0, k].astype(F32) + far[k].astype(F32)


def sum_feed_kernel(
    keep0, came0, far0, keep1, came1, far1, out0, out1, out2, out3
):
    rows = keep0.shape[2]
    for k, out in enumerate((out0, out1, out2, out3)):
        out[:rows, :] = plane_sum(keep0, came0, far0, k).astype(BF16)
        out[rows:, :] = plane_sum(keep1, came1, far1, k).astype(BF16)


def sum_last_kernel(
    keep0, came0, far0, keep1, came1, far1, out0, out1, out2, out3
):
    rows, size = keep0.shape[2], keep1.shape[3]
    for k, out in enumerate((out0, out1, out2, out3)):
        out[:rows, :] = plane_sum(keep0, came0, far0, k).astype(BF16)
        out[rows:, :size] = plane_sum(keep1, came1, far1, k).astype(BF16)
        rest = out.shape[1] - size
        out[rows:, size:] = jnp.zeros((out.shape[0] - rows, rest), BF16)


def unpack_feed_kernel(where, came0, came1, came2, came3, down_out, gate_out):
    rows = gate_out.shape[0]
    pieces = in_chip_order(where, [v[...] for v in (came0, came1, came2, came3)])
    for i, out in enumerate((down_out, gate_out)):
        span = slice(i * rows, (i + 1) * rows)
        out[...] = jnp.concatenate([v[span].astype(F32) for v in pieces], axis=1)


def unpack_last_kernel(
    where, came0, came1, came2, came3,
    up_out, query_out, key_out, value_out, output_out, gain_out,
):
    rows = query_out.shape[0]
    pieces = in_chip_order(where, [v[...] for v in (came0, came1, came2, came3)])
    two = query_out.shape[1] // len(pieces)
    size = two // 2
    pieces = [v.astype(F32) for v in pieces]
    up_out[...] = jnp.concatenate([v[:rows] for v in pieces], axis=1)
    for out, start, wide in (
        (query_out, 0, two), (key_out, two, size), (value_out, two + size, size),
        (output_out, 2 * two, two),
    ):
        blocks = [v[rows : 2 * rows, start : start + wide] for v in pieces]
        out[...] = jnp.concatenate(blocks, axis=1)
    gains = [v[2 * rows :, : 3 * two] for v in pieces]
    gain_out[...] = gains[0] + gains[1] + gains[2] + gains[3]


def lane_is_first(size):
    return lax.broadcasted_iota(jnp.int32, (1, 2 * size), 1) < size


def head_scale(values, first):
    size = values.shape[1] // 2
    squares = values * values
    left = jnp.sum(jnp.where(first, squares, 0.0), axis=1, keepdims=True)
    right = jnp.sum(jnp.where(first, 0.0, squares), axis=1, keepdims=True)
    return lax.rsqrt(jnp.where(first, left, right) / size + EPSILON)


def turn(values, cosine, sine):
    width = values.shape[1]
    quarter = width // 4
    lane = lax.broadcasted_iota(jnp.int32, (1, width), 1)
    low = (lane & quarter) == 0
    other = jnp.where(
        low, pltpu.roll(values, width - quarter, 1), pltpu.roll(values, quarter, 1)
    )
    return values * cosine + other * sine


def root_and_input(mine, other):
    rows = jnp.concatenate([mine[...], other[...]], axis=0).astype(F32)
    mean = jnp.mean(rows * rows, axis=1, keepdims=True)
    return rows, lax.rsqrt(mean + EPSILON)


def gain_row(buffers, start, k):
    rows = buffers[k][start : start + 16, :].astype(F32)
    return rows[0:1] + rows[1:2] + rows[2:3]


def allowed_of(down, across):
    return (across[0:1, :] <= down[:, 0:1]) & (across[1:2, :] == down[:, 1:2])


def attend_kernel(
    mine, other, first0, first1, first2, first3, cosine, sine, gains, down, across,
    qkv_out, turned_out, context_out, log_out,
):
    buffers = (first0, first1, first2, first3)
    half, part = mine.shape[0], first0.shape[1]
    rows, root = root_and_input(mine, other)
    start = half + 16
    qkv = None
    for k, buffer in enumerate(buffers):
        block = rows[:, k * part : (k + 1) * part] * root * gain_row(buffers, half, k)
        term = matmul(block.astype(BF16), buffer[start:, :])
        qkv = term if qkv is None else qkv + term
    qkv_out[...] = qkv
    two = qkv.shape[1] // 2
    size = two // 2
    first = lane_is_first(size)
    query, pair = qkv[:, :two], qkv[:, two:]
    query_turned = turn(
        query * head_scale(query, first) * gains[0:1, :], cosine[...], sine[...]
    ).astype(BF16)
    key_turned = turn(pair * head_scale(pair, first) * gains[1:2, :], cosine[...], sine[...])
    pair_rounded = jnp.where(first, key_turned, pair).astype(BF16)
    turned_out[:, :two] = query_turned
    turned_out[:, two:] = pair_rounded
    key, value = pair_rounded[:, :size], pair_rounded[:, size:]
    allowed = allowed_of(down, across)
    contexts, logs = [], []
    for h in range(2):
        raw = matmul_nt(query_turned[:, h * size : (h + 1) * size], key)
        scores = jnp.where(allowed, raw * size ** (-0.5), NEGATIVE)
        top = jnp.max(scores, axis=1, keepdims=True)
        powers = jnp.exp(scores - top)
        sums = jnp.sum(powers, axis=1, keepdims=True)
        prob = (powers * (1.0 / sums)).astype(BF16)
        contexts.append(matmul(prob, value))
        logs.append(top + jnp.log(sums))
    context_out[...] = jnp.concatenate(contexts, axis=1).astype(BF16)
    log_out[...] = jnp.where(first, logs[0], logs[1])


def attend_back_kernel(
    where, mine, other, first0, first1, first2, first3, cosine, sine, gains, down, across,
    qkv_in, turned, context_in, logs, grad_mine, grad_other, out_weight,
    gain_in, one_mine, one_other, inner_out, mixed_send, mixed_keep, mixed,
):
    buffers = (first0, first1, first2, first3)
    half, part = mine.shape[0], first0.shape[1]
    two = context_in.shape[1]
    size = two // 2
    first = lane_is_first(size)
    upstream = jnp.concatenate([grad_mine[...], grad_other[...]], axis=0)
    context = context_in[...]
    context_grad = matmul_nt(upstream, out_weight[:two, :]).astype(BF16)
    key, value = turned[:, two : two + size], turned[:, two + size :]
    allowed = allowed_of(down, across)
    products = context_grad.astype(F32) * context.astype(F32)
    query_grads = []
    key_grad = value_grad = None
    for h in range(2):
        query = turned[:, h * size : (h + 1) * size]
        grad = context_grad[:, h * size : (h + 1) * size]
        raw = matmul_nt(query, key)
        scores = jnp.where(allowed, raw * size ** (-0.5), NEGATIVE)
        prob = jnp.exp(scores - logs[:, h * size : h * size + 1])
        delta = jnp.sum(
            jnp.where(first if h == 0 else jnp.logical_not(first), products, 0.0),
            axis=1,
            keepdims=True,
        )
        value_term = matmul_tn(prob.astype(BF16), grad)
        score_grad = (prob * (matmul_nt(grad, value) - delta) * size ** (-0.5)).astype(BF16)
        query_grads.append(matmul(score_grad, key))
        key_term = matmul_tn(score_grad, query)
        key_grad = key_term if h == 0 else key_grad + key_term
        value_grad = value_term if h == 0 else value_grad + value_term
    pieces, head_parts = [], []
    for i, grad in enumerate(
        (jnp.concatenate(query_grads, axis=1), jnp.concatenate([key_grad, value_grad], axis=1))
    ):
        normed = turn(grad, cosine[...], -sine[...])
        proj = qkv_in[:, i * two : (i + 1) * two]
        scale = head_scale(proj, first)
        hat = proj * scale
        weighted = normed * gains[i : i + 1, :]
        product = weighted * hat
        left = jnp.sum(jnp.where(first, product, 0.0), axis=1, keepdims=True)
        right = jnp.sum(jnp.where(first, 0.0, product), axis=1, keepdims=True)
        inner = jnp.where(first, left, right) / size
        result = scale * (weighted - hat * inner)
        pieces.append(result if i == 0 else jnp.where(first, result, grad))
        head_parts.append(jnp.sum(normed * hat, axis=0, keepdims=True))
    head_line = head_parts[0] + pltpu.roll(head_parts[0], size, 1)
    head_line = jnp.where(first, head_line, pltpu.roll(head_parts[1], size, 1))
    rows_here = mixed_send.shape[2] - 8
    line = lax.broadcasted_iota(jnp.int32, (8, part), 0)
    qkv_grad = jnp.concatenate(pieces, axis=1).astype(BF16)
    rows, root = root_and_input(mine, other)
    inner_sum = jnp.zeros((2 * half, 1), F32)
    for k, buffer in enumerate(buffers):
        span = slice(k * part, (k + 1) * part)
        gain = gain_row(buffers, half, k)
        hat = rows[:, span] * root
        grad = matmul_nt(qkv_grad, buffer[half + 16 :, :])
        product = grad * hat
        lines = jnp.where(line == 0, jnp.sum(product, axis=0, keepdims=True), 0.0)
        lines = jnp.where(line == 1, gain_in[:, span], lines).astype(BF16)
        inner_sum = inner_sum + jnp.sum(product * gain, axis=1, keepdims=True)
        one_mine[:, span] = grad[:half].astype(BF16)
        one_other[:, span] = grad[half:].astype(BF16)
        mixed[:, : 2 * two] = matmul_tn((hat * gain).astype(BF16), qkv_grad).astype(BF16)
        mixed[:, 2 * two :] = matmul_tn(upstream[:, span], context).astype(BF16)
        heads = jnp.broadcast_to(head_line, (8, two)).astype(BF16)
        if mixed_send.shape[0] == 2:
            deal(where, mixed, k, mixed_send, mixed_keep, rows_here)
            for out in (mixed_send, mixed_keep):
                for j in range(2):
                    out[j, k, rows_here:, : 2 * two] = lines
                    out[j, k, rows_here:, 2 * two :] = heads
        else:
            mixed_send[k, ...] = mixed[...]
            mixed_keep[k, :, : 2 * two] = lines
            mixed_keep[k, :, 2 * two :] = heads
    wide = jnp.broadcast_to(inner_sum / (part * len(buffers)), (2 * half, 128))
    inner_out[...] = jnp.transpose(wide)[:8, :]


def rope_tables(places, head_size):
    half_size = head_size // 2
    frequency = THETA ** (-(jnp.arange(half_size).astype(F32) * 2.0 / head_size))
    angles = places.astype(F32)[:, None] * frequency[None, :]
    return (jnp.cos(angles), jnp.sin(angles))


def body(
    block_input,
    segments,
    positions,
    attention_gain,
    query_weight,
    key_weight,
    value_weight,
    query_gain,
    key_gain,
    output_weight,
    feedforward_gain,
    gate_weight,
    up_weight,
    down_weight,
    cotangent,
):
    tokens = block_input.shape[0]
    part = block_input.shape[1]
    head = query_gain.shape[0]
    cols = lax.axis_size("col")
    planes = lax.axis_size("dp")
    width = part * cols
    half = tokens // 2
    row = lax.axis_index("row")
    col = lax.axis_index("col")
    plane = lax.axis_index("dp")

    def mine_first(values):
        return jnp.where(row == 0, values, jnp.roll(values, half, axis=0))

    def natural(values):
        return jnp.where(row == 0, values, jnp.roll(values, half, axis=0))

    def both_rows(values):
        return jnp.concatenate([values, flip(values, "row", 1)], axis=0)

    q_size = query_weight.shape[1] // cols
    units = gate_weight.shape[1] // cols
    where = jnp.stack([row, col, plane]).astype(jnp.int32)
    shapes = [((half + 16 + part, part), BF16)] * cols
    first_in = exchange(
        kernel_call(
            pack_one_kernel,
            shapes,
            block_input,
            query_weight,
            key_weight,
            value_weight,
            attention_gain.reshape(1, part),
            feedforward_gain.reshape(1, part),
            scalars=where,
            fetch=4, room=60),
    )
    (input_mine,) = kernel_call(join_first_kernel, [((half, width), BF16)], *first_in, room=10)
    gain_parts = jnp.concatenate([v[half : half + 16] for v in first_in], axis=1).astype(F32)
    gain_one = gain_parts[0] + gain_parts[1] + gain_parts[2]
    input_other = flip(input_mine, "row", 1)
    gate_in = kernel_call(
        pack_gate_kernel,
        [((part, units), BF16)] * (cols + 1),
        gate_weight,
        up_weight,
        scalars=where,
        fetch=2, room=12)
    near_parts = exchange(gate_in[:cols])
    far_parts = [gate_in[cols]] + [flip(v, "dp", 1) for v in near_parts[1:]]
    inner_size = output_weight.shape[0]
    two_out = kernel_call(
        pack_two_kernel,
        [((half + inner_size, part), BF16)] * cols,
        output_weight,
        cotangent,
        scalars=where,
        fetch=2,
    )
    second_parts = exchange(two_out)
    three_out = kernel_call(
        pack_three_kernel,
        [((units, part), BF16)] * cols,
        down_weight,
        scalars=where,
        fetch=1,
    )
    down_parts = exchange(three_out)

    group = q_size // head
    segment_ids = mine_first(segments)
    places = mine_first(positions)
    index = mine_first(jnp.arange(tokens))

    cosine, sine_part = rope_tables(places, head)
    cos_lanes = jnp.concatenate([cosine] * (2 * group), axis=1)
    sin_lanes = jnp.concatenate([-sine_part, sine_part] * group, axis=1)
    head_gains = jnp.stack([jnp.tile(query_gain, group), jnp.tile(key_gain, group)])
    down = jnp.stack([index, segment_ids], axis=1)
    across = jnp.stack([index, segment_ids])
    common = (
        input_mine,
        input_other,
        *first_in,
        cos_lanes,
        sin_lanes,
        head_gains,
        down,
        across,
    )
    qkv, turned, context, logs = kernel_call(
        attend_kernel,
        [
            ((tokens, 2 * q_size), F32),
            ((tokens, 2 * q_size), BF16),
            ((tokens, q_size), BF16),
            ((tokens, q_size), F32),
        ],
        *common, room=26)

    context_parts = spread(context)
    (context_near,) = kernel_call(join_kernel, [((tokens, inner_size), BF16)], *context_parts, room=10)
    context_far = flip(context_near, "row", 1)
    (second_in,) = kernel_call(join_kernel, [((inner_size, width), BF16)], *second_parts, room=10)
    second_far = flip(second_in, "row", 1)
    (cot_mine,) = kernel_call(join_first_kernel, [((half, width), BF16)], *second_parts, room=10)
    cot_other = flip(cot_mine, "row", 1)

    share = half // cols
    normed_two, first_block, first_share = kernel_call(
        project_kernel,
        [((tokens, width), BF16), ((half, part), F32), ((share, width), F32)],
        input_mine,
        input_other,
        context_near,
        context_far,
        second_in,
        second_far,
        *first_in,
        scalars=where,
        scratch=[((half, width), F32)], room=24)
    gate_pre, up_pre, hidden = kernel_call(
        hidden_kernel,
        [((tokens, units), F32), ((tokens, units), F32), ((tokens, units), BF16)],
        normed_two,
        *near_parts,
        *far_parts,
        scalars=where, room=24)
    rows = part // planes
    if planes == 4:
        down_dealt = kernel_call(
            down_grad_kernel,
            [((2, cols, rows, units), BF16)] * 2,
            cot_mine,
            cot_other,
            hidden,
            scalars=where,
            scratch=[((part, units), BF16)], room=14)
    gate_grad, up_grad, two_mine, two_other = kernel_call(
        backward_kernel,
        [((tokens, units), BF16)] * 2 + [((half, width), BF16)] * 2,
        cot_mine,
        cot_other,
        gate_pre,
        up_pre,
        *down_parts,
        *near_parts,
        *far_parts,
        scalars=where, room=30)

    two_came = flip(two_other, "row", 1)
    two_pieces = kernel_call(
        pack_tokens_kernel,
        [((share, width), BF16)] * cols,
        two_mine,
        two_came,
        scalars=where,
        scratch=[((half, width), BF16)],
    )
    two_in = exchange(two_pieces)
    *first_pieces, feedforward_part = kernel_call(
        second_norm_kernel,
        [((share, width), BF16)] * cols + [((1, width), F32)],
        *two_in,
        first_share,
        cot_mine,
        *first_in,
        scalars=where,
    )
    first_back = exchange(first_pieces)
    (first_half,) = kernel_call(
        join_tokens_kernel, [((half, width), BF16)], *first_back, scalars=where
    )
    first_other = flip(first_half, "row", 1)

    def shifted(send, keep):
        came = flip(send, "dp", 1)
        rest = (keep[1].astype(F32) + came[1].astype(F32)).astype(BF16)
        return keep, came, flip(rest, "dp", 2)

    def scattered(split):
        return lax.psum_scatter(split, "dp", scatter_dimension=0, tiled=True)[0]

    if planes == 4:
        dealt = kernel_call(
            weight_grad_kernel,
            [((2, cols, rows, units), BF16)] * 4,
            normed_two,
            gate_grad,
            up_grad,
            scalars=where,
            scratch=[((part, units), BF16)], room=20)
        dealt = list(down_dealt) + list(dealt)
        down_terms, gate_terms, up_terms = [
            shifted(dealt[2 * i], dealt[2 * i + 1])
            for i in range(3)
        ]
        feed_out = kernel_call(
            sum_feed_kernel,
            [((2 * rows, units), BF16)] * cols,
            *down_terms,
            *gate_terms,
            room=16,
        )
    else:
        cot_all = jnp.concatenate([cot_mine, cot_other], axis=0)
        sums = [
            scattered(
                jnp.moveaxis(grad.astype(BF16).reshape(cols, planes, rows, units), 1, 0)
            )
            for grad in (
                matmul_tn(cot_all, hidden),
                matmul_tn(normed_two, gate_grad),
                matmul_tn(normed_two, up_grad),
            )
        ]
        feed_out = [jnp.concatenate([v[k] for v in sums[:2]], axis=0) for k in range(cols)]
    feed_in = exchange(feed_out)
    down_share, gate_share = kernel_call(
        unpack_feed_kernel,
        [((rows, cols * units), F32)] * 2,
        *feed_in,
        scalars=where,
        room=12,
    )

    result_mine, result_other = kernel_call(
        result_kernel, [((half, width), BF16)] * 2, hidden, *down_parts, room=12)
    result_came = flip(result_other, "row", 1)
    result_pieces = kernel_call(
        pack_features_kernel, [((half, part), BF16)] * cols, result_mine, result_came
    )
    result_in = exchange(result_pieces)
    result_mine = (first_block + total(result_in)).astype(BF16)
    block_output = natural(both_rows(result_mine))

    mixed_size = 3 * q_size
    if planes == 4:
        mixed_outs = [((2, cols, rows + 8, mixed_size), BF16)] * 2
    else:
        mixed_outs = [((cols, part, mixed_size), BF16), ((cols, 8, mixed_size), BF16)]
    one_mine, one_other, inner_part, mixed_first, mixed_second = kernel_call(
        attend_back_kernel,
        [((half, width), BF16), ((half, width), BF16), ((8, tokens), F32)] + mixed_outs,
        *common,
        qkv,
        turned,
        context,
        logs,
        first_half,
        first_other,
        second_in,
        feedforward_part,
        scalars=where,
        scratch=[((part, mixed_size), BF16)], room=34)
    one_came = flip(one_other, "row", 1)
    inner_came = flip(inner_part[:, half:], "row", 1)
    one_pieces = kernel_call(
        pack_last_kernel,
        [((half + 16, part), BF16)] * cols,
        one_mine,
        one_came,
        inner_part,
        inner_came, room=10)
    one_in = exchange(one_pieces)
    one_grad = total([v[:half] for v in one_in])
    inner_one = jnp.sum(total([v[half:] for v in one_in])[:3], axis=0)[:, None]
    weighted_one = one_grad * gain_one[:part]
    own_input = input_mine.astype(F32)
    root_one = lax.rsqrt(jnp.mean(own_input * own_input, axis=1, keepdims=True) + EPSILON)
    normal_one = own_input[:, :part] * root_one
    input_mine_grad = first_half[:, :part].astype(F32) + root_one * (
        weighted_one - normal_one * inner_one
    )
    input_grad = natural(both_rows(input_mine_grad))

    if planes == 4:
        mixed_terms = shifted(mixed_first, mixed_second)
        last_out = kernel_call(
            sum_last_kernel,
            [((2 * rows + 8, units), BF16)] * cols,
            *up_terms,
            *mixed_terms,
            room=16,
        )
    else:
        lines = jnp.broadcast_to(mixed_second[:, None], (cols, planes, 8, mixed_size))
        blocks = mixed_first.reshape(cols, planes, rows, mixed_size)
        mixed_sum = scattered(jnp.moveaxis(jnp.concatenate([blocks, lines], axis=2), 1, 0))
        mixed_sum = jnp.pad(mixed_sum, ((0, 0), (0, 0), (0, units - mixed_size)))
        last_out = [jnp.concatenate([sums[2][k], mixed_sum[k]], axis=0) for k in range(cols)]
    last_in = exchange(last_out)
    up_share, query_share, key_share, value_share, output_share, gain_sums = kernel_call(
        unpack_last_kernel,
        [
            ((rows, cols * units), F32),
            ((rows, cols * q_size), F32),
            ((rows, cols * head), F32),
            ((rows, cols * head), F32),
            ((rows, cols * q_size), F32),
            ((8, mixed_size), F32),
        ],
        *last_in,
        scalars=where,
        room=12,
    )
    gain_sums = gain_sums + flip(gain_sums, "row", 1)
    attention_share = lax.dynamic_slice_in_dim(gain_sums[0], plane * rows, rows, 0)
    feedforward_share = lax.dynamic_slice_in_dim(gain_sums[1], plane * rows, rows, 0)
    query_gain_grad = gain_sums[0, 2 * q_size : 2 * q_size + head]
    key_gain_grad = gain_sums[0, 2 * q_size + head :]
    return (
        block_output,
        input_grad,
        attention_share,
        query_share,
        key_share,
        value_share,
        query_gain_grad,
        key_gain_grad,
        output_share.T,
        feedforward_share,
        gate_share,
        up_share,
        down_share.T,
    )


def solution(mesh):
    placed = (
        P("dp", "col"),
        P("dp"),
        P("dp"),
        P("col"),
        P("col", "row"),
        P("col", "row"),
        P("col", "row"),
        P(),
        P(),
        P("row", "col"),
        P("col"),
        P("col", "row"),
        P("col", "row"),
        P("row", "col"),
        P("dp", "col"),
    )


    return jax.shard_map(
        body,
        mesh=mesh,
        in_specs=placed,
        out_specs=(
            P("dp", "col"),
            P("dp", "col"),
            P(("col", "dp")),
            P(("col", "dp"), "row"),
            P(("col", "dp"), "row"),
            P(("col", "dp"), "row"),
            P(),
            P(),
            P("row", ("col", "dp")),
            P(("col", "dp")),
            P(("col", "dp"), "row"),
            P(("col", "dp"), "row"),
            P("row", ("col", "dp")),
        ),
        check_vma=False,
    )
```

```python
import jax
import jax.numpy as jnp
from jax import lax
from jax.experimental import pallas as pl
from jax.experimental.pallas import tpu as pltpu
from jax.sharding import PartitionSpec as P


EPSILON = 1e-05
THETA = 1000000.0
NEGATIVE = -1e30


F32 = jnp.float32
BF16 = jnp.bfloat16


def matmul(left, right):
    return jnp.dot(left, right, preferred_element_type=F32)


def matmul_nt(left, right):
    return lax.dot_general(left, right, (((1,), (1,)), ((), ())), preferred_element_type=F32)


def matmul_tn(left, right):
    return lax.dot_general(left, right, (((0,), (0,)), ((), ())), preferred_element_type=F32)


def flip(values, axis, distance):
    size = lax.axis_size(axis)
    return lax.ppermute(values, axis, [(i, i ^ distance) for i in range(size)])


def spread(values):
    return [values] + [flip(values, "col", k) for k in range(1, lax.axis_size("col"))]


def exchange(pieces):
    return [pieces[0]] + [flip(pieces[k], "col", k) for k in range(1, len(pieces))]


def total(parts):
    result = parts[0].astype(F32)
    for part in parts[1:]:
        result = result + part.astype(F32)
    return result


def kernel_call(kernel, outs, *args, scalars=None, scratch=(), fetch=0, room=8):
    specs = [pl.BlockSpec(memory_space=pltpu.HBM)] * fetch
    specs = specs + [pl.BlockSpec(memory_space=pltpu.VMEM)] * (len(args) - fetch)
    scratch_shapes = [pltpu.VMEM(shape, dtype) for shape, dtype in scratch]
    if fetch:
        scratch_shapes = [pltpu.VMEM(v.shape, v.dtype) for v in args[:fetch]] + scratch_shapes
        scratch_shapes.append(pltpu.SemaphoreType.DMA((fetch,)))
    if scalars is not None:
        args = (scalars,) + args
        specs = [pl.BlockSpec(memory_space=pltpu.SMEM)] + specs
    return pl.pallas_call(
        kernel,
        out_shape=[jax.ShapeDtypeStruct(shape, dtype) for shape, dtype in outs],
        in_specs=specs,
        out_specs=[pl.BlockSpec(memory_space=pltpu.VMEM)] * len(outs),
        scratch_shapes=scratch_shapes,
        compiler_params=pltpu.CompilerParams(vmem_limit_bytes=room * 1024 * 1024),
    )(*args)


def fetched(sources, targets, semaphores):
    copies = [
        pltpu.make_async_copy(source, target, semaphores.at[i])
        for i, (source, target) in enumerate(zip(sources, targets))
    ]
    for copy in copies:
        copy.start()
    for copy in copies:
        copy.wait()


def pack_one_kernel(
    where, x_in, query_in, key_in, value_in, gain_first, gain_second,
    out0, out1, out2, out3, x, query, key, value, semaphores,
):
    fetched((x_in, query_in, key_in, value_in), (x, query, key, value), semaphores)
    outs = (out0, out1, out2, out3)
    row, col = where[0], where[1]
    half = x.shape[0] // 2
    cols = len(outs)
    q_size, kv_size = query.shape[1] // cols, key.shape[1] // cols
    line = lax.broadcasted_iota(jnp.int32, (16, x.shape[1]), 0)
    rows = jnp.zeros((16, x.shape[1]), F32)
    for g, gain in enumerate((gain_first, gain_second)):
        rest = gain[...]
        for p in range(3):
            part = rest.astype(BF16).astype(F32)
            rows = jnp.where(line == 3 * g + p, part, rows)
            rest = rest - part
    mine = x[pl.ds(pl.multiple_of(row * half, half), half), :]
    for k, out in enumerate(outs):
        block = col ^ k
        out[:half, :] = mine
        out[half : half + 16, :] = rows.astype(BF16)
        out[half + 16 :, :q_size] = query[:, pl.ds(pl.multiple_of(block * q_size, q_size), q_size)]
        pair = pl.multiple_of((block >> 1) * (2 * kv_size), 2 * kv_size)
        odd = (block & 1) == 1
        both = []
        for weight in (key, value):
            two = weight[:, pl.ds(pair, 2 * kv_size)]
            both.append(jnp.where(odd, two[:, kv_size:], two[:, :kv_size]))
        out[half + 16 :, q_size:] = jnp.concatenate(both, axis=1)


def pack_two_kernel(
    where, weight_in, cot_in, out0, out1, out2, out3, weight, cot, semaphores
):
    fetched((weight_in, cot_in), (weight, cot), semaphores)
    outs = (out0, out1, out2, out3)
    size, half = weight.shape[0] // len(outs), cot.shape[0] // 2
    for k, out in enumerate(outs):
        out[:half, :] = cot[pl.ds(pl.multiple_of(where[0] * half, half), half), :]
        for j in range(len(outs)):
            source = pl.multiple_of((where[1] ^ (k ^ j)) * size, size)
            out[half + j * size : half + (j + 1) * size, :] = weight[pl.ds(source, size), :]


def pack_three_kernel(where, down_in, out0, out1, out2, out3, down, semaphores):
    fetched((down_in,), (down,), semaphores)
    outs = (out0, out1, out2, out3)
    size = down.shape[0] // len(outs)
    for k, out in enumerate(outs):
        out[...] = down[pl.ds(pl.multiple_of((where[1] ^ k) * size, size), size), :]


def pack_gate_kernel(
    where, gate_in, up_in, out0, out1, out2, out3, out4, gate, up, semaphores
):
    fetched((gate_in, up_in), (gate, up), semaphores)
    outs = (out0, out1, out2, out3, out4)
    col, odd_plane = where[1], (where[2] & 1) == 1
    cols = len(outs) - 1
    size = gate.shape[1] // cols

    def piece(weight, block):
        two = weight[:, pl.ds(pl.multiple_of((block >> 1) * (2 * size), 2 * size), 2 * size)]
        return jnp.where((block & 1) == 1, two[:, size:], two[:, :size])

    @pl.when(jnp.logical_not(odd_plane))
    def _():
        for k in range(cols):
            outs[k][...] = piece(gate, col ^ k)
        outs[cols][...] = piece(up, col)

    @pl.when(odd_plane)
    def _():
        for k in range(cols):
            outs[k][...] = piece(up, col ^ k)
        outs[cols][...] = piece(gate, col)


def join_kernel(first0, first1, first2, first3, out):
    part, size = first0.shape[1], out.shape[0]
    for k, piece in enumerate((first0, first1, first2, first3)):
        out[:, k * part : (k + 1) * part] = piece[piece.shape[0] - size :, :]


def project_kernel(
    where, mine, other, context_near, context_far, joined, joined_far,
    first0, first1, first2, first3, normed_out, own_out, share_out, sum_scratch,
):
    buffers = (first0, first1, first2, first3)
    half, part = mine.shape[0], first0.shape[1]
    share = share_out.shape[0]
    top = mine[...].astype(F32) + matmul(context_near[:half, :], joined[...])
    top = top + matmul(context_far[half:, :], joined_far[...])
    low = other[...].astype(F32) + matmul(context_near[half:, :], joined[...])
    low = low + matmul(context_far[:half, :], joined_far[...])
    sum_scratch[...] = top
    own_out[...] = top[:, :part]
    share_out[...] = sum_scratch[pl.ds(pl.multiple_of(where[1] * share, share), share), :]
    gain = jnp.concatenate([gain_row(buffers, half + 3, k) for k in range(len(buffers))], axis=1)
    for i, rows in enumerate((top, low)):
        root = lax.rsqrt(jnp.mean(rows * rows, axis=1, keepdims=True) + EPSILON)
        normed_out[i * half : (i + 1) * half, :] = (rows * root * gain).astype(BF16)


def hidden_kernel(
    where, normed, near0, near1, near2, near3, far0, far1, far2, far3,
    gate_out, up_out, hidden_out,
):
    part = near0.shape[0]
    first_pre = second_pre = None
    for k, (near, far) in enumerate(
        ((near0, far0), (near1, far1), (near2, far2), (near3, far3))
    ):
        block = normed[:, k * part : (k + 1) * part]
        one, two = matmul(block, near[...]), matmul(block, far[...])
        first_pre = one if k == 0 else first_pre + one
        second_pre = two if k == 0 else second_pre + two
    even = (where[2] & 1) == 0
    gate_pre = jnp.where(even, first_pre, second_pre)
    up_pre = jnp.where(even, second_pre, first_pre)
    gate_out[...] = gate_pre
    up_out[...] = up_pre
    hidden_out[...] = (gate_pre * (1.0 / (1.0 + jnp.exp(-gate_pre))) * up_pre).astype(BF16)


def backward_kernel(
    where, cot_mine, cot_other, gate_in, up_in, down0, down1, down2, down3,
    near0, near1, near2, near3, far0, far1, far2, far3,
    gate_grad_out, up_grad_out, mine_out, other_out,
):
    half, part = mine_out.shape[0], near0.shape[0]
    size = gate_in.shape[1]
    parts = []
    for rows in (cot_mine, cot_other):
        grad = None
        for k, down in enumerate((down0, down1, down2, down3)):
            term = matmul_nt(rows[:, k * part : (k + 1) * part], down[:size, :])
            grad = term if k == 0 else grad + term
        parts.append(grad)
    hidden_grad = jnp.concatenate(parts, axis=0)
    gate_pre, up_pre = gate_in[...], up_in[...]
    sigmoid_gate = 1.0 / (1.0 + jnp.exp(-gate_pre))
    gate_grad = (
        hidden_grad * up_pre * sigmoid_gate * (1.0 + gate_pre * (1.0 - sigmoid_gate))
    ).astype(BF16)
    up_grad = (hidden_grad * (gate_pre * sigmoid_gate)).astype(BF16)
    gate_grad_out[...] = gate_grad
    up_grad_out[...] = up_grad
    even = (where[2] & 1) == 0
    near_grad = jnp.where(even, gate_grad, up_grad)
    far_grad = jnp.where(even, up_grad, gate_grad)
    for k, (near, far) in enumerate(
        ((near0, far0), (near1, far1), (near2, far2), (near3, far3))
    ):
        block = matmul_nt(near_grad, near[...]) + matmul_nt(far_grad, far[...])
        mine_out[:, k * part : (k + 1) * part] = block[:half].astype(BF16)
        other_out[:, k * part : (k + 1) * part] = block[half:].astype(BF16)


def result_kernel(hidden, down0, down1, down2, down3, mine_out, other_out):
    half, part = mine_out.shape[0], down0.shape[1]
    for k, down in enumerate((down0, down1, down2, down3)):
        block = matmul(hidden[...], down[: hidden.shape[1], :])
        mine_out[:, k * part : (k + 1) * part] = block[:half].astype(BF16)
        other_out[:, k * part : (k + 1) * part] = block[half:].astype(BF16)


def deal(where, scratch, k, send, keep, rows):
    for j in range(2):
        for out, m in ((send, 1 + 2 * j), (keep, 2 * j)):
            start = pl.multiple_of((where[2] ^ m) * rows, rows)
            out[j, k, :rows, :] = scratch[pl.ds(start, rows), :]


def down_grad_kernel(where, cot_mine, cot_other, hidden, send, keep, scratch):
    half = hidden.shape[0] // 2
    cols, rows = send.shape[1], send.shape[2]
    part = cot_mine.shape[1] // cols
    for k in range(cols):
        span = slice(k * part, (k + 1) * part)
        grad = matmul_tn(cot_mine[:, span], hidden[:half, :])
        grad = grad + matmul_tn(cot_other[:, span], hidden[half:, :])
        scratch[...] = grad.astype(BF16)
        deal(where, scratch, k, send, keep, rows)


def weight_grad_kernel(
    where, normed, gate_grad, up_grad, gate_send, gate_keep, up_send, up_keep, scratch
):
    cols, rows = gate_send.shape[1], gate_send.shape[2]
    part = normed.shape[1] // cols
    for upstream, send, keep in ((gate_grad, gate_send, gate_keep), (up_grad, up_send, up_keep)):
        for k in range(cols):
            span = slice(k * part, (k + 1) * part)
            scratch[...] = matmul_tn(normed[:, span], upstream[...]).astype(BF16)
            deal(where, scratch, k, send, keep, rows)


def pack_tokens_kernel(where, ours, came, out0, out1, out2, out3, scratch):
    outs = (out0, out1, out2, out3)
    share, part = out0.shape[0], out0.shape[1] // len(outs)
    scratch[...] = (ours[...].astype(F32) + came[...].astype(F32)).astype(BF16)
    for k, out in enumerate(outs):
        rows = pl.ds(pl.multiple_of((where[1] ^ k) * share, share), share)
        for j in range(len(outs)):
            source = k ^ j
            out[:, j * part : (j + 1) * part] = scratch[rows, source * part : (source + 1) * part]


def second_norm_kernel(
    where, came0, came1, came2, came3, sums, cot_mine, first0, first1, first2, first3,
    out0, out1, out2, out3, gain_out,
):
    buffers = (first0, first1, first2, first3)
    outs = (out0, out1, out2, out3)
    share, part = out0.shape[0], out0.shape[1] // len(outs)
    half = share * len(outs)
    grad = came0[...].astype(F32) + came1[...].astype(F32)
    grad = grad + came2[...].astype(F32) + came3[...].astype(F32)
    gain = jnp.concatenate([gain_row(buffers, half + 3, k) for k in range(len(buffers))], axis=1)
    rows = sums[...]
    root = lax.rsqrt(jnp.mean(rows * rows, axis=1, keepdims=True) + EPSILON)
    normal = rows * root
    weighted = grad * gain
    gain_out[...] = jnp.sum(grad * normal, axis=0, keepdims=True)
    inner = jnp.mean(weighted * normal, axis=1, keepdims=True)
    cot = cot_mine[pl.ds(pl.multiple_of(where[1] * share, share), share), :].astype(F32)
    first = (cot + root * (weighted - normal * inner)).astype(BF16)
    for k, out in enumerate(outs):
        for j in range(len(outs)):
            source = k ^ j
            out[:, j * part : (j + 1) * part] = first[:, source * part : (source + 1) * part]


def join_tokens_kernel(where, came0, came1, came2, came3, out):
    share = came0.shape[0]
    for k, came in enumerate((came0, came1, came2, came3)):
        out[pl.ds(pl.multiple_of((where[1] ^ k) * share, share), share), :] = came[...]


def pack_features_kernel(ours, came, out0, out1, out2, out3):
    part = out0.shape[1]
    for k, out in enumerate((out0, out1, out2, out3)):
        span = slice(k * part, (k + 1) * part)
        out[...] = (ours[:, span].astype(F32) + came[:, span].astype(F32)).astype(BF16)


def pack_last_kernel(ours, came, inner, inner_came, out0, out1, out2, out3):
    half, part = ours.shape[0], out0.shape[1]
    line = lax.broadcasted_iota(jnp.int32, (16, part), 0)
    rows = jnp.zeros((16, part), F32)
    rest = inner[0:1, :half] + inner_came[0:1, :]
    for p in range(3):
        piece = rest.astype(BF16).astype(F32)
        rows = jnp.where(line == p, piece, rows)
        rest = rest - piece
    for k, out in enumerate((out0, out1, out2, out3)):
        span = slice(k * part, (k + 1) * part)
        out[:half, :] = (ours[:, span].astype(F32) + came[:, span].astype(F32)).astype(BF16)
        out[half:, :] = rows.astype(BF16)


def join_first_kernel(first0, first1, first2, first3, out):
    part, size = first0.shape[1], out.shape[0]
    for k, piece in enumerate((first0, first1, first2, first3)):
        out[:, k * part : (k + 1) * part] = piece[:size, :]


def in_chip_order(where, pieces):
    odd, high = (where[1] & 1) == 1, (where[1] & 2) == 2
    ordered = []
    for s in range(4):
        low_pair = jnp.where(odd, pieces[s ^ 1], pieces[s])
        high_pair = jnp.where(odd, pieces[s ^ 3], pieces[s ^ 2])
        ordered.append(jnp.where(high, high_pair, low_pair))
    return ordered


def plane_sum(keep, came, far, k):
    return keep[0, k].astype(F32) + came[0, k].astype(F32) + far[k].astype(F32)


def sum_feed_kernel(
    keep0, came0, far0, keep1, came1, far1, out0, out1, out2, out3
):
    rows = keep0.shape[2]
    for k, out in enumerate((out0, out1, out2, out3)):
        out[:rows, :] = plane_sum(keep0, came0, far0, k).astype(BF16)
        out[rows:, :] = plane_sum(keep1, came1, far1, k).astype(BF16)


def sum_last_kernel(
    keep0, came0, far0, keep1, came1, far1, out0, out1, out2, out3
):
    rows, size = keep0.shape[2], keep1.shape[3]
    for k, out in enumerate((out0, out1, out2, out3)):
        out[:rows, :] = plane_sum(keep0, came0, far0, k).astype(BF16)
        out[rows:, :size] = plane_sum(keep1, came1, far1, k).astype(BF16)
        rest = out.shape[1] - size
        out[rows:, size:] = jnp.zeros((out.shape[0] - rows, rest), BF16)


def unpack_feed_kernel(where, came0, came1, came2, came3, down_out, gate_out):
    rows = gate_out.shape[0]
    pieces = in_chip_order(where, [v[...] for v in (came0, came1, came2, came3)])
    for i, out in enumerate((down_out, gate_out)):
        span = slice(i * rows, (i + 1) * rows)
        out[...] = jnp.concatenate([v[span].astype(F32) for v in pieces], axis=1)


def unpack_last_kernel(
    where, came0, came1, came2, came3,
    up_out, query_out, key_out, value_out, output_out, gain_out,
):
    rows = query_out.shape[0]
    pieces = in_chip_order(where, [v[...] for v in (came0, came1, came2, came3)])
    two = query_out.shape[1] // len(pieces)
    size = two // 2
    pieces = [v.astype(F32) for v in pieces]
    up_out[...] = jnp.concatenate([v[:rows] for v in pieces], axis=1)
    for out, start, wide in (
        (query_out, 0, two), (key_out, two, size), (value_out, two + size, size),
        (output_out, 2 * two, two),
    ):
        blocks = [v[rows : 2 * rows, start : start + wide] for v in pieces]
        out[...] = jnp.concatenate(blocks, axis=1)
    gains = [v[2 * rows :, : 3 * two] for v in pieces]
    gain_out[...] = gains[0] + gains[1] + gains[2] + gains[3]


def gain_kernel(where, ours, came, attention_out, feed_out, query_out, key_out):
    lines = ours[...] + came[...]
    rows, head = attention_out.shape[1], query_out.shape[1]
    odd, high = (where[2] & 1) == 1, (where[2] & 2) == 2
    for out, i in ((attention_out, 0), (feed_out, 1)):
        parts = [lines[i : i + 1, p * rows : (p + 1) * rows] for p in range(4)]
        low = jnp.where(odd, parts[1], parts[0])
        out[...] = jnp.where(high, jnp.where(odd, parts[3], parts[2]), low)
    query_out[...] = lines[0:1, 4 * rows : 4 * rows + head]
    key_out[...] = lines[0:1, 4 * rows + head :]


def lane_is_first(size):
    return lax.broadcasted_iota(jnp.int32, (1, 2 * size), 1) < size


def head_scale(values, first):
    size = values.shape[1] // 2
    squares = values * values
    left = jnp.sum(jnp.where(first, squares, 0.0), axis=1, keepdims=True)
    right = jnp.sum(jnp.where(first, 0.0, squares), axis=1, keepdims=True)
    return lax.rsqrt(jnp.where(first, left, right) / size + EPSILON)


def turn(values, cosine, sine):
    width = values.shape[1]
    quarter = width // 4
    lane = lax.broadcasted_iota(jnp.int32, (1, width), 1)
    low = (lane & quarter) == 0
    other = jnp.where(
        low, pltpu.roll(values, width - quarter, 1), pltpu.roll(values, quarter, 1)
    )
    return values * cosine + other * sine


def root_and_input(mine, other):
    rows = jnp.concatenate([mine[...], other[...]], axis=0).astype(F32)
    mean = jnp.mean(rows * rows, axis=1, keepdims=True)
    return rows, lax.rsqrt(mean + EPSILON)


def gain_row(buffers, start, k):
    rows = buffers[k][start : start + 16, :].astype(F32)
    return rows[0:1] + rows[1:2] + rows[2:3]


def allowed_of(down, across):
    return (across[0:1, :] <= down[:, 0:1]) & (across[1:2, :] == down[:, 1:2])


def attend_kernel(
    mine, other, first0, first1, first2, first3, cosine, sine, gains, down, across,
    qkv_out, turned_out, context_out, log_out,
):
    buffers = (first0, first1, first2, first3)
    half, part = mine.shape[0], first0.shape[1]
    rows, root = root_and_input(mine, other)
    start = half + 16
    qkv = None
    for k, buffer in enumerate(buffers):
        block = rows[:, k * part : (k + 1) * part] * root * gain_row(buffers, half, k)
        term = matmul(block.astype(BF16), buffer[start:, :])
        qkv = term if qkv is None else qkv + term
    qkv_out[...] = qkv
    two = qkv.shape[1] // 2
    size = two // 2
    first = lane_is_first(size)
    query, pair = qkv[:, :two], qkv[:, two:]
    query_turned = turn(
        query * head_scale(query, first) * gains[0:1, :], cosine[...], sine[...]
    ).astype(BF16)
    key_turned = turn(pair * head_scale(pair, first) * gains[1:2, :], cosine[...], sine[...])
    pair_rounded = jnp.where(first, key_turned, pair).astype(BF16)
    turned_out[:, :two] = query_turned
    turned_out[:, two:] = pair_rounded
    key, value = pair_rounded[:, :size], pair_rounded[:, size:]
    allowed = allowed_of(down, across)
    contexts, logs = [], []
    for h in range(2):
        raw = matmul_nt(query_turned[:, h * size : (h + 1) * size], key)
        scores = jnp.where(allowed, raw * size ** (-0.5), NEGATIVE)
        top = jnp.max(scores, axis=1, keepdims=True)
        powers = jnp.exp(scores - top)
        sums = jnp.sum(powers, axis=1, keepdims=True)
        prob = (powers * (1.0 / sums)).astype(BF16)
        contexts.append(matmul(prob, value))
        logs.append(top + jnp.log(sums))
    context_out[...] = jnp.concatenate(contexts, axis=1).astype(BF16)
    log_out[...] = jnp.where(first, logs[0], logs[1])


def attend_back_kernel(
    where, mine, other, first0, first1, first2, first3, cosine, sine, gains, down, across,
    qkv_in, turned, context_in, logs, grad_mine, grad_other, out_weight,
    gain_in, one_mine, one_other, inner_out, mixed_send, mixed_keep, mixed,
):
    buffers = (first0, first1, first2, first3)
    half, part = mine.shape[0], first0.shape[1]
    two = context_in.shape[1]
    size = two // 2
    first = lane_is_first(size)
    upstream = jnp.concatenate([grad_mine[...], grad_other[...]], axis=0)
    context = context_in[...]
    context_grad = matmul_nt(upstream, out_weight[:two, :]).astype(BF16)
    key, value = turned[:, two : two + size], turned[:, two + size :]
    allowed = allowed_of(down, across)
    products = context_grad.astype(F32) * context.astype(F32)
    query_grads = []
    key_grad = value_grad = None
    for h in range(2):
        query = turned[:, h * size : (h + 1) * size]
        grad = context_grad[:, h * size : (h + 1) * size]
        raw = matmul_nt(query, key)
        scores = jnp.where(allowed, raw * size ** (-0.5), NEGATIVE)
        prob = jnp.exp(scores - logs[:, h * size : h * size + 1])
        delta = jnp.sum(
            jnp.where(first if h == 0 else jnp.logical_not(first), products, 0.0),
            axis=1,
            keepdims=True,
        )
        value_term = matmul_tn(prob.astype(BF16), grad)
        score_grad = (prob * (matmul_nt(grad, value) - delta) * size ** (-0.5)).astype(BF16)
        query_grads.append(matmul(score_grad, key))
        key_term = matmul_tn(score_grad, query)
        key_grad = key_term if h == 0 else key_grad + key_term
        value_grad = value_term if h == 0 else value_grad + value_term
    pieces, head_parts = [], []
    for i, grad in enumerate(
        (jnp.concatenate(query_grads, axis=1), jnp.concatenate([key_grad, value_grad], axis=1))
    ):
        normed = turn(grad, cosine[...], -sine[...])
        proj = qkv_in[:, i * two : (i + 1) * two]
        scale = head_scale(proj, first)
        hat = proj * scale
        weighted = normed * gains[i : i + 1, :]
        product = weighted * hat
        left = jnp.sum(jnp.where(first, product, 0.0), axis=1, keepdims=True)
        right = jnp.sum(jnp.where(first, 0.0, product), axis=1, keepdims=True)
        inner = jnp.where(first, left, right) / size
        result = scale * (weighted - hat * inner)
        pieces.append(result if i == 0 else jnp.where(first, result, grad))
        head_parts.append(jnp.sum(normed * hat, axis=0, keepdims=True))
    head_line = head_parts[0] + pltpu.roll(head_parts[0], size, 1)
    head_line = jnp.where(first, head_line, pltpu.roll(head_parts[1], size, 1))
    rows_here = mixed_send.shape[2] - 8
    line = lax.broadcasted_iota(jnp.int32, (8, part), 0)
    qkv_grad = jnp.concatenate(pieces, axis=1).astype(BF16)
    rows, root = root_and_input(mine, other)
    inner_sum = jnp.zeros((2 * half, 1), F32)
    for k, buffer in enumerate(buffers):
        span = slice(k * part, (k + 1) * part)
        gain = gain_row(buffers, half, k)
        hat = rows[:, span] * root
        grad = matmul_nt(qkv_grad, buffer[half + 16 :, :])
        product = grad * hat
        lines = jnp.where(line == 0, jnp.sum(product, axis=0, keepdims=True), 0.0)
        lines = jnp.where(line == 1, gain_in[:, span], lines).astype(BF16)
        inner_sum = inner_sum + jnp.sum(product * gain, axis=1, keepdims=True)
        one_mine[:, span] = grad[:half].astype(BF16)
        one_other[:, span] = grad[half:].astype(BF16)
        mixed[:, : 2 * two] = matmul_tn((hat * gain).astype(BF16), qkv_grad).astype(BF16)
        mixed[:, 2 * two :] = matmul_tn(upstream[:, span], context).astype(BF16)
        heads = jnp.broadcast_to(head_line, (8, two)).astype(BF16)
        if mixed_send.shape[0] == 2:
            deal(where, mixed, k, mixed_send, mixed_keep, rows_here)
            for out in (mixed_send, mixed_keep):
                for j in range(2):
                    out[j, k, rows_here:, : 2 * two] = lines
                    out[j, k, rows_here:, 2 * two :] = heads
        else:
            mixed_send[k, ...] = mixed[...]
            mixed_keep[k, :, : 2 * two] = lines
            mixed_keep[k, :, 2 * two :] = heads
    wide = jnp.broadcast_to(inner_sum / (part * len(buffers)), (2 * half, 128))
    inner_out[...] = jnp.transpose(wide)[:8, :]


def rope_tables(places, head_size):
    half_size = head_size // 2
    frequency = THETA ** (-(jnp.arange(half_size).astype(F32) * 2.0 / head_size))
    angles = places.astype(F32)[:, None] * frequency[None, :]
    return (jnp.cos(angles), jnp.sin(angles))


def body(
    block_input,
    segments,
    positions,
    attention_gain,
    query_weight,
    key_weight,
    value_weight,
    query_gain,
    key_gain,
    output_weight,
    feedforward_gain,
    gate_weight,
    up_weight,
    down_weight,
    cotangent,
):
    tokens = block_input.shape[0]
    part = block_input.shape[1]
    head = query_gain.shape[0]
    cols = lax.axis_size("col")
    planes = lax.axis_size("dp")
    width = part * cols
    half = tokens // 2
    row = lax.axis_index("row")
    col = lax.axis_index("col")
    plane = lax.axis_index("dp")

    def mine_first(values):
        return jnp.where(row == 0, values, jnp.roll(values, half, axis=0))

    def natural(values):
        return jnp.where(row == 0, values, jnp.roll(values, half, axis=0))

    q_size = query_weight.shape[1] // cols
    units = gate_weight.shape[1] // cols
    where = jnp.stack([row, col, plane]).astype(jnp.int32)
    shapes = [((half + 16 + part, part), BF16)] * cols
    first_in = exchange(
        kernel_call(
            pack_one_kernel,
            shapes,
            block_input,
            query_weight,
            key_weight,
            value_weight,
            attention_gain.reshape(1, part),
            feedforward_gain.reshape(1, part),
            scalars=where,
            fetch=4, room=60),
    )
    (input_mine,) = kernel_call(join_first_kernel, [((half, width), BF16)], *first_in, room=10)
    gain_parts = jnp.concatenate([v[half : half + 16] for v in first_in], axis=1).astype(F32)
    gain_one = gain_parts[0] + gain_parts[1] + gain_parts[2]
    input_other = flip(input_mine, "row", 1)
    gate_in = kernel_call(
        pack_gate_kernel,
        [((part, units), BF16)] * (cols + 1),
        gate_weight,
        up_weight,
        scalars=where,
        fetch=2, room=12)
    near_parts = exchange(gate_in[:cols])
    far_parts = [gate_in[cols]] + [flip(v, "dp", 1) for v in near_parts[1:]]
    inner_size = output_weight.shape[0]
    two_out = kernel_call(
        pack_two_kernel,
        [((half + inner_size, part), BF16)] * cols,
        output_weight,
        cotangent,
        scalars=where,
        fetch=2,
    )
    second_parts = exchange(two_out)
    three_out = kernel_call(
        pack_three_kernel,
        [((units, part), BF16)] * cols,
        down_weight,
        scalars=where,
        fetch=1,
    )
    down_parts = exchange(three_out)

    group = q_size // head
    segment_ids = mine_first(segments)
    places = mine_first(positions)
    index = mine_first(jnp.arange(tokens))

    cosine, sine_part = rope_tables(places, head)
    cos_lanes = jnp.concatenate([cosine] * (2 * group), axis=1)
    sin_lanes = jnp.concatenate([-sine_part, sine_part] * group, axis=1)
    head_gains = jnp.stack([jnp.tile(query_gain, group), jnp.tile(key_gain, group)])
    down = jnp.stack([index, segment_ids], axis=1)
    across = jnp.stack([index, segment_ids])
    common = (
        input_mine,
        input_other,
        *first_in,
        cos_lanes,
        sin_lanes,
        head_gains,
        down,
        across,
    )
    qkv, turned, context, logs = kernel_call(
        attend_kernel,
        [
            ((tokens, 2 * q_size), F32),
            ((tokens, 2 * q_size), BF16),
            ((tokens, q_size), BF16),
            ((tokens, q_size), F32),
        ],
        *common, room=26)

    context_parts = spread(context)
    (context_near,) = kernel_call(join_kernel, [((tokens, inner_size), BF16)], *context_parts, room=10)
    context_far = flip(context_near, "row", 1)
    (second_in,) = kernel_call(join_kernel, [((inner_size, width), BF16)], *second_parts, room=10)
    second_far = flip(second_in, "row", 1)
    (cot_mine,) = kernel_call(join_first_kernel, [((half, width), BF16)], *second_parts, room=10)
    cot_other = flip(cot_mine, "row", 1)

    share = half // cols
    normed_two, first_block, first_share = kernel_call(
        project_kernel,
        [((tokens, width), BF16), ((half, part), F32), ((share, width), F32)],
        input_mine,
        input_other,
        context_near,
        context_far,
        second_in,
        second_far,
        *first_in,
        scalars=where,
        scratch=[((half, width), F32)], room=24)
    gate_pre, up_pre, hidden = kernel_call(
        hidden_kernel,
        [((tokens, units), F32), ((tokens, units), F32), ((tokens, units), BF16)],
        normed_two,
        *near_parts,
        *far_parts,
        scalars=where, room=24)
    rows = part // planes
    if planes == 4:
        down_dealt = kernel_call(
            down_grad_kernel,
            [((2, cols, rows, units), BF16)] * 2,
            cot_mine,
            cot_other,
            hidden,
            scalars=where,
            scratch=[((part, units), BF16)], room=14)
    gate_grad, up_grad, two_mine, two_other = kernel_call(
        backward_kernel,
        [((tokens, units), BF16)] * 2 + [((half, width), BF16)] * 2,
        cot_mine,
        cot_other,
        gate_pre,
        up_pre,
        *down_parts,
        *near_parts,
        *far_parts,
        scalars=where, room=30)

    two_came = flip(two_other, "row", 1)
    two_pieces = kernel_call(
        pack_tokens_kernel,
        [((share, width), BF16)] * cols,
        two_mine,
        two_came,
        scalars=where,
        scratch=[((half, width), BF16)],
    )
    two_in = exchange(two_pieces)
    *first_pieces, feedforward_part = kernel_call(
        second_norm_kernel,
        [((share, width), BF16)] * cols + [((1, width), F32)],
        *two_in,
        first_share,
        cot_mine,
        *first_in,
        scalars=where,
    )
    first_back = exchange(first_pieces)
    (first_half,) = kernel_call(
        join_tokens_kernel, [((half, width), BF16)], *first_back, scalars=where
    )
    first_other = flip(first_half, "row", 1)

    def shifted(send, keep):
        came = flip(send, "dp", 1)
        rest = (keep[1].astype(F32) + came[1].astype(F32)).astype(BF16)
        return keep, came, flip(rest, "dp", 2)

    def scattered(split):
        return lax.psum_scatter(split, "dp", scatter_dimension=0, tiled=True)[0]

    if planes == 4:
        dealt = kernel_call(
            weight_grad_kernel,
            [((2, cols, rows, units), BF16)] * 4,
            normed_two,
            gate_grad,
            up_grad,
            scalars=where,
            scratch=[((part, units), BF16)], room=20)
        dealt = list(down_dealt) + list(dealt)
        down_terms, gate_terms, up_terms = [
            shifted(dealt[2 * i], dealt[2 * i + 1])
            for i in range(3)
        ]
        feed_out = kernel_call(
            sum_feed_kernel,
            [((2 * rows, units), BF16)] * cols,
            *down_terms,
            *gate_terms,
            room=16,
        )
    else:
        cot_all = jnp.concatenate([cot_mine, cot_other], axis=0)
        sums = [
            scattered(
                jnp.moveaxis(grad.astype(BF16).reshape(cols, planes, rows, units), 1, 0)
            )
            for grad in (
                matmul_tn(cot_all, hidden),
                matmul_tn(normed_two, gate_grad),
                matmul_tn(normed_two, up_grad),
            )
        ]
        feed_out = [jnp.concatenate([v[k] for v in sums[:2]], axis=0) for k in range(cols)]
    feed_in = exchange(feed_out)
    down_share, gate_share = kernel_call(
        unpack_feed_kernel,
        [((rows, cols * units), F32)] * 2,
        *feed_in,
        scalars=where,
        room=12,
    )

    result_mine, result_other = kernel_call(
        result_kernel, [((half, width), BF16)] * 2, hidden, *down_parts, room=12)
    result_came = flip(result_other, "row", 1)
    result_pieces = kernel_call(
        pack_features_kernel, [((half, part), BF16)] * cols, result_mine, result_came
    )
    result_in = exchange(result_pieces)
    result_mine = (first_block + total(result_in)).astype(BF16)
    result_far = flip(result_mine, "row", 1)
    block_output = natural(jnp.concatenate([result_mine, result_far], axis=0))

    mixed_size = 3 * q_size
    if planes == 4:
        mixed_outs = [((2, cols, rows + 8, mixed_size), BF16)] * 2
    else:
        mixed_outs = [((cols, part, mixed_size), BF16), ((cols, 8, mixed_size), BF16)]
    one_mine, one_other, inner_part, mixed_first, mixed_second = kernel_call(
        attend_back_kernel,
        [((half, width), BF16), ((half, width), BF16), ((8, tokens), F32)] + mixed_outs,
        *common,
        qkv,
        turned,
        context,
        logs,
        first_half,
        first_other,
        second_in,
        feedforward_part,
        scalars=where,
        scratch=[((part, mixed_size), BF16)], room=34)
    one_came = flip(one_other, "row", 1)
    inner_came = flip(inner_part[:, half:], "row", 1)
    one_pieces = kernel_call(
        pack_last_kernel,
        [((half + 16, part), BF16)] * cols,
        one_mine,
        one_came,
        inner_part,
        inner_came, room=10)
    one_in = exchange(one_pieces)
    one_grad = total([v[:half] for v in one_in])
    inner_one = jnp.sum(total([v[half:] for v in one_in])[:3], axis=0)[:, None]
    weighted_one = one_grad * gain_one[:part]
    own_input = input_mine.astype(F32)
    root_one = lax.rsqrt(jnp.mean(own_input * own_input, axis=1, keepdims=True) + EPSILON)
    normal_one = own_input[:, :part] * root_one
    input_mine_grad = first_half[:, :part].astype(F32) + root_one * (
        weighted_one - normal_one * inner_one
    )
    input_far_grad = flip(input_mine_grad, "row", 1)
    input_grad = natural(jnp.concatenate([input_mine_grad, input_far_grad], axis=0))

    if planes == 4:
        mixed_terms = shifted(mixed_first, mixed_second)
        last_out = kernel_call(
            sum_last_kernel,
            [((2 * rows + 8, units), BF16)] * cols,
            *up_terms,
            *mixed_terms,
            room=16,
        )
    else:
        lines = jnp.broadcast_to(mixed_second[:, None], (cols, planes, 8, mixed_size))
        blocks = mixed_first.reshape(cols, planes, rows, mixed_size)
        mixed_sum = scattered(jnp.moveaxis(jnp.concatenate([blocks, lines], axis=2), 1, 0))
        mixed_sum = jnp.pad(mixed_sum, ((0, 0), (0, 0), (0, units - mixed_size)))
        last_out = [jnp.concatenate([sums[2][k], mixed_sum[k]], axis=0) for k in range(cols)]
    last_in = exchange(last_out)
    up_share, query_share, key_share, value_share, output_share, gain_sums = kernel_call(
        unpack_last_kernel,
        [
            ((rows, cols * units), F32),
            ((rows, cols * q_size), F32),
            ((rows, cols * head), F32),
            ((rows, cols * head), F32),
            ((rows, cols * q_size), F32),
            ((8, mixed_size), F32),
        ],
        *last_in,
        scalars=where,
        room=12,
    )
    gain_came = flip(gain_sums, "row", 1)
    if planes == 4:
        attention_share, feedforward_share, query_gain_grad, key_gain_grad = [
            v.reshape(-1)
            for v in kernel_call(
                gain_kernel,
                [((1, rows), F32), ((1, rows), F32), ((1, head), F32), ((1, head), F32)],
                gain_sums,
                gain_came,
                scalars=where,
            )
        ]
    else:
        gain_sums = gain_sums + gain_came
        attention_share = lax.dynamic_slice_in_dim(gain_sums[0], plane * rows, rows, 0)
        feedforward_share = lax.dynamic_slice_in_dim(gain_sums[1], plane * rows, rows, 0)
        query_gain_grad = gain_sums[0, 2 * q_size : 2 * q_size + head]
        key_gain_grad = gain_sums[0, 2 * q_size + head :]
    return (
        block_output,
        input_grad,
        attention_share,
        query_share,
        key_share,
        value_share,
        query_gain_grad,
        key_gain_grad,
        output_share.T,
        feedforward_share,
        gate_share,
        up_share,
        down_share.T,
    )


def solution(mesh):
    placed = (
        P("dp", "col"),
        P("dp"),
        P("dp"),
        P("col"),
        P("col", "row"),
        P("col", "row"),
        P("col", "row"),
        P(),
        P(),
        P("row", "col"),
        P("col"),
        P("col", "row"),
        P("col", "row"),
        P("row", "col"),
        P("dp", "col"),
    )


    return jax.shard_map(
        body,
        mesh=mesh,
        in_specs=placed,
        out_specs=(
            P("dp", "col"),
            P("dp", "col"),
            P(("col", "dp")),
            P(("col", "dp"), "row"),
            P(("col", "dp"), "row"),
            P(("col", "dp"), "row"),
            P(),
            P(),
            P("row", ("col", "dp")),
            P(("col", "dp")),
            P(("col", "dp"), "row"),
            P(("col", "dp"), "row"),
            P("row", ("col", "dp")),
        ),
        check_vma=False,
    )
```

```python
import jax
import jax.numpy as jnp
from jax import lax
from jax.experimental import pallas as pl
from jax.experimental.pallas import tpu as pltpu
from jax.sharding import PartitionSpec as P


EPSILON = 1e-05
THETA = 1000000.0
NEGATIVE = -1e30


F32 = jnp.float32
BF16 = jnp.bfloat16


def matmul(left, right):
    return jnp.dot(left, right, preferred_element_type=F32)


def matmul_nt(left, right):
    return lax.dot_general(left, right, (((1,), (1,)), ((), ())), preferred_element_type=F32)


def matmul_tn(left, right):
    return lax.dot_general(left, right, (((0,), (0,)), ((), ())), preferred_element_type=F32)


def flip(values, axis, distance):
    size = lax.axis_size(axis)
    return lax.ppermute(values, axis, [(i, i ^ distance) for i in range(size)])


def spread(values):
    return [values] + [flip(values, "col", k) for k in range(1, lax.axis_size("col"))]


def exchange(pieces):
    return [pieces[0]] + [flip(pieces[k], "col", k) for k in range(1, len(pieces))]


def total(parts):
    result = parts[0].astype(F32)
    for part in parts[1:]:
        result = result + part.astype(F32)
    return result


def kernel_call(kernel, outs, *args, scalars=None, scratch=(), fetch=0, room=8):
    specs = [pl.BlockSpec(memory_space=pltpu.HBM)] * fetch
    specs = specs + [pl.BlockSpec(memory_space=pltpu.VMEM)] * (len(args) - fetch)
    scratch_shapes = [pltpu.VMEM(shape, dtype) for shape, dtype in scratch]
    if fetch:
        scratch_shapes = [pltpu.VMEM(v.shape, v.dtype) for v in args[:fetch]] + scratch_shapes
        scratch_shapes.append(pltpu.SemaphoreType.DMA((fetch,)))
    if scalars is not None:
        args = (scalars,) + args
        specs = [pl.BlockSpec(memory_space=pltpu.SMEM)] + specs
    return pl.pallas_call(
        kernel,
        out_shape=[jax.ShapeDtypeStruct(shape, dtype) for shape, dtype in outs],
        in_specs=specs,
        out_specs=[pl.BlockSpec(memory_space=pltpu.VMEM)] * len(outs),
        scratch_shapes=scratch_shapes,
        compiler_params=pltpu.CompilerParams(vmem_limit_bytes=room * 1024 * 1024),
    )(*args)


def fetched(sources, targets, semaphores):
    copies = [
        pltpu.make_async_copy(source, target, semaphores.at[i])
        for i, (source, target) in enumerate(zip(sources, targets))
    ]
    for copy in copies:
        copy.start()
    for copy in copies:
        copy.wait()


def pack_one_kernel(
    where, x_in, query_in, key_in, value_in, gain_first, gain_second,
    out0, out1, out2, out3, x, query, key, value, semaphores,
):
    fetched((x_in, query_in, key_in, value_in), (x, query, key, value), semaphores)
    outs = (out0, out1, out2, out3)
    row, col = where[0], where[1]
    half = x.shape[0] // 2
    cols = len(outs)
    q_size, kv_size = query.shape[1] // cols, key.shape[1] // cols
    line = lax.broadcasted_iota(jnp.int32, (16, x.shape[1]), 0)
    rows = jnp.zeros((16, x.shape[1]), F32)
    for g, gain in enumerate((gain_first, gain_second)):
        rest = gain[...]
        for p in range(3):
            part = rest.astype(BF16).astype(F32)
            rows = jnp.where(line == 3 * g + p, part, rows)
            rest = rest - part
    mine = x[pl.ds(pl.multiple_of(row * half, half), half), :]
    for k, out in enumerate(outs):
        block = col ^ k
        out[:half, :] = mine
        out[half : half + 16, :] = rows.astype(BF16)
        out[half + 16 :, :q_size] = query[:, pl.ds(pl.multiple_of(block * q_size, q_size), q_size)]
        pair = pl.multiple_of((block >> 1) * (2 * kv_size), 2 * kv_size)
        odd = (block & 1) == 1
        both = []
        for weight in (key, value):
            two = weight[:, pl.ds(pair, 2 * kv_size)]
            both.append(jnp.where(odd, two[:, kv_size:], two[:, :kv_size]))
        out[half + 16 :, q_size:] = jnp.concatenate(both, axis=1)


def pack_two_kernel(
    where, weight_in, cot_in, out0, out1, out2, out3, weight, cot, semaphores
):
    fetched((weight_in, cot_in), (weight, cot), semaphores)
    outs = (out0, out1, out2, out3)
    size, half = weight.shape[0] // len(outs), cot.shape[0] // 2
    for k, out in enumerate(outs):
        out[:half, :] = cot[pl.ds(pl.multiple_of(where[0] * half, half), half), :]
        for j in range(len(outs)):
            source = pl.multiple_of((where[1] ^ (k ^ j)) * size, size)
            out[half + j * size : half + (j + 1) * size, :] = weight[pl.ds(source, size), :]


def pack_three_kernel(where, down_in, out0, out1, out2, out3, down, semaphores):
    fetched((down_in,), (down,), semaphores)
    outs = (out0, out1, out2, out3)
    size = down.shape[0] // len(outs)
    for k, out in enumerate(outs):
        out[...] = down[pl.ds(pl.multiple_of((where[1] ^ k) * size, size), size), :]


def pack_gate_kernel(
    where, gate_in, up_in, out0, out1, out2, out3, out4, gate, up, semaphores
):
    fetched((gate_in, up_in), (gate, up), semaphores)
    outs = (out0, out1, out2, out3, out4)
    col, odd_plane = where[1], (where[2] & 1) == 1
    cols = len(outs) - 1
    size = gate.shape[1] // cols

    def piece(weight, block):
        two = weight[:, pl.ds(pl.multiple_of((block >> 1) * (2 * size), 2 * size), 2 * size)]
        return jnp.where((block & 1) == 1, two[:, size:], two[:, :size])

    @pl.when(jnp.logical_not(odd_plane))
    def _():
        for k in range(cols):
            outs[k][...] = piece(gate, col ^ k)
        outs[cols][...] = piece(up, col)

    @pl.when(odd_plane)
    def _():
        for k in range(cols):
            outs[k][...] = piece(up, col ^ k)
        outs[cols][...] = piece(gate, col)


def join_kernel(first0, first1, first2, first3, out):
    part, size = first0.shape[1], out.shape[0]
    for k, piece in enumerate((first0, first1, first2, first3)):
        out[:, k * part : (k + 1) * part] = piece[piece.shape[0] - size :, :]


def project_kernel(
    where, mine, other, context_near, context_far, joined, joined_far,
    first0, first1, first2, first3, normed_out, own_out, share_out, sum_scratch,
):
    buffers = (first0, first1, first2, first3)
    half, part = mine.shape[0], first0.shape[1]
    share = share_out.shape[0]
    top = mine[...].astype(F32) + matmul(context_near[:half, :], joined[...])
    top = top + matmul(context_far[half:, :], joined_far[...])
    low = other[...].astype(F32) + matmul(context_near[half:, :], joined[...])
    low = low + matmul(context_far[:half, :], joined_far[...])
    sum_scratch[...] = top
    own_out[...] = top[:, :part]
    share_out[...] = sum_scratch[pl.ds(pl.multiple_of(where[1] * share, share), share), :]
    gain = jnp.concatenate([gain_row(buffers, half + 3, k) for k in range(len(buffers))], axis=1)
    for i, rows in enumerate((top, low)):
        root = lax.rsqrt(jnp.mean(rows * rows, axis=1, keepdims=True) + EPSILON)
        normed_out[i * half : (i + 1) * half, :] = (rows * root * gain).astype(BF16)


def hidden_kernel(
    where, normed, near0, near1, near2, near3, far0, far1, far2, far3,
    gate_out, up_out, hidden_out,
):
    part = near0.shape[0]
    first_pre = second_pre = None
    for k, (near, far) in enumerate(
        ((near0, far0), (near1, far1), (near2, far2), (near3, far3))
    ):
        block = normed[:, k * part : (k + 1) * part]
        one, two = matmul(block, near[...]), matmul(block, far[...])
        first_pre = one if k == 0 else first_pre + one
        second_pre = two if k == 0 else second_pre + two
    even = (where[2] & 1) == 0
    gate_pre = jnp.where(even, first_pre, second_pre)
    up_pre = jnp.where(even, second_pre, first_pre)
    gate_out[...] = gate_pre
    up_out[...] = up_pre
    hidden_out[...] = (gate_pre * (1.0 / (1.0 + jnp.exp(-gate_pre))) * up_pre).astype(BF16)


def backward_kernel(
    where, cot_mine, cot_other, gate_in, up_in, down0, down1, down2, down3,
    near0, near1, near2, near3, far0, far1, far2, far3,
    gate_grad_out, up_grad_out, mine_out, other_out,
):
    half, part = mine_out.shape[0], near0.shape[0]
    size = gate_in.shape[1]
    parts = []
    for rows in (cot_mine, cot_other):
        grad = None
        for k, down in enumerate((down0, down1, down2, down3)):
            term = matmul_nt(rows[:, k * part : (k + 1) * part], down[:size, :])
            grad = term if k == 0 else grad + term
        parts.append(grad)
    hidden_grad = jnp.concatenate(parts, axis=0)
    gate_pre, up_pre = gate_in[...], up_in[...]
    sigmoid_gate = 1.0 / (1.0 + jnp.exp(-gate_pre))
    gate_grad = (
        hidden_grad * up_pre * sigmoid_gate * (1.0 + gate_pre * (1.0 - sigmoid_gate))
    ).astype(BF16)
    up_grad = (hidden_grad * (gate_pre * sigmoid_gate)).astype(BF16)
    gate_grad_out[...] = gate_grad
    up_grad_out[...] = up_grad
    even = (where[2] & 1) == 0
    near_grad = jnp.where(even, gate_grad, up_grad)
    far_grad = jnp.where(even, up_grad, gate_grad)
    for k, (near, far) in enumerate(
        ((near0, far0), (near1, far1), (near2, far2), (near3, far3))
    ):
        block = matmul_nt(near_grad, near[...]) + matmul_nt(far_grad, far[...])
        mine_out[:, k * part : (k + 1) * part] = block[:half].astype(BF16)
        other_out[:, k * part : (k + 1) * part] = block[half:].astype(BF16)


def result_kernel(hidden, down0, down1, down2, down3, mine_out, other_out):
    half, part = mine_out.shape[0], down0.shape[1]
    for k, down in enumerate((down0, down1, down2, down3)):
        block = matmul(hidden[...], down[: hidden.shape[1], :])
        mine_out[:, k * part : (k + 1) * part] = block[:half].astype(BF16)
        other_out[:, k * part : (k + 1) * part] = block[half:].astype(BF16)


def deal(where, scratch, k, send, keep, rows):
    for j in range(2):
        for out, m in ((send, 1 + 2 * j), (keep, 2 * j)):
            start = pl.multiple_of((where[2] ^ m) * rows, rows)
            out[j, k, :rows, :] = scratch[pl.ds(start, rows), :]


def down_grad_kernel(where, cot_mine, cot_other, hidden, send, keep, scratch):
    half = hidden.shape[0] // 2
    cols, rows = send.shape[1], send.shape[2]
    part = cot_mine.shape[1] // cols
    for k in range(cols):
        span = slice(k * part, (k + 1) * part)
        grad = matmul_tn(cot_mine[:, span], hidden[:half, :])
        grad = grad + matmul_tn(cot_other[:, span], hidden[half:, :])
        scratch[...] = grad.astype(BF16)
        deal(where, scratch, k, send, keep, rows)


def weight_grad_kernel(
    where, normed, gate_grad, up_grad, gate_send, gate_keep, up_send, up_keep, scratch
):
    cols, rows = gate_send.shape[1], gate_send.shape[2]
    part = normed.shape[1] // cols
    for upstream, send, keep in ((gate_grad, gate_send, gate_keep), (up_grad, up_send, up_keep)):
        for k in range(cols):
            span = slice(k * part, (k + 1) * part)
            scratch[...] = matmul_tn(normed[:, span], upstream[...]).astype(BF16)
            deal(where, scratch, k, send, keep, rows)


def pack_tokens_kernel(where, ours, came, out0, out1, out2, out3, scratch):
    outs = (out0, out1, out2, out3)
    share, part = out0.shape[0], out0.shape[1] // len(outs)
    scratch[...] = (ours[...].astype(F32) + came[...].astype(F32)).astype(BF16)
    for k, out in enumerate(outs):
        rows = pl.ds(pl.multiple_of((where[1] ^ k) * share, share), share)
        for j in range(len(outs)):
            source = k ^ j
            out[:, j * part : (j + 1) * part] = scratch[rows, source * part : (source + 1) * part]


def second_norm_kernel(
    where, came0, came1, came2, came3, sums, cot_mine, first0, first1, first2, first3,
    out0, out1, out2, out3, gain_out,
):
    buffers = (first0, first1, first2, first3)
    outs = (out0, out1, out2, out3)
    share, part = out0.shape[0], out0.shape[1] // len(outs)
    half = share * len(outs)
    grad = came0[...].astype(F32) + came1[...].astype(F32)
    grad = grad + came2[...].astype(F32) + came3[...].astype(F32)
    gain = jnp.concatenate([gain_row(buffers, half + 3, k) for k in range(len(buffers))], axis=1)
    rows = sums[...]
    root = lax.rsqrt(jnp.mean(rows * rows, axis=1, keepdims=True) + EPSILON)
    normal = rows * root
    weighted = grad * gain
    gain_out[...] = jnp.sum(grad * normal, axis=0, keepdims=True)
    inner = jnp.mean(weighted * normal, axis=1, keepdims=True)
    cot = cot_mine[pl.ds(pl.multiple_of(where[1] * share, share), share), :].astype(F32)
    first = (cot + root * (weighted - normal * inner)).astype(BF16)
    for k, out in enumerate(outs):
        for j in range(len(outs)):
            source = k ^ j
            out[:, j * part : (j + 1) * part] = first[:, source * part : (source + 1) * part]


def join_tokens_kernel(where, came0, came1, came2, came3, out):
    share = came0.shape[0]
    for k, came in enumerate((came0, came1, came2, came3)):
        out[pl.ds(pl.multiple_of((where[1] ^ k) * share, share), share), :] = came[...]


def pack_features_kernel(ours, came, out0, out1, out2, out3):
    part = out0.shape[1]
    for k, out in enumerate((out0, out1, out2, out3)):
        span = slice(k * part, (k + 1) * part)
        out[...] = (ours[:, span].astype(F32) + came[:, span].astype(F32)).astype(BF16)


def pack_last_kernel(ours, came, inner, inner_came, out0, out1, out2, out3):
    half, part = ours.shape[0], out0.shape[1]
    line = lax.broadcasted_iota(jnp.int32, (16, part), 0)
    rows = jnp.zeros((16, part), F32)
    rest = inner[0:1, :half] + inner_came[0:1, :]
    for p in range(3):
        piece = rest.astype(BF16).astype(F32)
        rows = jnp.where(line == p, piece, rows)
        rest = rest - piece
    for k, out in enumerate((out0, out1, out2, out3)):
        span = slice(k * part, (k + 1) * part)
        out[:half, :] = (ours[:, span].astype(F32) + came[:, span].astype(F32)).astype(BF16)
        out[half:, :] = rows.astype(BF16)


def join_first_kernel(first0, first1, first2, first3, out):
    part, size = first0.shape[1], out.shape[0]
    for k, piece in enumerate((first0, first1, first2, first3)):
        out[:, k * part : (k + 1) * part] = piece[:size, :]


def in_chip_order(where, pieces):
    odd, high = (where[1] & 1) == 1, (where[1] & 2) == 2
    ordered = []
    for s in range(4):
        low_pair = jnp.where(odd, pieces[s ^ 1], pieces[s])
        high_pair = jnp.where(odd, pieces[s ^ 3], pieces[s ^ 2])
        ordered.append(jnp.where(high, high_pair, low_pair))
    return ordered


def plane_sum(keep, came, far, k):
    return keep[0, k].astype(F32) + came[0, k].astype(F32) + far[k].astype(F32)


def sum_feed_kernel(
    keep0, came0, far0, keep1, came1, far1, out0, out1, out2, out3
):
    rows = keep0.shape[2]
    for k, out in enumerate((out0, out1, out2, out3)):
        out[:rows, :] = plane_sum(keep0, came0, far0, k).astype(BF16)
        out[rows:, :] = plane_sum(keep1, came1, far1, k).astype(BF16)


def sum_kernel(keep, came, far, out0, out1, out2, out3):
    for k, out in enumerate((out0, out1, out2, out3)):
        out[...] = plane_sum(keep, came, far, k).astype(BF16)


def unpack_feed_kernel(where, came0, came1, came2, came3, down_out, gate_out):
    rows = gate_out.shape[0]
    pieces = in_chip_order(where, [v[...] for v in (came0, came1, came2, came3)])
    for i, out in enumerate((down_out, gate_out)):
        span = slice(i * rows, (i + 1) * rows)
        out[...] = jnp.concatenate([v[span].astype(F32) for v in pieces], axis=1)


def unpack_up_kernel(where, came0, came1, came2, came3, up_out):
    pieces = in_chip_order(where, [v[...] for v in (came0, came1, came2, came3)])
    up_out[...] = jnp.concatenate([v.astype(F32) for v in pieces], axis=1)


def unpack_last_kernel(
    where, came0, came1, came2, came3, query_out, key_out, value_out, output_out, gain_out
):
    rows = query_out.shape[0]
    pieces = in_chip_order(where, [v[...] for v in (came0, came1, came2, came3)])
    two = query_out.shape[1] // len(pieces)
    size = two // 2
    pieces = [v.astype(F32) for v in pieces]
    for out, start, wide in (
        (query_out, 0, two), (key_out, two, size), (value_out, two + size, size),
        (output_out, 2 * two, two),
    ):
        out[...] = jnp.concatenate([v[:rows, start : start + wide] for v in pieces], axis=1)
    gain_out[...] = pieces[0][rows:] + pieces[1][rows:] + pieces[2][rows:] + pieces[3][rows:]


def gain_kernel(where, ours, came, attention_out, feed_out, query_out, key_out):
    lines = ours[...] + came[...]
    rows, head = attention_out.shape[1], query_out.shape[1]
    odd, high = (where[2] & 1) == 1, (where[2] & 2) == 2
    for out, i in ((attention_out, 0), (feed_out, 1)):
        parts = [lines[i : i + 1, p * rows : (p + 1) * rows] for p in range(4)]
        low = jnp.where(odd, parts[1], parts[0])
        out[...] = jnp.where(high, jnp.where(odd, parts[3], parts[2]), low)
    query_out[...] = lines[0:1, 4 * rows : 4 * rows + head]
    key_out[...] = lines[0:1, 4 * rows + head :]


def lane_is_first(size):
    return lax.broadcasted_iota(jnp.int32, (1, 2 * size), 1) < size


def head_scale(values, first):
    size = values.shape[1] // 2
    squares = values * values
    left = jnp.sum(jnp.where(first, squares, 0.0), axis=1, keepdims=True)
    right = jnp.sum(jnp.where(first, 0.0, squares), axis=1, keepdims=True)
    return lax.rsqrt(jnp.where(first, left, right) / size + EPSILON)


def turn(values, cosine, sine):
    width = values.shape[1]
    quarter = width // 4
    lane = lax.broadcasted_iota(jnp.int32, (1, width), 1)
    low = (lane & quarter) == 0
    other = jnp.where(
        low, pltpu.roll(values, width - quarter, 1), pltpu.roll(values, quarter, 1)
    )
    return values * cosine + other * sine


def root_and_input(mine, other):
    rows = jnp.concatenate([mine[...], other[...]], axis=0).astype(F32)
    mean = jnp.mean(rows * rows, axis=1, keepdims=True)
    return rows, lax.rsqrt(mean + EPSILON)


def gain_row(buffers, start, k):
    rows = buffers[k][start : start + 16, :].astype(F32)
    return rows[0:1] + rows[1:2] + rows[2:3]


def allowed_of(down, across):
    return (across[0:1, :] <= down[:, 0:1]) & (across[1:2, :] == down[:, 1:2])


def attend_kernel(
    mine, other, first0, first1, first2, first3, cosine, sine, gains, down, across,
    qkv_out, turned_out, context_out, log_out,
):
    buffers = (first0, first1, first2, first3)
    half, part = mine.shape[0], first0.shape[1]
    rows, root = root_and_input(mine, other)
    start = half + 16
    qkv = None
    for k, buffer in enumerate(buffers):
        block = rows[:, k * part : (k + 1) * part] * root * gain_row(buffers, half, k)
        term = matmul(block.astype(BF16), buffer[start:, :])
        qkv = term if qkv is None else qkv + term
    qkv_out[...] = qkv
    two = qkv.shape[1] // 2
    size = two // 2
    first = lane_is_first(size)
    query, pair = qkv[:, :two], qkv[:, two:]
    query_turned = turn(
        query * head_scale(query, first) * gains[0:1, :], cosine[...], sine[...]
    ).astype(BF16)
    key_turned = turn(pair * head_scale(pair, first) * gains[1:2, :], cosine[...], sine[...])
    pair_rounded = jnp.where(first, key_turned, pair).astype(BF16)
    turned_out[:, :two] = query_turned
    turned_out[:, two:] = pair_rounded
    key, value = pair_rounded[:, :size], pair_rounded[:, size:]
    allowed = allowed_of(down, across)
    contexts, logs = [], []
    for h in range(2):
        raw = matmul_nt(query_turned[:, h * size : (h + 1) * size], key)
        scores = jnp.where(allowed, raw * size ** (-0.5), NEGATIVE)
        top = jnp.max(scores, axis=1, keepdims=True)
        powers = jnp.exp(scores - top)
        sums = jnp.sum(powers, axis=1, keepdims=True)
        prob = (powers * (1.0 / sums)).astype(BF16)
        contexts.append(matmul(prob, value))
        logs.append(top + jnp.log(sums))
    context_out[...] = jnp.concatenate(contexts, axis=1).astype(BF16)
    log_out[...] = jnp.where(first, logs[0], logs[1])


def attend_back_kernel(
    where, mine, other, first0, first1, first2, first3, cosine, sine, gains, down, across,
    qkv_in, turned, context_in, logs, grad_mine, grad_other, out_weight,
    gain_in, one_mine, one_other, inner_out, mixed_send, mixed_keep, mixed,
):
    buffers = (first0, first1, first2, first3)
    half, part = mine.shape[0], first0.shape[1]
    two = context_in.shape[1]
    size = two // 2
    first = lane_is_first(size)
    upstream = jnp.concatenate([grad_mine[...], grad_other[...]], axis=0)
    context = context_in[...]
    context_grad = matmul_nt(upstream, out_weight[:two, :]).astype(BF16)
    key, value = turned[:, two : two + size], turned[:, two + size :]
    allowed = allowed_of(down, across)
    products = context_grad.astype(F32) * context.astype(F32)
    query_grads = []
    key_grad = value_grad = None
    for h in range(2):
        query = turned[:, h * size : (h + 1) * size]
        grad = context_grad[:, h * size : (h + 1) * size]
        raw = matmul_nt(query, key)
        scores = jnp.where(allowed, raw * size ** (-0.5), NEGATIVE)
        prob = jnp.exp(scores - logs[:, h * size : h * size + 1])
        delta = jnp.sum(
            jnp.where(first if h == 0 else jnp.logical_not(first), products, 0.0),
            axis=1,
            keepdims=True,
        )
        value_term = matmul_tn(prob.astype(BF16), grad)
        score_grad = (prob * (matmul_nt(grad, value) - delta) * size ** (-0.5)).astype(BF16)
        query_grads.append(matmul(score_grad, key))
        key_term = matmul_tn(score_grad, query)
        key_grad = key_term if h == 0 else key_grad + key_term
        value_grad = value_term if h == 0 else value_grad + value_term
    pieces, head_parts = [], []
    for i, grad in enumerate(
        (jnp.concatenate(query_grads, axis=1), jnp.concatenate([key_grad, value_grad], axis=1))
    ):
        normed = turn(grad, cosine[...], -sine[...])
        proj = qkv_in[:, i * two : (i + 1) * two]
        scale = head_scale(proj, first)
        hat = proj * scale
        weighted = normed * gains[i : i + 1, :]
        product = weighted * hat
        left = jnp.sum(jnp.where(first, product, 0.0), axis=1, keepdims=True)
        right = jnp.sum(jnp.where(first, 0.0, product), axis=1, keepdims=True)
        inner = jnp.where(first, left, right) / size
        result = scale * (weighted - hat * inner)
        pieces.append(result if i == 0 else jnp.where(first, result, grad))
        head_parts.append(jnp.sum(normed * hat, axis=0, keepdims=True))
    head_line = head_parts[0] + pltpu.roll(head_parts[0], size, 1)
    head_line = jnp.where(first, head_line, pltpu.roll(head_parts[1], size, 1))
    rows_here = mixed_send.shape[2] - 8
    line = lax.broadcasted_iota(jnp.int32, (8, part), 0)
    qkv_grad = jnp.concatenate(pieces, axis=1).astype(BF16)
    rows, root = root_and_input(mine, other)
    inner_sum = jnp.zeros((2 * half, 1), F32)
    for k, buffer in enumerate(buffers):
        span = slice(k * part, (k + 1) * part)
        gain = gain_row(buffers, half, k)
        hat = rows[:, span] * root
        grad = matmul_nt(qkv_grad, buffer[half + 16 :, :])
        product = grad * hat
        lines = jnp.where(line == 0, jnp.sum(product, axis=0, keepdims=True), 0.0)
        lines = jnp.where(line == 1, gain_in[:, span], lines).astype(BF16)
        inner_sum = inner_sum + jnp.sum(product * gain, axis=1, keepdims=True)
        one_mine[:, span] = grad[:half].astype(BF16)
        one_other[:, span] = grad[half:].astype(BF16)
        mixed[:, : 2 * two] = matmul_tn((hat * gain).astype(BF16), qkv_grad).astype(BF16)
        mixed[:, 2 * two :] = matmul_tn(upstream[:, span], context).astype(BF16)
        heads = jnp.broadcast_to(head_line, (8, two)).astype(BF16)
        if mixed_send.shape[0] == 2:
            deal(where, mixed, k, mixed_send, mixed_keep, rows_here)
            for out in (mixed_send, mixed_keep):
                for j in range(2):
                    out[j, k, rows_here:, : 2 * two] = lines
                    out[j, k, rows_here:, 2 * two :] = heads
        else:
            mixed_send[k, ...] = mixed[...]
            mixed_keep[k, :, : 2 * two] = lines
            mixed_keep[k, :, 2 * two :] = heads
    wide = jnp.broadcast_to(inner_sum / (part * len(buffers)), (2 * half, 128))
    inner_out[...] = jnp.transpose(wide)[:8, :]


def rope_tables(places, head_size):
    half_size = head_size // 2
    frequency = THETA ** (-(jnp.arange(half_size).astype(F32) * 2.0 / head_size))
    angles = places.astype(F32)[:, None] * frequency[None, :]
    return (jnp.cos(angles), jnp.sin(angles))


def body(
    block_input,
    segments,
    positions,
    attention_gain,
    query_weight,
    key_weight,
    value_weight,
    query_gain,
    key_gain,
    output_weight,
    feedforward_gain,
    gate_weight,
    up_weight,
    down_weight,
    cotangent,
):
    tokens = block_input.shape[0]
    part = block_input.shape[1]
    head = query_gain.shape[0]
    cols = lax.axis_size("col")
    planes = lax.axis_size("dp")
    width = part * cols
    half = tokens // 2
    row = lax.axis_index("row")
    col = lax.axis_index("col")
    plane = lax.axis_index("dp")

    def mine_first(values):
        return jnp.where(row == 0, values, jnp.roll(values, half, axis=0))

    def natural(values):
        return jnp.where(row == 0, values, jnp.roll(values, half, axis=0))

    q_size = query_weight.shape[1] // cols
    units = gate_weight.shape[1] // cols
    where = jnp.stack([row, col, plane]).astype(jnp.int32)
    shapes = [((half + 16 + part, part), BF16)] * cols
    first_in = exchange(
        kernel_call(
            pack_one_kernel,
            shapes,
            block_input,
            query_weight,
            key_weight,
            value_weight,
            attention_gain.reshape(1, part),
            feedforward_gain.reshape(1, part),
            scalars=where,
            fetch=4, room=60),
    )
    (input_mine,) = kernel_call(join_first_kernel, [((half, width), BF16)], *first_in, room=10)
    gain_parts = jnp.concatenate([v[half : half + 16] for v in first_in], axis=1).astype(F32)
    gain_one = gain_parts[0] + gain_parts[1] + gain_parts[2]
    input_other = flip(input_mine, "row", 1)
    gate_in = kernel_call(
        pack_gate_kernel,
        [((part, units), BF16)] * (cols + 1),
        gate_weight,
        up_weight,
        scalars=where,
        fetch=2, room=12)
    near_parts = exchange(gate_in[:cols])
    far_parts = [gate_in[cols]] + [flip(v, "dp", 1) for v in near_parts[1:]]
    inner_size = output_weight.shape[0]
    two_out = kernel_call(
        pack_two_kernel,
        [((half + inner_size, part), BF16)] * cols,
        output_weight,
        cotangent,
        scalars=where,
        fetch=2,
    )
    second_parts = exchange(two_out)
    three_out = kernel_call(
        pack_three_kernel,
        [((units, part), BF16)] * cols,
        down_weight,
        scalars=where,
        fetch=1,
    )
    down_parts = exchange(three_out)

    group = q_size // head
    segment_ids = mine_first(segments)
    places = mine_first(positions)
    index = mine_first(jnp.arange(tokens))

    cosine, sine_part = rope_tables(places, head)
    cos_lanes = jnp.concatenate([cosine] * (2 * group), axis=1)
    sin_lanes = jnp.concatenate([-sine_part, sine_part] * group, axis=1)
    head_gains = jnp.stack([jnp.tile(query_gain, group), jnp.tile(key_gain, group)])
    down = jnp.stack([index, segment_ids], axis=1)
    across = jnp.stack([index, segment_ids])
    common = (
        input_mine,
        input_other,
        *first_in,
        cos_lanes,
        sin_lanes,
        head_gains,
        down,
        across,
    )
    qkv, turned, context, logs = kernel_call(
        attend_kernel,
        [
            ((tokens, 2 * q_size), F32),
            ((tokens, 2 * q_size), BF16),
            ((tokens, q_size), BF16),
            ((tokens, q_size), F32),
        ],
        *common, room=26)

    context_parts = spread(context)
    (context_near,) = kernel_call(join_kernel, [((tokens, inner_size), BF16)], *context_parts, room=10)
    context_far = flip(context_near, "row", 1)
    (second_in,) = kernel_call(join_kernel, [((inner_size, width), BF16)], *second_parts, room=10)
    second_far = flip(second_in, "row", 1)
    (cot_mine,) = kernel_call(join_first_kernel, [((half, width), BF16)], *second_parts, room=10)
    cot_other = flip(cot_mine, "row", 1)

    share = half // cols
    normed_two, first_block, first_share = kernel_call(
        project_kernel,
        [((tokens, width), BF16), ((half, part), F32), ((share, width), F32)],
        input_mine,
        input_other,
        context_near,
        context_far,
        second_in,
        second_far,
        *first_in,
        scalars=where,
        scratch=[((half, width), F32)], room=24)
    gate_pre, up_pre, hidden = kernel_call(
        hidden_kernel,
        [((tokens, units), F32), ((tokens, units), F32), ((tokens, units), BF16)],
        normed_two,
        *near_parts,
        *far_parts,
        scalars=where, room=24)
    rows = part // planes
    if planes == 4:
        down_dealt = kernel_call(
            down_grad_kernel,
            [((2, cols, rows, units), BF16)] * 2,
            cot_mine,
            cot_other,
            hidden,
            scalars=where,
            scratch=[((part, units), BF16)], room=14)
    gate_grad, up_grad, two_mine, two_other = kernel_call(
        backward_kernel,
        [((tokens, units), BF16)] * 2 + [((half, width), BF16)] * 2,
        cot_mine,
        cot_other,
        gate_pre,
        up_pre,
        *down_parts,
        *near_parts,
        *far_parts,
        scalars=where, room=30)

    two_came = flip(two_other, "row", 1)
    two_pieces = kernel_call(
        pack_tokens_kernel,
        [((share, width), BF16)] * cols,
        two_mine,
        two_came,
        scalars=where,
        scratch=[((half, width), BF16)],
    )
    two_in = exchange(two_pieces)
    *first_pieces, feedforward_part = kernel_call(
        second_norm_kernel,
        [((share, width), BF16)] * cols + [((1, width), F32)],
        *two_in,
        first_share,
        cot_mine,
        *first_in,
        scalars=where,
    )
    first_back = exchange(first_pieces)
    (first_half,) = kernel_call(
        join_tokens_kernel, [((half, width), BF16)], *first_back, scalars=where
    )
    first_other = flip(first_half, "row", 1)

    def shifted(send, keep):
        came = flip(send, "dp", 1)
        rest = (keep[1].astype(F32) + came[1].astype(F32)).astype(BF16)
        return keep, came, flip(rest, "dp", 2)

    def scattered(split):
        return lax.psum_scatter(split, "dp", scatter_dimension=0, tiled=True)[0]

    if planes == 4:
        dealt = kernel_call(
            weight_grad_kernel,
            [((2, cols, rows, units), BF16)] * 4,
            normed_two,
            gate_grad,
            up_grad,
            scalars=where,
            scratch=[((part, units), BF16)], room=20)
        dealt = list(down_dealt) + list(dealt)
        down_terms, gate_terms, up_terms = [
            shifted(dealt[2 * i], dealt[2 * i + 1])
            for i in range(3)
        ]
        feed_out = kernel_call(
            sum_feed_kernel,
            [((2 * rows, units), BF16)] * cols,
            *down_terms,
            *gate_terms,
            room=16,
        )
        up_out = kernel_call(
            sum_kernel, [((rows, units), BF16)] * cols, *up_terms, room=12
        )
    else:
        cot_all = jnp.concatenate([cot_mine, cot_other], axis=0)
        sums = [
            scattered(
                jnp.moveaxis(grad.astype(BF16).reshape(cols, planes, rows, units), 1, 0)
            )
            for grad in (
                matmul_tn(cot_all, hidden),
                matmul_tn(normed_two, gate_grad),
                matmul_tn(normed_two, up_grad),
            )
        ]
        feed_out = [jnp.concatenate([v[k] for v in sums[:2]], axis=0) for k in range(cols)]
        up_out = [sums[2][k] for k in range(cols)]
    feed_in = exchange(feed_out)
    down_share, gate_share = kernel_call(
        unpack_feed_kernel,
        [((rows, cols * units), F32)] * 2,
        *feed_in,
        scalars=where,
        room=12,
    )

    up_in = exchange(up_out)
    (up_share,) = kernel_call(
        unpack_up_kernel, [((rows, cols * units), F32)], *up_in, scalars=where
    )

    result_mine, result_other = kernel_call(
        result_kernel, [((half, width), BF16)] * 2, hidden, *down_parts, room=12)
    result_came = flip(result_other, "row", 1)
    result_pieces = kernel_call(
        pack_features_kernel, [((half, part), BF16)] * cols, result_mine, result_came
    )
    result_in = exchange(result_pieces)
    result_mine = (first_block + total(result_in)).astype(BF16)
    result_far = flip(result_mine, "row", 1)
    block_output = natural(jnp.concatenate([result_mine, result_far], axis=0))

    mixed_size = 3 * q_size
    if planes == 4:
        mixed_outs = [((2, cols, rows + 8, mixed_size), BF16)] * 2
    else:
        mixed_outs = [((cols, part, mixed_size), BF16), ((cols, 8, mixed_size), BF16)]
    one_mine, one_other, inner_part, mixed_first, mixed_second = kernel_call(
        attend_back_kernel,
        [((half, width), BF16), ((half, width), BF16), ((8, tokens), F32)] + mixed_outs,
        *common,
        qkv,
        turned,
        context,
        logs,
        first_half,
        first_other,
        second_in,
        feedforward_part,
        scalars=where,
        scratch=[((part, mixed_size), BF16)], room=34)
    one_came = flip(one_other, "row", 1)
    inner_came = flip(inner_part[:, half:], "row", 1)
    one_pieces = kernel_call(
        pack_last_kernel,
        [((half + 16, part), BF16)] * cols,
        one_mine,
        one_came,
        inner_part,
        inner_came, room=10)
    one_in = exchange(one_pieces)
    one_grad = total([v[:half] for v in one_in])
    inner_one = jnp.sum(total([v[half:] for v in one_in])[:3], axis=0)[:, None]
    weighted_one = one_grad * gain_one[:part]
    own_input = input_mine.astype(F32)
    root_one = lax.rsqrt(jnp.mean(own_input * own_input, axis=1, keepdims=True) + EPSILON)
    normal_one = own_input[:, :part] * root_one
    input_mine_grad = first_half[:, :part].astype(F32) + root_one * (
        weighted_one - normal_one * inner_one
    )
    input_far_grad = flip(input_mine_grad, "row", 1)
    input_grad = natural(jnp.concatenate([input_mine_grad, input_far_grad], axis=0))

    if planes == 4:
        mixed_terms = shifted(mixed_first, mixed_second)
        last_out = kernel_call(sum_kernel, [((rows + 8, mixed_size), BF16)] * cols, *mixed_terms)
    else:
        lines = jnp.broadcast_to(mixed_second[:, None], (cols, planes, 8, mixed_size))
        blocks = mixed_first.reshape(cols, planes, rows, mixed_size)
        mixed_sum = scattered(jnp.moveaxis(jnp.concatenate([blocks, lines], axis=2), 1, 0))
        last_out = [mixed_sum[k] for k in range(cols)]
    last_in = exchange(last_out)
    query_share, key_share, value_share, output_share, gain_sums = kernel_call(
        unpack_last_kernel,
        [
            ((rows, cols * q_size), F32),
            ((rows, cols * head), F32),
            ((rows, cols * head), F32),
            ((rows, cols * q_size), F32),
            ((8, mixed_size), F32),
        ],
        *last_in,
        scalars=where,
    )
    gain_came = flip(gain_sums, "row", 1)
    if planes == 4:
        attention_share, feedforward_share, query_gain_grad, key_gain_grad = [
            v.reshape(-1)
            for v in kernel_call(
                gain_kernel,
                [((1, rows), F32), ((1, rows), F32), ((1, head), F32), ((1, head), F32)],
                gain_sums,
                gain_came,
                scalars=where,
            )
        ]
    else:
        gain_sums = gain_sums + gain_came
        attention_share = lax.dynamic_slice_in_dim(gain_sums[0], plane * rows, rows, 0)
        feedforward_share = lax.dynamic_slice_in_dim(gain_sums[1], plane * rows, rows, 0)
        query_gain_grad = gain_sums[0, 2 * q_size : 2 * q_size + head]
        key_gain_grad = gain_sums[0, 2 * q_size + head :]
    return (
        block_output,
        input_grad,
        attention_share,
        query_share,
        key_share,
        value_share,
        query_gain_grad,
        key_gain_grad,
        output_share.T,
        feedforward_share,
        gate_share,
        up_share,
        down_share.T,
    )


def solution(mesh):
    placed = (
        P("dp", "col"),
        P("dp"),
        P("dp"),
        P("col"),
        P("col", "row"),
        P("col", "row"),
        P("col", "row"),
        P(),
        P(),
        P("row", "col"),
        P("col"),
        P("col", "row"),
        P("col", "row"),
        P("row", "col"),
        P("dp", "col"),
    )


    return jax.shard_map(
        body,
        mesh=mesh,
        in_specs=placed,
        out_specs=(
            P("dp", "col"),
            P("dp", "col"),
            P(("col", "dp")),
            P(("col", "dp"), "row"),
            P(("col", "dp"), "row"),
            P(("col", "dp"), "row"),
            P(),
            P(),
            P("row", ("col", "dp")),
            P(("col", "dp")),
            P(("col", "dp"), "row"),
            P(("col", "dp"), "row"),
            P("row", ("col", "dp")),
        ),
        check_vma=False,
    )
```

```python
import jax
import jax.numpy as jnp
from jax import lax
from jax.experimental import pallas as pl
from jax.experimental.pallas import tpu as pltpu
from jax.sharding import PartitionSpec as P


EPSILON = 1e-05
THETA = 1000000.0
NEGATIVE = -1e30


F32 = jnp.float32
BF16 = jnp.bfloat16


def matmul(left, right):
    return jnp.dot(left, right, preferred_element_type=F32)


def matmul_nt(left, right):
    return lax.dot_general(left, right, (((1,), (1,)), ((), ())), preferred_element_type=F32)


def matmul_tn(left, right):
    return lax.dot_general(left, right, (((0,), (0,)), ((), ())), preferred_element_type=F32)


def flip(values, axis, distance):
    size = lax.axis_size(axis)
    return lax.ppermute(values, axis, [(i, i ^ distance) for i in range(size)])


def spread(values):
    return [values] + [flip(values, "col", k) for k in range(1, lax.axis_size("col"))]


def exchange(pieces):
    return [pieces[0]] + [flip(pieces[k], "col", k) for k in range(1, len(pieces))]


def total(parts):
    result = parts[0].astype(F32)
    for part in parts[1:]:
        result = result + part.astype(F32)
    return result


def kernel_call(kernel, outs, *args, placed=False, scratch=(), fetch=0, room=8):
    specs = [pl.BlockSpec(memory_space=pltpu.HBM)] * fetch
    specs = specs + [pl.BlockSpec(memory_space=pltpu.VMEM)] * (len(args) - fetch)
    scratch_shapes = [pltpu.VMEM(shape, dtype) for shape, dtype in scratch]
    if fetch:
        scratch_shapes = [pltpu.VMEM(v.shape, v.dtype) for v in args[:fetch]] + scratch_shapes
        scratch_shapes.append(pltpu.SemaphoreType.DMA((fetch,)))
    if placed:
        plain = kernel

        def kernel(*refs):
            plain(tuple(lax.axis_index(axis) for axis in ("row", "col", "dp")), *refs)

    return pl.pallas_call(
        kernel,
        out_shape=[jax.ShapeDtypeStruct(shape, dtype) for shape, dtype in outs],
        in_specs=specs,
        out_specs=[pl.BlockSpec(memory_space=pltpu.VMEM)] * len(outs),
        scratch_shapes=scratch_shapes,
        compiler_params=pltpu.CompilerParams(vmem_limit_bytes=room * 1024 * 1024),
    )(*args)


def fetched(sources, targets, semaphores):
    copies = [
        pltpu.make_async_copy(source, target, semaphores.at[i])
        for i, (source, target) in enumerate(zip(sources, targets))
    ]
    for copy in copies:
        copy.start()
    for copy in copies:
        copy.wait()


def pack_one_kernel(
    where, x_in, query_in, key_in, value_in, gain_first, gain_second,
    out0, out1, out2, out3, x, query, key, value, semaphores,
):
    fetched((x_in, query_in, key_in, value_in), (x, query, key, value), semaphores)
    outs = (out0, out1, out2, out3)
    row, col = where[0], where[1]
    half = x.shape[0] // 2
    cols = len(outs)
    q_size, kv_size = query.shape[1] // cols, key.shape[1] // cols
    line = lax.broadcasted_iota(jnp.int32, (16, x.shape[1]), 0)
    rows = jnp.zeros((16, x.shape[1]), F32)
    for g, gain in enumerate((gain_first, gain_second)):
        rest = gain[...]
        for p in range(3):
            part = rest.astype(BF16).astype(F32)
            rows = jnp.where(line == 3 * g + p, part, rows)
            rest = rest - part
    mine = x[pl.ds(pl.multiple_of(row * half, half), half), :]
    for k, out in enumerate(outs):
        block = col ^ k
        out[:half, :] = mine
        out[half : half + 16, :] = rows.astype(BF16)
        out[half + 16 :, :q_size] = query[:, pl.ds(pl.multiple_of(block * q_size, q_size), q_size)]
        pair = pl.multiple_of((block >> 1) * (2 * kv_size), 2 * kv_size)
        odd = (block & 1) == 1
        both = []
        for weight in (key, value):
            two = weight[:, pl.ds(pair, 2 * kv_size)]
            both.append(jnp.where(odd, two[:, kv_size:], two[:, :kv_size]))
        out[half + 16 :, q_size:] = jnp.concatenate(both, axis=1)


def pack_two_kernel(
    where, weight_in, cot_in, out0, out1, out2, out3, weight, cot, semaphores
):
    fetched((weight_in, cot_in), (weight, cot), semaphores)
    outs = (out0, out1, out2, out3)
    size, half = weight.shape[0] // len(outs), cot.shape[0] // 2
    for k, out in enumerate(outs):
        out[:half, :] = cot[pl.ds(pl.multiple_of(where[0] * half, half), half), :]
        for j in range(len(outs)):
            source = pl.multiple_of((where[1] ^ (k ^ j)) * size, size)
            out[half + j * size : half + (j + 1) * size, :] = weight[pl.ds(source, size), :]


def pack_three_kernel(where, down_in, out0, out1, out2, out3, down, semaphores):
    fetched((down_in,), (down,), semaphores)
    outs = (out0, out1, out2, out3)
    size = down.shape[0] // len(outs)
    for k, out in enumerate(outs):
        out[...] = down[pl.ds(pl.multiple_of((where[1] ^ k) * size, size), size), :]


def pack_gate_kernel(
    where, gate_in, up_in, out0, out1, out2, out3, out4, gate, up, semaphores
):
    fetched((gate_in, up_in), (gate, up), semaphores)
    outs = (out0, out1, out2, out3, out4)
    col, odd_plane = where[1], (where[2] & 1) == 1
    cols = len(outs) - 1
    size = gate.shape[1] // cols

    def piece(weight, block):
        two = weight[:, pl.ds(pl.multiple_of((block >> 1) * (2 * size), 2 * size), 2 * size)]
        return jnp.where((block & 1) == 1, two[:, size:], two[:, :size])

    @pl.when(jnp.logical_not(odd_plane))
    def _():
        for k in range(cols):
            outs[k][...] = piece(gate, col ^ k)
        outs[cols][...] = piece(up, col)

    @pl.when(odd_plane)
    def _():
        for k in range(cols):
            outs[k][...] = piece(up, col ^ k)
        outs[cols][...] = piece(gate, col)


def join_kernel(first0, first1, first2, first3, out):
    part, size = first0.shape[1], out.shape[0]
    for k, piece in enumerate((first0, first1, first2, first3)):
        out[:, k * part : (k + 1) * part] = piece[piece.shape[0] - size :, :]


def project_kernel(
    where, mine, other, context_near, context_far, joined, joined_far,
    first0, first1, first2, first3, normed_out, own_out, share_out, sum_scratch,
):
    buffers = (first0, first1, first2, first3)
    half, part = mine.shape[0], first0.shape[1]
    share = share_out.shape[0]
    top = mine[...].astype(F32) + matmul(context_near[:half, :], joined[...])
    top = top + matmul(context_far[half:, :], joined_far[...])
    low = other[...].astype(F32) + matmul(context_near[half:, :], joined[...])
    low = low + matmul(context_far[:half, :], joined_far[...])
    sum_scratch[...] = top
    own_out[...] = top[:, :part]
    share_out[...] = sum_scratch[pl.ds(pl.multiple_of(where[1] * share, share), share), :]
    gain = jnp.concatenate([gain_row(buffers, half + 3, k) for k in range(len(buffers))], axis=1)
    for i, rows in enumerate((top, low)):
        root = lax.rsqrt(jnp.mean(rows * rows, axis=1, keepdims=True) + EPSILON)
        normed_out[i * half : (i + 1) * half, :] = (rows * root * gain).astype(BF16)


def hidden_kernel(
    where, normed, near0, near1, near2, near3, far0, far1, far2, far3,
    gate_out, up_out, hidden_out,
):
    part = near0.shape[0]
    first_pre = second_pre = None
    for k, (near, far) in enumerate(
        ((near0, far0), (near1, far1), (near2, far2), (near3, far3))
    ):
        block = normed[:, k * part : (k + 1) * part]
        one, two = matmul(block, near[...]), matmul(block, far[...])
        first_pre = one if k == 0 else first_pre + one
        second_pre = two if k == 0 else second_pre + two
    even = (where[2] & 1) == 0
    gate_pre = jnp.where(even, first_pre, second_pre)
    up_pre = jnp.where(even, second_pre, first_pre)
    gate_out[...] = gate_pre
    up_out[...] = up_pre
    hidden_out[...] = (gate_pre * (1.0 / (1.0 + jnp.exp(-gate_pre))) * up_pre).astype(BF16)


def backward_kernel(
    where, cot_mine, cot_other, gate_in, up_in, down0, down1, down2, down3,
    near0, near1, near2, near3, far0, far1, far2, far3,
    gate_grad_out, up_grad_out, mine_out, other_out,
):
    half, part = mine_out.shape[0], near0.shape[0]
    size = gate_in.shape[1]
    parts = []
    for rows in (cot_mine, cot_other):
        grad = None
        for k, down in enumerate((down0, down1, down2, down3)):
            term = matmul_nt(rows[:, k * part : (k + 1) * part], down[:size, :])
            grad = term if k == 0 else grad + term
        parts.append(grad)
    hidden_grad = jnp.concatenate(parts, axis=0)
    gate_pre, up_pre = gate_in[...], up_in[...]
    sigmoid_gate = 1.0 / (1.0 + jnp.exp(-gate_pre))
    gate_grad = (
        hidden_grad * up_pre * sigmoid_gate * (1.0 + gate_pre * (1.0 - sigmoid_gate))
    ).astype(BF16)
    up_grad = (hidden_grad * (gate_pre * sigmoid_gate)).astype(BF16)
    gate_grad_out[...] = gate_grad
    up_grad_out[...] = up_grad
    even = (where[2] & 1) == 0
    near_grad = jnp.where(even, gate_grad, up_grad)
    far_grad = jnp.where(even, up_grad, gate_grad)
    for k, (near, far) in enumerate(
        ((near0, far0), (near1, far1), (near2, far2), (near3, far3))
    ):
        block = matmul_nt(near_grad, near[...]) + matmul_nt(far_grad, far[...])
        mine_out[:, k * part : (k + 1) * part] = block[:half].astype(BF16)
        other_out[:, k * part : (k + 1) * part] = block[half:].astype(BF16)


def result_kernel(hidden, down0, down1, down2, down3, mine_out, other_out):
    half, part = mine_out.shape[0], down0.shape[1]
    for k, down in enumerate((down0, down1, down2, down3)):
        block = matmul(hidden[...], down[: hidden.shape[1], :])
        mine_out[:, k * part : (k + 1) * part] = block[:half].astype(BF16)
        other_out[:, k * part : (k + 1) * part] = block[half:].astype(BF16)


def deal(where, scratch, k, send, keep, rows):
    for j in range(2):
        for out, m in ((send, 1 + 2 * j), (keep, 2 * j)):
            start = pl.multiple_of((where[2] ^ m) * rows, rows)
            out[j, k, :rows, :] = scratch[pl.ds(start, rows), :]


def down_grad_kernel(where, cot_mine, cot_other, hidden, send, keep, scratch):
    half = hidden.shape[0] // 2
    cols, rows = send.shape[1], send.shape[2]
    part = cot_mine.shape[1] // cols
    for k in range(cols):
        span = slice(k * part, (k + 1) * part)
        grad = matmul_tn(cot_mine[:, span], hidden[:half, :])
        grad = grad + matmul_tn(cot_other[:, span], hidden[half:, :])
        scratch[...] = grad.astype(BF16)
        deal(where, scratch, k, send, keep, rows)


def weight_grad_kernel(
    where, normed, gate_grad, up_grad, gate_send, gate_keep, up_send, up_keep, scratch
):
    cols, rows = gate_send.shape[1], gate_send.shape[2]
    part = normed.shape[1] // cols
    for upstream, send, keep in ((gate_grad, gate_send, gate_keep), (up_grad, up_send, up_keep)):
        for k in range(cols):
            span = slice(k * part, (k + 1) * part)
            scratch[...] = matmul_tn(normed[:, span], upstream[...]).astype(BF16)
            deal(where, scratch, k, send, keep, rows)


def pack_tokens_kernel(where, ours, came, out0, out1, out2, out3, scratch):
    outs = (out0, out1, out2, out3)
    share, part = out0.shape[0], out0.shape[1] // len(outs)
    scratch[...] = (ours[...].astype(F32) + came[...].astype(F32)).astype(BF16)
    for k, out in enumerate(outs):
        rows = pl.ds(pl.multiple_of((where[1] ^ k) * share, share), share)
        for j in range(len(outs)):
            source = k ^ j
            out[:, j * part : (j + 1) * part] = scratch[rows, source * part : (source + 1) * part]


def second_norm_kernel(
    where, came0, came1, came2, came3, sums, cot_mine, first0, first1, first2, first3,
    out0, out1, out2, out3, gain_out,
):
    buffers = (first0, first1, first2, first3)
    outs = (out0, out1, out2, out3)
    share, part = out0.shape[0], out0.shape[1] // len(outs)
    half = share * len(outs)
    grad = came0[...].astype(F32) + came1[...].astype(F32)
    grad = grad + came2[...].astype(F32) + came3[...].astype(F32)
    gain = jnp.concatenate([gain_row(buffers, half + 3, k) for k in range(len(buffers))], axis=1)
    rows = sums[...]
    root = lax.rsqrt(jnp.mean(rows * rows, axis=1, keepdims=True) + EPSILON)
    normal = rows * root
    weighted = grad * gain
    gain_out[...] = jnp.sum(grad * normal, axis=0, keepdims=True)
    inner = jnp.mean(weighted * normal, axis=1, keepdims=True)
    cot = cot_mine[pl.ds(pl.multiple_of(where[1] * share, share), share), :].astype(F32)
    first = (cot + root * (weighted - normal * inner)).astype(BF16)
    for k, out in enumerate(outs):
        for j in range(len(outs)):
            source = k ^ j
            out[:, j * part : (j + 1) * part] = first[:, source * part : (source + 1) * part]


def join_tokens_kernel(where, came0, came1, came2, came3, out):
    share = came0.shape[0]
    for k, came in enumerate((came0, came1, came2, came3)):
        out[pl.ds(pl.multiple_of((where[1] ^ k) * share, share), share), :] = came[...]


def pack_features_kernel(ours, came, out0, out1, out2, out3):
    part = out0.shape[1]
    for k, out in enumerate((out0, out1, out2, out3)):
        span = slice(k * part, (k + 1) * part)
        out[...] = (ours[:, span].astype(F32) + came[:, span].astype(F32)).astype(BF16)


def pack_last_kernel(ours, came, inner, inner_came, out0, out1, out2, out3):
    half, part = ours.shape[0], out0.shape[1]
    line = lax.broadcasted_iota(jnp.int32, (16, part), 0)
    rows = jnp.zeros((16, part), F32)
    rest = inner[0:1, :half] + inner_came[0:1, :]
    for p in range(3):
        piece = rest.astype(BF16).astype(F32)
        rows = jnp.where(line == p, piece, rows)
        rest = rest - piece
    for k, out in enumerate((out0, out1, out2, out3)):
        span = slice(k * part, (k + 1) * part)
        out[:half, :] = (ours[:, span].astype(F32) + came[:, span].astype(F32)).astype(BF16)
        out[half:, :] = rows.astype(BF16)


def join_first_kernel(first0, first1, first2, first3, out):
    part, size = first0.shape[1], out.shape[0]
    for k, piece in enumerate((first0, first1, first2, first3)):
        out[:, k * part : (k + 1) * part] = piece[:size, :]


def in_chip_order(where, pieces):
    odd, high = (where[1] & 1) == 1, (where[1] & 2) == 2
    ordered = []
    for s in range(4):
        low_pair = jnp.where(odd, pieces[s ^ 1], pieces[s])
        high_pair = jnp.where(odd, pieces[s ^ 3], pieces[s ^ 2])
        ordered.append(jnp.where(high, high_pair, low_pair))
    return ordered


def plane_sum(keep, came, far, k):
    return keep[0, k].astype(F32) + came[0, k].astype(F32) + far[k].astype(F32)


def sum_feed_kernel(
    keep0, came0, far0, keep1, came1, far1, out0, out1, out2, out3
):
    rows = keep0.shape[2]
    for k, out in enumerate((out0, out1, out2, out3)):
        out[:rows, :] = plane_sum(keep0, came0, far0, k).astype(BF16)
        out[rows:, :] = plane_sum(keep1, came1, far1, k).astype(BF16)


def sum_kernel(keep, came, far, out0, out1, out2, out3):
    for k, out in enumerate((out0, out1, out2, out3)):
        out[...] = plane_sum(keep, came, far, k).astype(BF16)


def unpack_feed_kernel(where, came0, came1, came2, came3, down_out, gate_out):
    rows = gate_out.shape[0]
    pieces = in_chip_order(where, [v[...] for v in (came0, came1, came2, came3)])
    for i, out in enumerate((down_out, gate_out)):
        span = slice(i * rows, (i + 1) * rows)
        out[...] = jnp.concatenate([v[span].astype(F32) for v in pieces], axis=1)


def unpack_up_kernel(where, came0, came1, came2, came3, up_out):
    pieces = in_chip_order(where, [v[...] for v in (came0, came1, came2, came3)])
    up_out[...] = jnp.concatenate([v.astype(F32) for v in pieces], axis=1)


def unpack_last_kernel(
    where, came0, came1, came2, came3, query_out, key_out, value_out, output_out, gain_out
):
    rows = query_out.shape[0]
    pieces = in_chip_order(where, [v[...] for v in (came0, came1, came2, came3)])
    two = query_out.shape[1] // len(pieces)
    size = two // 2
    pieces = [v.astype(F32) for v in pieces]
    for out, start, wide in (
        (query_out, 0, two), (key_out, two, size), (value_out, two + size, size),
        (output_out, 2 * two, two),
    ):
        out[...] = jnp.concatenate([v[:rows, start : start + wide] for v in pieces], axis=1)
    gain_out[...] = pieces[0][rows:] + pieces[1][rows:] + pieces[2][rows:] + pieces[3][rows:]


def gain_kernel(where, ours, came, attention_out, feed_out, query_out, key_out):
    lines = ours[...] + came[...]
    rows, head = attention_out.shape[1], query_out.shape[1]
    odd, high = (where[2] & 1) == 1, (where[2] & 2) == 2
    for out, i in ((attention_out, 0), (feed_out, 1)):
        parts = [lines[i : i + 1, p * rows : (p + 1) * rows] for p in range(4)]
        low = jnp.where(odd, parts[1], parts[0])
        out[...] = jnp.where(high, jnp.where(odd, parts[3], parts[2]), low)
    query_out[...] = lines[0:1, 4 * rows : 4 * rows + head]
    key_out[...] = lines[0:1, 4 * rows + head :]


def lane_is_first(size):
    return lax.broadcasted_iota(jnp.int32, (1, 2 * size), 1) < size


def head_scale(values, first):
    size = values.shape[1] // 2
    squares = values * values
    left = jnp.sum(jnp.where(first, squares, 0.0), axis=1, keepdims=True)
    right = jnp.sum(jnp.where(first, 0.0, squares), axis=1, keepdims=True)
    return lax.rsqrt(jnp.where(first, left, right) / size + EPSILON)


def turn(values, cosine, sine):
    width = values.shape[1]
    quarter = width // 4
    lane = lax.broadcasted_iota(jnp.int32, (1, width), 1)
    low = (lane & quarter) == 0
    other = jnp.where(
        low, pltpu.roll(values, width - quarter, 1), pltpu.roll(values, quarter, 1)
    )
    return values * cosine + other * sine


def root_and_input(mine, other):
    rows = jnp.concatenate([mine[...], other[...]], axis=0).astype(F32)
    mean = jnp.mean(rows * rows, axis=1, keepdims=True)
    return rows, lax.rsqrt(mean + EPSILON)


def gain_row(buffers, start, k):
    rows = buffers[k][start : start + 16, :].astype(F32)
    return rows[0:1] + rows[1:2] + rows[2:3]


def allowed_of(down, across):
    return (across[0:1, :] <= down[:, 0:1]) & (across[1:2, :] == down[:, 1:2])


def attend_kernel(
    mine, other, first0, first1, first2, first3, cosine, sine, gains, down, across,
    qkv_out, turned_out, context_out, log_out,
):
    buffers = (first0, first1, first2, first3)
    half, part = mine.shape[0], first0.shape[1]
    rows, root = root_and_input(mine, other)
    start = half + 16
    qkv = None
    for k, buffer in enumerate(buffers):
        block = rows[:, k * part : (k + 1) * part] * root * gain_row(buffers, half, k)
        term = matmul(block.astype(BF16), buffer[start:, :])
        qkv = term if qkv is None else qkv + term
    qkv_out[...] = qkv
    two = qkv.shape[1] // 2
    size = two // 2
    first = lane_is_first(size)
    query, pair = qkv[:, :two], qkv[:, two:]
    query_turned = turn(
        query * head_scale(query, first) * gains[0:1, :], cosine[...], sine[...]
    ).astype(BF16)
    key_turned = turn(pair * head_scale(pair, first) * gains[1:2, :], cosine[...], sine[...])
    pair_rounded = jnp.where(first, key_turned, pair).astype(BF16)
    turned_out[:, :two] = query_turned
    turned_out[:, two:] = pair_rounded
    key, value = pair_rounded[:, :size], pair_rounded[:, size:]
    allowed = allowed_of(down, across)
    contexts, logs = [], []
    for h in range(2):
        raw = matmul_nt(query_turned[:, h * size : (h + 1) * size], key)
        scores = jnp.where(allowed, raw * size ** (-0.5), NEGATIVE)
        top = jnp.max(scores, axis=1, keepdims=True)
        powers = jnp.exp(scores - top)
        sums = jnp.sum(powers, axis=1, keepdims=True)
        prob = (powers * (1.0 / sums)).astype(BF16)
        contexts.append(matmul(prob, value))
        logs.append(top + jnp.log(sums))
    context_out[...] = jnp.concatenate(contexts, axis=1).astype(BF16)
    log_out[...] = jnp.where(first, logs[0], logs[1])


def attend_back_kernel(
    where, mine, other, first0, first1, first2, first3, cosine, sine, gains, down, across,
    qkv_in, turned, context_in, logs, grad_mine, grad_other, out_weight,
    gain_in, one_mine, one_other, inner_out, mixed_send, mixed_keep, mixed,
):
    buffers = (first0, first1, first2, first3)
    half, part = mine.shape[0], first0.shape[1]
    two = context_in.shape[1]
    size = two // 2
    first = lane_is_first(size)
    upstream = jnp.concatenate([grad_mine[...], grad_other[...]], axis=0)
    context = context_in[...]
    context_grad = matmul_nt(upstream, out_weight[:two, :]).astype(BF16)
    key, value = turned[:, two : two + size], turned[:, two + size :]
    allowed = allowed_of(down, across)
    products = context_grad.astype(F32) * context.astype(F32)
    query_grads = []
    key_grad = value_grad = None
    for h in range(2):
        query = turned[:, h * size : (h + 1) * size]
        grad = context_grad[:, h * size : (h + 1) * size]
        raw = matmul_nt(query, key)
        scores = jnp.where(allowed, raw * size ** (-0.5), NEGATIVE)
        prob = jnp.exp(scores - logs[:, h * size : h * size + 1])
        delta = jnp.sum(
            jnp.where(first if h == 0 else jnp.logical_not(first), products, 0.0),
            axis=1,
            keepdims=True,
        )
        value_term = matmul_tn(prob.astype(BF16), grad)
        score_grad = (prob * (matmul_nt(grad, value) - delta) * size ** (-0.5)).astype(BF16)
        query_grads.append(matmul(score_grad, key))
        key_term = matmul_tn(score_grad, query)
        key_grad = key_term if h == 0 else key_grad + key_term
        value_grad = value_term if h == 0 else value_grad + value_term
    pieces, head_parts = [], []
    for i, grad in enumerate(
        (jnp.concatenate(query_grads, axis=1), jnp.concatenate([key_grad, value_grad], axis=1))
    ):
        normed = turn(grad, cosine[...], -sine[...])
        proj = qkv_in[:, i * two : (i + 1) * two]
        scale = head_scale(proj, first)
        hat = proj * scale
        weighted = normed * gains[i : i + 1, :]
        product = weighted * hat
        left = jnp.sum(jnp.where(first, product, 0.0), axis=1, keepdims=True)
        right = jnp.sum(jnp.where(first, 0.0, product), axis=1, keepdims=True)
        inner = jnp.where(first, left, right) / size
        result = scale * (weighted - hat * inner)
        pieces.append(result if i == 0 else jnp.where(first, result, grad))
        head_parts.append(jnp.sum(normed * hat, axis=0, keepdims=True))
    head_line = head_parts[0] + pltpu.roll(head_parts[0], size, 1)
    head_line = jnp.where(first, head_line, pltpu.roll(head_parts[1], size, 1))
    rows_here = mixed_send.shape[2] - 8
    line = lax.broadcasted_iota(jnp.int32, (8, part), 0)
    qkv_grad = jnp.concatenate(pieces, axis=1).astype(BF16)
    rows, root = root_and_input(mine, other)
    inner_sum = jnp.zeros((2 * half, 1), F32)
    for k, buffer in enumerate(buffers):
        span = slice(k * part, (k + 1) * part)
        gain = gain_row(buffers, half, k)
        hat = rows[:, span] * root
        grad = matmul_nt(qkv_grad, buffer[half + 16 :, :])
        product = grad * hat
        lines = jnp.where(line == 0, jnp.sum(product, axis=0, keepdims=True), 0.0)
        lines = jnp.where(line == 1, gain_in[:, span], lines).astype(BF16)
        inner_sum = inner_sum + jnp.sum(product * gain, axis=1, keepdims=True)
        one_mine[:, span] = grad[:half].astype(BF16)
        one_other[:, span] = grad[half:].astype(BF16)
        mixed[:, : 2 * two] = matmul_tn((hat * gain).astype(BF16), qkv_grad).astype(BF16)
        mixed[:, 2 * two :] = matmul_tn(upstream[:, span], context).astype(BF16)
        heads = jnp.broadcast_to(head_line, (8, two)).astype(BF16)
        if mixed_send.shape[0] == 2:
            deal(where, mixed, k, mixed_send, mixed_keep, rows_here)
            for out in (mixed_send, mixed_keep):
                for j in range(2):
                    out[j, k, rows_here:, : 2 * two] = lines
                    out[j, k, rows_here:, 2 * two :] = heads
        else:
            mixed_send[k, ...] = mixed[...]
            mixed_keep[k, :, : 2 * two] = lines
            mixed_keep[k, :, 2 * two :] = heads
    wide = jnp.broadcast_to(inner_sum / (part * len(buffers)), (2 * half, 128))
    inner_out[...] = jnp.transpose(wide)[:8, :]


def rope_tables(places, head_size):
    half_size = head_size // 2
    frequency = THETA ** (-(jnp.arange(half_size).astype(F32) * 2.0 / head_size))
    angles = places.astype(F32)[:, None] * frequency[None, :]
    return (jnp.cos(angles), jnp.sin(angles))


def body(
    block_input,
    segments,
    positions,
    attention_gain,
    query_weight,
    key_weight,
    value_weight,
    query_gain,
    key_gain,
    output_weight,
    feedforward_gain,
    gate_weight,
    up_weight,
    down_weight,
    cotangent,
):
    tokens = block_input.shape[0]
    part = block_input.shape[1]
    head = query_gain.shape[0]
    cols = lax.axis_size("col")
    planes = lax.axis_size("dp")
    width = part * cols
    half = tokens // 2
    row = lax.axis_index("row")
    plane = lax.axis_index("dp")

    def mine_first(values):
        return jnp.where(row == 0, values, jnp.roll(values, half, axis=0))

    def natural(values):
        return jnp.where(row == 0, values, jnp.roll(values, half, axis=0))

    q_size = query_weight.shape[1] // cols
    units = gate_weight.shape[1] // cols
    shapes = [((half + 16 + part, part), BF16)] * cols
    first_in = exchange(
        kernel_call(
            pack_one_kernel,
            shapes,
            block_input,
            query_weight,
            key_weight,
            value_weight,
            attention_gain.reshape(1, part),
            feedforward_gain.reshape(1, part),
            placed=True,
            fetch=4, room=60),
    )
    (input_mine,) = kernel_call(join_first_kernel, [((half, width), BF16)], *first_in, room=10)
    gain_parts = jnp.concatenate([v[half : half + 16] for v in first_in], axis=1).astype(F32)
    gain_one = gain_parts[0] + gain_parts[1] + gain_parts[2]
    input_other = flip(input_mine, "row", 1)
    gate_in = kernel_call(
        pack_gate_kernel,
        [((part, units), BF16)] * (cols + 1),
        gate_weight,
        up_weight,
        placed=True,
        fetch=2, room=12)
    near_parts = exchange(gate_in[:cols])
    far_parts = [gate_in[cols]] + [flip(v, "dp", 1) for v in near_parts[1:]]
    inner_size = output_weight.shape[0]
    two_out = kernel_call(
        pack_two_kernel,
        [((half + inner_size, part), BF16)] * cols,
        output_weight,
        cotangent,
        placed=True,
        fetch=2,
    )
    second_parts = exchange(two_out)
    three_out = kernel_call(
        pack_three_kernel,
        [((units, part), BF16)] * cols,
        down_weight,
        placed=True,
        fetch=1,
    )
    down_parts = exchange(three_out)

    group = q_size // head
    segment_ids = mine_first(segments)
    places = mine_first(positions)
    index = mine_first(jnp.arange(tokens))

    cosine, sine_part = rope_tables(places, head)
    cos_lanes = jnp.concatenate([cosine] * (2 * group), axis=1)
    sin_lanes = jnp.concatenate([-sine_part, sine_part] * group, axis=1)
    head_gains = jnp.stack([jnp.tile(query_gain, group), jnp.tile(key_gain, group)])
    down = jnp.stack([index, segment_ids], axis=1)
    across = jnp.stack([index, segment_ids])
    common = (
        input_mine,
        input_other,
        *first_in,
        cos_lanes,
        sin_lanes,
        head_gains,
        down,
        across,
    )
    qkv, turned, context, logs = kernel_call(
        attend_kernel,
        [
            ((tokens, 2 * q_size), F32),
            ((tokens, 2 * q_size), BF16),
            ((tokens, q_size), BF16),
            ((tokens, q_size), F32),
        ],
        *common, room=26)

    context_parts = spread(context)
    (context_near,) = kernel_call(join_kernel, [((tokens, inner_size), BF16)], *context_parts, room=10)
    context_far = flip(context_near, "row", 1)
    (second_in,) = kernel_call(join_kernel, [((inner_size, width), BF16)], *second_parts, room=10)
    second_far = flip(second_in, "row", 1)
    (cot_mine,) = kernel_call(join_first_kernel, [((half, width), BF16)], *second_parts, room=10)
    cot_other = flip(cot_mine, "row", 1)

    share = half // cols
    normed_two, first_block, first_share = kernel_call(
        project_kernel,
        [((tokens, width), BF16), ((half, part), F32), ((share, width), F32)],
        input_mine,
        input_other,
        context_near,
        context_far,
        second_in,
        second_far,
        *first_in,
        placed=True,
        scratch=[((half, width), F32)], room=24)
    gate_pre, up_pre, hidden = kernel_call(
        hidden_kernel,
        [((tokens, units), F32), ((tokens, units), F32), ((tokens, units), BF16)],
        normed_two,
        *near_parts,
        *far_parts,
        placed=True, room=24)
    rows = part // planes
    if planes == 4:
        down_dealt = kernel_call(
            down_grad_kernel,
            [((2, cols, rows, units), BF16)] * 2,
            cot_mine,
            cot_other,
            hidden,
            placed=True,
            scratch=[((part, units), BF16)], room=14)
    gate_grad, up_grad, two_mine, two_other = kernel_call(
        backward_kernel,
        [((tokens, units), BF16)] * 2 + [((half, width), BF16)] * 2,
        cot_mine,
        cot_other,
        gate_pre,
        up_pre,
        *down_parts,
        *near_parts,
        *far_parts,
        placed=True, room=30)

    two_came = flip(two_other, "row", 1)
    two_pieces = kernel_call(
        pack_tokens_kernel,
        [((share, width), BF16)] * cols,
        two_mine,
        two_came,
        placed=True,
        scratch=[((half, width), BF16)],
    )
    two_in = exchange(two_pieces)
    *first_pieces, feedforward_part = kernel_call(
        second_norm_kernel,
        [((share, width), BF16)] * cols + [((1, width), F32)],
        *two_in,
        first_share,
        cot_mine,
        *first_in,
        placed=True,
    )
    first_back = exchange(first_pieces)
    (first_half,) = kernel_call(
        join_tokens_kernel, [((half, width), BF16)], *first_back, placed=True
    )
    first_other = flip(first_half, "row", 1)

    def shifted(send, keep):
        came = flip(send, "dp", 1)
        rest = (keep[1].astype(F32) + came[1].astype(F32)).astype(BF16)
        return keep, came, flip(rest, "dp", 2)

    def scattered(split):
        return lax.psum_scatter(split, "dp", scatter_dimension=0, tiled=True)[0]

    if planes == 4:
        dealt = kernel_call(
            weight_grad_kernel,
            [((2, cols, rows, units), BF16)] * 4,
            normed_two,
            gate_grad,
            up_grad,
            placed=True,
            scratch=[((part, units), BF16)], room=20)
        dealt = list(down_dealt) + list(dealt)
        down_terms, gate_terms, up_terms = [
            shifted(dealt[2 * i], dealt[2 * i + 1])
            for i in range(3)
        ]
        feed_out = kernel_call(
            sum_feed_kernel,
            [((2 * rows, units), BF16)] * cols,
            *down_terms,
            *gate_terms,
            room=16,
        )
        up_out = kernel_call(
            sum_kernel, [((rows, units), BF16)] * cols, *up_terms, room=12
        )
    else:
        cot_all = jnp.concatenate([cot_mine, cot_other], axis=0)
        sums = [
            scattered(
                jnp.moveaxis(grad.astype(BF16).reshape(cols, planes, rows, units), 1, 0)
            )
            for grad in (
                matmul_tn(cot_all, hidden),
                matmul_tn(normed_two, gate_grad),
                matmul_tn(normed_two, up_grad),
            )
        ]
        feed_out = [jnp.concatenate([v[k] for v in sums[:2]], axis=0) for k in range(cols)]
        up_out = [sums[2][k] for k in range(cols)]
    feed_in = exchange(feed_out)
    down_share, gate_share = kernel_call(
        unpack_feed_kernel,
        [((rows, cols * units), F32)] * 2,
        *feed_in,
        placed=True,
        room=12,
    )

    up_in = exchange(up_out)
    (up_share,) = kernel_call(unpack_up_kernel, [((rows, cols * units), F32)], *up_in, placed=True)

    result_mine, result_other = kernel_call(
        result_kernel, [((half, width), BF16)] * 2, hidden, *down_parts, room=12)
    result_came = flip(result_other, "row", 1)
    result_pieces = kernel_call(
        pack_features_kernel, [((half, part), BF16)] * cols, result_mine, result_came
    )
    result_in = exchange(result_pieces)
    result_mine = (first_block + total(result_in)).astype(BF16)
    result_far = flip(result_mine, "row", 1)
    block_output = natural(jnp.concatenate([result_mine, result_far], axis=0))

    mixed_size = 3 * q_size
    if planes == 4:
        mixed_outs = [((2, cols, rows + 8, mixed_size), BF16)] * 2
    else:
        mixed_outs = [((cols, part, mixed_size), BF16), ((cols, 8, mixed_size), BF16)]
    one_mine, one_other, inner_part, mixed_first, mixed_second = kernel_call(
        attend_back_kernel,
        [((half, width), BF16), ((half, width), BF16), ((8, tokens), F32)] + mixed_outs,
        *common,
        qkv,
        turned,
        context,
        logs,
        first_half,
        first_other,
        second_in,
        feedforward_part,
        placed=True,
        scratch=[((part, mixed_size), BF16)], room=34)
    one_came = flip(one_other, "row", 1)
    inner_came = flip(inner_part[:, half:], "row", 1)
    one_pieces = kernel_call(
        pack_last_kernel,
        [((half + 16, part), BF16)] * cols,
        one_mine,
        one_came,
        inner_part,
        inner_came, room=10)
    one_in = exchange(one_pieces)
    one_grad = total([v[:half] for v in one_in])
    inner_one = jnp.sum(total([v[half:] for v in one_in])[:3], axis=0)[:, None]
    weighted_one = one_grad * gain_one[:part]
    own_input = input_mine.astype(F32)
    root_one = lax.rsqrt(jnp.mean(own_input * own_input, axis=1, keepdims=True) + EPSILON)
    normal_one = own_input[:, :part] * root_one
    input_mine_grad = first_half[:, :part].astype(F32) + root_one * (
        weighted_one - normal_one * inner_one
    )
    input_far_grad = flip(input_mine_grad, "row", 1)
    input_grad = natural(jnp.concatenate([input_mine_grad, input_far_grad], axis=0))

    if planes == 4:
        mixed_terms = shifted(mixed_first, mixed_second)
        last_out = kernel_call(sum_kernel, [((rows + 8, mixed_size), BF16)] * cols, *mixed_terms)
    else:
        lines = jnp.broadcast_to(mixed_second[:, None], (cols, planes, 8, mixed_size))
        blocks = mixed_first.reshape(cols, planes, rows, mixed_size)
        mixed_sum = scattered(jnp.moveaxis(jnp.concatenate([blocks, lines], axis=2), 1, 0))
        last_out = [mixed_sum[k] for k in range(cols)]
    last_in = exchange(last_out)
    query_share, key_share, value_share, output_share, gain_sums = kernel_call(
        unpack_last_kernel,
        [
            ((rows, cols * q_size), F32),
            ((rows, cols * head), F32),
            ((rows, cols * head), F32),
            ((rows, cols * q_size), F32),
            ((8, mixed_size), F32),
        ],
        *last_in,
        placed=True,
    )
    gain_came = flip(gain_sums, "row", 1)
    if planes == 4:
        attention_share, feedforward_share, query_gain_grad, key_gain_grad = [
            v.reshape(-1)
            for v in kernel_call(
                gain_kernel,
                [((1, rows), F32), ((1, rows), F32), ((1, head), F32), ((1, head), F32)],
                gain_sums,
                gain_came,
                placed=True,
            )
        ]
    else:
        gain_sums = gain_sums + gain_came
        attention_share = lax.dynamic_slice_in_dim(gain_sums[0], plane * rows, rows, 0)
        feedforward_share = lax.dynamic_slice_in_dim(gain_sums[1], plane * rows, rows, 0)
        query_gain_grad = gain_sums[0, 2 * q_size : 2 * q_size + head]
        key_gain_grad = gain_sums[0, 2 * q_size + head :]
    return (
        block_output,
        input_grad,
        attention_share,
        query_share,
        key_share,
        value_share,
        query_gain_grad,
        key_gain_grad,
        output_share.T,
        feedforward_share,
        gate_share,
        up_share,
        down_share.T,
    )


def solution(mesh):
    placed = (
        P("dp", "col"),
        P("dp"),
        P("dp"),
        P("col"),
        P("col", "row"),
        P("col", "row"),
        P("col", "row"),
        P(),
        P(),
        P("row", "col"),
        P("col"),
        P("col", "row"),
        P("col", "row"),
        P("row", "col"),
        P("dp", "col"),
    )


    return jax.shard_map(
        body,
        mesh=mesh,
        in_specs=placed,
        out_specs=(
            P("dp", "col"),
            P("dp", "col"),
            P(("col", "dp")),
            P(("col", "dp"), "row"),
            P(("col", "dp"), "row"),
            P(("col", "dp"), "row"),
            P(),
            P(),
            P("row", ("col", "dp")),
            P(("col", "dp")),
            P(("col", "dp"), "row"),
            P(("col", "dp"), "row"),
            P("row", ("col", "dp")),
        ),
        check_vma=False,
    )
```

```python
import jax
import jax.numpy as jnp
from jax import lax
from jax.experimental import pallas as pl
from jax.experimental.pallas import tpu as pltpu
from jax.sharding import PartitionSpec as P


EPSILON = 1e-05
THETA = 1000000.0
NEGATIVE = -1e30


F32 = jnp.float32
BF16 = jnp.bfloat16


def matmul(left, right):
    return jnp.dot(left, right, preferred_element_type=F32)


def matmul_nt(left, right):
    return lax.dot_general(left, right, (((1,), (1,)), ((), ())), preferred_element_type=F32)


def matmul_tn(left, right):
    return lax.dot_general(left, right, (((0,), (0,)), ((), ())), preferred_element_type=F32)


def flip(values, axis, distance):
    size = lax.axis_size(axis)
    return lax.ppermute(values, axis, [(i, i ^ distance) for i in range(size)])


def spread(values):
    return [values] + [flip(values, "col", k) for k in range(1, lax.axis_size("col"))]


def exchange(pieces):
    return [pieces[0]] + [flip(pieces[k], "col", k) for k in range(1, len(pieces))]


def total(parts):
    result = parts[0].astype(F32)
    for part in parts[1:]:
        result = result + part.astype(F32)
    return result


def kernel_call(kernel, outs, *args, placed=False, scratch=(), fetch=0, room=8):
    specs = [pl.BlockSpec(memory_space=pltpu.HBM)] * fetch
    specs = specs + [pl.BlockSpec(memory_space=pltpu.VMEM)] * (len(args) - fetch)
    scratch_shapes = [pltpu.VMEM(shape, dtype) for shape, dtype in scratch]
    if fetch:
        scratch_shapes = [pltpu.VMEM(v.shape, v.dtype) for v in args[:fetch]] + scratch_shapes
        scratch_shapes.append(pltpu.SemaphoreType.DMA((fetch,)))
    if placed:
        plain = kernel

        def kernel(*refs):
            plain(tuple(lax.axis_index(axis) for axis in ("row", "col", "dp")), *refs)

    return pl.pallas_call(
        kernel,
        out_shape=[jax.ShapeDtypeStruct(shape, dtype) for shape, dtype in outs],
        in_specs=specs,
        out_specs=[pl.BlockSpec(memory_space=pltpu.VMEM)] * len(outs),
        scratch_shapes=scratch_shapes,
        compiler_params=pltpu.CompilerParams(vmem_limit_bytes=room * 1024 * 1024),
    )(*args)


def fetched(sources, targets, semaphores):
    copies = [
        pltpu.make_async_copy(source, target, semaphores.at[i])
        for i, (source, target) in enumerate(zip(sources, targets))
    ]
    for copy in copies:
        copy.start()
    for copy in copies:
        copy.wait()


def pack_one_kernel(
    where, x_in, query_in, key_in, value_in, gain_first, gain_second,
    out0, out1, out2, out3, x, query, key, value, semaphores,
):
    fetched((x_in, query_in, key_in, value_in), (x, query, key, value), semaphores)
    outs = (out0, out1, out2, out3)
    row, col = where[0], where[1]
    half = x.shape[0] // 2
    cols = len(outs)
    q_size, kv_size = query.shape[1] // cols, key.shape[1] // cols
    line = lax.broadcasted_iota(jnp.int32, (16, x.shape[1]), 0)
    rows = jnp.zeros((16, x.shape[1]), F32)
    for g, gain in enumerate((gain_first, gain_second)):
        rest = gain[...]
        for p in range(3):
            part = rest.astype(BF16).astype(F32)
            rows = jnp.where(line == 3 * g + p, part, rows)
            rest = rest - part
    mine = x[pl.ds(pl.multiple_of(row * half, half), half), :]
    for k, out in enumerate(outs):
        block = col ^ k
        out[:half, :] = mine
        out[half : half + 16, :] = rows.astype(BF16)
        out[half + 16 :, :q_size] = query[:, pl.ds(pl.multiple_of(block * q_size, q_size), q_size)]
        pair = pl.multiple_of((block >> 1) * (2 * kv_size), 2 * kv_size)
        odd = (block & 1) == 1
        both = []
        for weight in (key, value):
            two = weight[:, pl.ds(pair, 2 * kv_size)]
            both.append(jnp.where(odd, two[:, kv_size:], two[:, :kv_size]))
        out[half + 16 :, q_size:] = jnp.concatenate(both, axis=1)


def pack_two_kernel(where, weight_in, out0, out1, out2, out3, weight, semaphores):
    fetched((weight_in,), (weight,), semaphores)
    outs = (out0, out1, out2, out3)
    size = weight.shape[0] // len(outs)
    for k, out in enumerate(outs):
        for j in range(len(outs)):
            source = pl.multiple_of((where[1] ^ (k ^ j)) * size, size)
            out[j * size : (j + 1) * size, :] = weight[pl.ds(source, size), :]


def pack_three_kernel(where, down_in, out0, out1, out2, out3, down, semaphores):
    fetched((down_in,), (down,), semaphores)
    outs = (out0, out1, out2, out3)
    size = down.shape[0] // len(outs)
    for k, out in enumerate(outs):
        out[...] = down[pl.ds(pl.multiple_of((where[1] ^ k) * size, size), size), :]


def pack_gate_kernel(
    where, gate_in, up_in, out0, out1, out2, out3, out4, gate, up, semaphores
):
    fetched((gate_in, up_in), (gate, up), semaphores)
    outs = (out0, out1, out2, out3, out4)
    col, odd_plane = where[1], (where[2] & 1) == 1
    cols = len(outs) - 1
    size = gate.shape[1] // cols

    def piece(weight, block):
        two = weight[:, pl.ds(pl.multiple_of((block >> 1) * (2 * size), 2 * size), 2 * size)]
        return jnp.where((block & 1) == 1, two[:, size:], two[:, :size])

    @pl.when(jnp.logical_not(odd_plane))
    def _():
        for k in range(cols):
            outs[k][...] = piece(gate, col ^ k)
        outs[cols][...] = piece(up, col)

    @pl.when(odd_plane)
    def _():
        for k in range(cols):
            outs[k][...] = piece(up, col ^ k)
        outs[cols][...] = piece(gate, col)


def join_kernel(first0, first1, first2, first3, out):
    part, size = first0.shape[1], out.shape[0]
    for k, piece in enumerate((first0, first1, first2, first3)):
        out[:, k * part : (k + 1) * part] = piece[piece.shape[0] - size :, :]


def project_kernel(
    where, mine, other, context_near, context_far, joined, joined_far,
    first0, first1, first2, first3, normed_out, own_out, share_out, sum_scratch,
):
    buffers = (first0, first1, first2, first3)
    half, part = mine.shape[0], first0.shape[1]
    share = share_out.shape[0]
    top = mine[...].astype(F32) + matmul(context_near[:half, :], joined[...])
    top = top + matmul(context_far[half:, :], joined_far[...])
    low = other[...].astype(F32) + matmul(context_near[half:, :], joined[...])
    low = low + matmul(context_far[:half, :], joined_far[...])
    sum_scratch[...] = top
    own_out[...] = top[:, :part]
    share_out[...] = sum_scratch[pl.ds(pl.multiple_of(where[1] * share, share), share), :]
    gain = jnp.concatenate([gain_row(buffers, half + 3, k) for k in range(len(buffers))], axis=1)
    for i, rows in enumerate((top, low)):
        root = lax.rsqrt(jnp.mean(rows * rows, axis=1, keepdims=True) + EPSILON)
        normed_out[i * half : (i + 1) * half, :] = (rows * root * gain).astype(BF16)


def hidden_kernel(
    where, normed, near0, near1, near2, near3, far0, far1, far2, far3,
    gate_out, up_out, hidden_out,
):
    part = near0.shape[0]
    first_pre = second_pre = None
    for k, (near, far) in enumerate(
        ((near0, far0), (near1, far1), (near2, far2), (near3, far3))
    ):
        block = normed[:, k * part : (k + 1) * part]
        one, two = matmul(block, near[...]), matmul(block, far[...])
        first_pre = one if k == 0 else first_pre + one
        second_pre = two if k == 0 else second_pre + two
    even = (where[2] & 1) == 0
    gate_pre = jnp.where(even, first_pre, second_pre)
    up_pre = jnp.where(even, second_pre, first_pre)
    gate_out[...] = gate_pre
    up_out[...] = up_pre
    hidden_out[...] = (gate_pre * (1.0 / (1.0 + jnp.exp(-gate_pre))) * up_pre).astype(BF16)


def backward_kernel(
    where, cot_mine, cot_other, gate_in, up_in, down0, down1, down2, down3,
    near0, near1, near2, near3, far0, far1, far2, far3,
    gate_grad_out, up_grad_out, mine_out, other_out,
):
    half, part = mine_out.shape[0], near0.shape[0]
    size = gate_in.shape[1]
    parts = []
    for rows in (cot_mine, cot_other):
        grad = None
        for k, down in enumerate((down0, down1, down2, down3)):
            term = matmul_nt(rows[:, k * part : (k + 1) * part], down[:size, :])
            grad = term if k == 0 else grad + term
        parts.append(grad)
    hidden_grad = jnp.concatenate(parts, axis=0)
    gate_pre, up_pre = gate_in[...], up_in[...]
    sigmoid_gate = 1.0 / (1.0 + jnp.exp(-gate_pre))
    gate_grad = (
        hidden_grad * up_pre * sigmoid_gate * (1.0 + gate_pre * (1.0 - sigmoid_gate))
    ).astype(BF16)
    up_grad = (hidden_grad * (gate_pre * sigmoid_gate)).astype(BF16)
    gate_grad_out[...] = gate_grad
    up_grad_out[...] = up_grad
    even = (where[2] & 1) == 0
    near_grad = jnp.where(even, gate_grad, up_grad)
    far_grad = jnp.where(even, up_grad, gate_grad)
    for k, (near, far) in enumerate(
        ((near0, far0), (near1, far1), (near2, far2), (near3, far3))
    ):
        block = matmul_nt(near_grad, near[...]) + matmul_nt(far_grad, far[...])
        mine_out[:, k * part : (k + 1) * part] = block[:half].astype(BF16)
        other_out[:, k * part : (k + 1) * part] = block[half:].astype(BF16)


def result_kernel(hidden, down0, down1, down2, down3, mine_out, other_out):
    half, part = mine_out.shape[0], down0.shape[1]
    for k, down in enumerate((down0, down1, down2, down3)):
        block = matmul(hidden[...], down[: hidden.shape[1], :])
        mine_out[:, k * part : (k + 1) * part] = block[:half].astype(BF16)
        other_out[:, k * part : (k + 1) * part] = block[half:].astype(BF16)


def deal(where, scratch, k, send, keep, rows):
    for j in range(2):
        for out, m in ((send, 1 + 2 * j), (keep, 2 * j)):
            start = pl.multiple_of((where[2] ^ m) * rows, rows)
            out[j, k, :rows, :] = scratch[pl.ds(start, rows), :]


def down_grad_kernel(where, cot_mine, cot_other, hidden, send, keep, scratch):
    half = hidden.shape[0] // 2
    cols, rows = send.shape[1], send.shape[2]
    part = cot_mine.shape[1] // cols
    for k in range(cols):
        span = slice(k * part, (k + 1) * part)
        grad = matmul_tn(cot_mine[:, span], hidden[:half, :])
        grad = grad + matmul_tn(cot_other[:, span], hidden[half:, :])
        scratch[...] = grad.astype(BF16)
        deal(where, scratch, k, send, keep, rows)


def weight_grad_kernel(
    where, normed, gate_grad, up_grad, gate_send, gate_keep, up_send, up_keep, scratch
):
    cols, rows = gate_send.shape[1], gate_send.shape[2]
    part = normed.shape[1] // cols
    for upstream, send, keep in ((gate_grad, gate_send, gate_keep), (up_grad, up_send, up_keep)):
        for k in range(cols):
            span = slice(k * part, (k + 1) * part)
            scratch[...] = matmul_tn(normed[:, span], upstream[...]).astype(BF16)
            deal(where, scratch, k, send, keep, rows)


def pack_tokens_kernel(where, ours, came, out0, out1, out2, out3, scratch):
    outs = (out0, out1, out2, out3)
    share, part = out0.shape[0], out0.shape[1] // len(outs)
    scratch[...] = (ours[...].astype(F32) + came[...].astype(F32)).astype(BF16)
    for k, out in enumerate(outs):
        rows = pl.ds(pl.multiple_of((where[1] ^ k) * share, share), share)
        for j in range(len(outs)):
            source = k ^ j
            out[:, j * part : (j + 1) * part] = scratch[rows, source * part : (source + 1) * part]


def second_norm_kernel(
    where, came0, came1, came2, came3, sums, cot_mine, first0, first1, first2, first3,
    out0, out1, out2, out3, gain_out,
):
    buffers = (first0, first1, first2, first3)
    outs = (out0, out1, out2, out3)
    share, part = out0.shape[0], out0.shape[1] // len(outs)
    half = share * len(outs)
    grad = came0[...].astype(F32) + came1[...].astype(F32)
    grad = grad + came2[...].astype(F32) + came3[...].astype(F32)
    gain = jnp.concatenate([gain_row(buffers, half + 3, k) for k in range(len(buffers))], axis=1)
    rows = sums[...]
    root = lax.rsqrt(jnp.mean(rows * rows, axis=1, keepdims=True) + EPSILON)
    normal = rows * root
    weighted = grad * gain
    gain_out[...] = jnp.sum(grad * normal, axis=0, keepdims=True)
    inner = jnp.mean(weighted * normal, axis=1, keepdims=True)
    cot = cot_mine[pl.ds(pl.multiple_of(where[1] * share, share), share), :].astype(F32)
    first = (cot + root * (weighted - normal * inner)).astype(BF16)
    for k, out in enumerate(outs):
        for j in range(len(outs)):
            source = k ^ j
            out[:, j * part : (j + 1) * part] = first[:, source * part : (source + 1) * part]


def join_tokens_kernel(where, came0, came1, came2, came3, out):
    share = came0.shape[0]
    for k, came in enumerate((came0, came1, came2, came3)):
        out[pl.ds(pl.multiple_of((where[1] ^ k) * share, share), share), :] = came[...]


def pack_features_kernel(ours, came, out0, out1, out2, out3):
    part = out0.shape[1]
    for k, out in enumerate((out0, out1, out2, out3)):
        span = slice(k * part, (k + 1) * part)
        out[...] = (ours[:, span].astype(F32) + came[:, span].astype(F32)).astype(BF16)


def pack_last_kernel(ours, came, inner, inner_came, out0, out1, out2, out3):
    half, part = ours.shape[0], out0.shape[1]
    line = lax.broadcasted_iota(jnp.int32, (16, part), 0)
    rows = jnp.zeros((16, part), F32)
    rest = inner[0:1, :half] + inner_came[0:1, :]
    for p in range(3):
        piece = rest.astype(BF16).astype(F32)
        rows = jnp.where(line == p, piece, rows)
        rest = rest - piece
    for k, out in enumerate((out0, out1, out2, out3)):
        span = slice(k * part, (k + 1) * part)
        out[:half, :] = (ours[:, span].astype(F32) + came[:, span].astype(F32)).astype(BF16)
        out[half:, :] = rows.astype(BF16)


def join_first_kernel(first0, first1, first2, first3, out):
    part, size = first0.shape[1], out.shape[0]
    for k, piece in enumerate((first0, first1, first2, first3)):
        out[:, k * part : (k + 1) * part] = piece[:size, :]


def in_chip_order(where, pieces):
    odd, high = (where[1] & 1) == 1, (where[1] & 2) == 2
    ordered = []
    for s in range(4):
        low_pair = jnp.where(odd, pieces[s ^ 1], pieces[s])
        high_pair = jnp.where(odd, pieces[s ^ 3], pieces[s ^ 2])
        ordered.append(jnp.where(high, high_pair, low_pair))
    return ordered


def plane_sum(keep, came, far, k):
    return keep[0, k].astype(F32) + came[0, k].astype(F32) + far[k].astype(F32)


def sum_feed_kernel(
    keep0, came0, far0, keep1, came1, far1, out0, out1, out2, out3
):
    rows = keep0.shape[2]
    for k, out in enumerate((out0, out1, out2, out3)):
        out[:rows, :] = plane_sum(keep0, came0, far0, k).astype(BF16)
        out[rows:, :] = plane_sum(keep1, came1, far1, k).astype(BF16)


def sum_kernel(keep, came, far, out0, out1, out2, out3):
    for k, out in enumerate((out0, out1, out2, out3)):
        out[...] = plane_sum(keep, came, far, k).astype(BF16)


def unpack_feed_kernel(where, came0, came1, came2, came3, down_out, gate_out):
    rows = gate_out.shape[0]
    pieces = in_chip_order(where, [v[...] for v in (came0, came1, came2, came3)])
    for i, out in enumerate((down_out, gate_out)):
        span = slice(i * rows, (i + 1) * rows)
        out[...] = jnp.concatenate([v[span].astype(F32) for v in pieces], axis=1)


def unpack_up_kernel(where, came0, came1, came2, came3, up_out):
    pieces = in_chip_order(where, [v[...] for v in (came0, came1, came2, came3)])
    up_out[...] = jnp.concatenate([v.astype(F32) for v in pieces], axis=1)


def unpack_last_kernel(
    where, came0, came1, came2, came3, query_out, key_out, value_out, output_out, gain_out
):
    rows = query_out.shape[0]
    pieces = in_chip_order(where, [v[...] for v in (came0, came1, came2, came3)])
    two = query_out.shape[1] // len(pieces)
    size = two // 2
    pieces = [v.astype(F32) for v in pieces]
    for out, start, wide in (
        (query_out, 0, two), (key_out, two, size), (value_out, two + size, size),
        (output_out, 2 * two, two),
    ):
        out[...] = jnp.concatenate([v[:rows, start : start + wide] for v in pieces], axis=1)
    gain_out[...] = pieces[0][rows:] + pieces[1][rows:] + pieces[2][rows:] + pieces[3][rows:]


def gain_kernel(where, ours, came, attention_out, feed_out, query_out, key_out):
    lines = ours[...] + came[...]
    rows, head = attention_out.shape[1], query_out.shape[1]
    odd, high = (where[2] & 1) == 1, (where[2] & 2) == 2
    for out, i in ((attention_out, 0), (feed_out, 1)):
        parts = [lines[i : i + 1, p * rows : (p + 1) * rows] for p in range(4)]
        low = jnp.where(odd, parts[1], parts[0])
        out[...] = jnp.where(high, jnp.where(odd, parts[3], parts[2]), low)
    query_out[...] = lines[0:1, 4 * rows : 4 * rows + head]
    key_out[...] = lines[0:1, 4 * rows + head :]


def lane_is_first(size):
    return lax.broadcasted_iota(jnp.int32, (1, 2 * size), 1) < size


def head_scale(values, first):
    size = values.shape[1] // 2
    squares = values * values
    left = jnp.sum(jnp.where(first, squares, 0.0), axis=1, keepdims=True)
    right = jnp.sum(jnp.where(first, 0.0, squares), axis=1, keepdims=True)
    return lax.rsqrt(jnp.where(first, left, right) / size + EPSILON)


def turn(values, cosine, sine):
    width = values.shape[1]
    quarter = width // 4
    lane = lax.broadcasted_iota(jnp.int32, (1, width), 1)
    low = (lane & quarter) == 0
    other = jnp.where(
        low, pltpu.roll(values, width - quarter, 1), pltpu.roll(values, quarter, 1)
    )
    return values * cosine + other * sine


def root_and_input(mine, other):
    rows = jnp.concatenate([mine[...], other[...]], axis=0).astype(F32)
    mean = jnp.mean(rows * rows, axis=1, keepdims=True)
    return rows, lax.rsqrt(mean + EPSILON)


def gain_row(buffers, start, k):
    rows = buffers[k][start : start + 16, :].astype(F32)
    return rows[0:1] + rows[1:2] + rows[2:3]


def allowed_of(down, across):
    return (across[0:1, :] <= down[:, 0:1]) & (across[1:2, :] == down[:, 1:2])


def attend_kernel(
    mine, other, first0, first1, first2, first3, cosine, sine, gains, down, across,
    qkv_out, turned_out, context_out, log_out,
):
    buffers = (first0, first1, first2, first3)
    half, part = mine.shape[0], first0.shape[1]
    rows, root = root_and_input(mine, other)
    start = half + 16
    qkv = None
    for k, buffer in enumerate(buffers):
        block = rows[:, k * part : (k + 1) * part] * root * gain_row(buffers, half, k)
        term = matmul(block.astype(BF16), buffer[start:, :])
        qkv = term if qkv is None else qkv + term
    qkv_out[...] = qkv
    two = qkv.shape[1] // 2
    size = two // 2
    first = lane_is_first(size)
    query, pair = qkv[:, :two], qkv[:, two:]
    query_turned = turn(
        query * head_scale(query, first) * gains[0:1, :], cosine[...], sine[...]
    ).astype(BF16)
    key_turned = turn(pair * head_scale(pair, first) * gains[1:2, :], cosine[...], sine[...])
    pair_rounded = jnp.where(first, key_turned, pair).astype(BF16)
    turned_out[:, :two] = query_turned
    turned_out[:, two:] = pair_rounded
    key, value = pair_rounded[:, :size], pair_rounded[:, size:]
    allowed = allowed_of(down, across)
    contexts, logs = [], []
    for h in range(2):
        raw = matmul_nt(query_turned[:, h * size : (h + 1) * size], key)
        scores = jnp.where(allowed, raw * size ** (-0.5), NEGATIVE)
        top = jnp.max(scores, axis=1, keepdims=True)
        powers = jnp.exp(scores - top)
        sums = jnp.sum(powers, axis=1, keepdims=True)
        prob = (powers * (1.0 / sums)).astype(BF16)
        contexts.append(matmul(prob, value))
        logs.append(top + jnp.log(sums))
    context_out[...] = jnp.concatenate(contexts, axis=1).astype(BF16)
    log_out[...] = jnp.where(first, logs[0], logs[1])


def attend_back_kernel(
    where, mine, other, first0, first1, first2, first3, cosine, sine, gains, down, across,
    qkv_in, turned, context_in, logs, grad_mine, grad_other, out_weight,
    gain_in, one_mine, one_other, inner_out, mixed_send, mixed_keep, mixed,
):
    buffers = (first0, first1, first2, first3)
    half, part = mine.shape[0], first0.shape[1]
    two = context_in.shape[1]
    size = two // 2
    first = lane_is_first(size)
    upstream = jnp.concatenate([grad_mine[...], grad_other[...]], axis=0)
    context = context_in[...]
    context_grad = matmul_nt(upstream, out_weight[:two, :]).astype(BF16)
    key, value = turned[:, two : two + size], turned[:, two + size :]
    allowed = allowed_of(down, across)
    products = context_grad.astype(F32) * context.astype(F32)
    query_grads = []
    key_grad = value_grad = None
    for h in range(2):
        query = turned[:, h * size : (h + 1) * size]
        grad = context_grad[:, h * size : (h + 1) * size]
        raw = matmul_nt(query, key)
        scores = jnp.where(allowed, raw * size ** (-0.5), NEGATIVE)
        prob = jnp.exp(scores - logs[:, h * size : h * size + 1])
        delta = jnp.sum(
            jnp.where(first if h == 0 else jnp.logical_not(first), products, 0.0),
            axis=1,
            keepdims=True,
        )
        value_term = matmul_tn(prob.astype(BF16), grad)
        score_grad = (prob * (matmul_nt(grad, value) - delta) * size ** (-0.5)).astype(BF16)
        query_grads.append(matmul(score_grad, key))
        key_term = matmul_tn(score_grad, query)
        key_grad = key_term if h == 0 else key_grad + key_term
        value_grad = value_term if h == 0 else value_grad + value_term
    pieces, head_parts = [], []
    for i, grad in enumerate(
        (jnp.concatenate(query_grads, axis=1), jnp.concatenate([key_grad, value_grad], axis=1))
    ):
        normed = turn(grad, cosine[...], -sine[...])
        proj = qkv_in[:, i * two : (i + 1) * two]
        scale = head_scale(proj, first)
        hat = proj * scale
        weighted = normed * gains[i : i + 1, :]
        product = weighted * hat
        left = jnp.sum(jnp.where(first, product, 0.0), axis=1, keepdims=True)
        right = jnp.sum(jnp.where(first, 0.0, product), axis=1, keepdims=True)
        inner = jnp.where(first, left, right) / size
        result = scale * (weighted - hat * inner)
        pieces.append(result if i == 0 else jnp.where(first, result, grad))
        head_parts.append(jnp.sum(normed * hat, axis=0, keepdims=True))
    head_line = head_parts[0] + pltpu.roll(head_parts[0], size, 1)
    head_line = jnp.where(first, head_line, pltpu.roll(head_parts[1], size, 1))
    rows_here = mixed_send.shape[2] - 8
    line = lax.broadcasted_iota(jnp.int32, (8, part), 0)
    qkv_grad = jnp.concatenate(pieces, axis=1).astype(BF16)
    rows, root = root_and_input(mine, other)
    inner_sum = jnp.zeros((2 * half, 1), F32)
    for k, buffer in enumerate(buffers):
        span = slice(k * part, (k + 1) * part)
        gain = gain_row(buffers, half, k)
        hat = rows[:, span] * root
        grad = matmul_nt(qkv_grad, buffer[half + 16 :, :])
        product = grad * hat
        lines = jnp.where(line == 0, jnp.sum(product, axis=0, keepdims=True), 0.0)
        lines = jnp.where(line == 1, gain_in[:, span], lines).astype(BF16)
        inner_sum = inner_sum + jnp.sum(product * gain, axis=1, keepdims=True)
        one_mine[:, span] = grad[:half].astype(BF16)
        one_other[:, span] = grad[half:].astype(BF16)
        mixed[:, : 2 * two] = matmul_tn((hat * gain).astype(BF16), qkv_grad).astype(BF16)
        mixed[:, 2 * two :] = matmul_tn(upstream[:, span], context).astype(BF16)
        heads = jnp.broadcast_to(head_line, (8, two)).astype(BF16)
        if mixed_send.shape[0] == 2:
            deal(where, mixed, k, mixed_send, mixed_keep, rows_here)
            for out in (mixed_send, mixed_keep):
                for j in range(2):
                    out[j, k, rows_here:, : 2 * two] = lines
                    out[j, k, rows_here:, 2 * two :] = heads
        else:
            mixed_send[k, ...] = mixed[...]
            mixed_keep[k, :, : 2 * two] = lines
            mixed_keep[k, :, 2 * two :] = heads
    wide = jnp.broadcast_to(inner_sum / (part * len(buffers)), (2 * half, 128))
    inner_out[...] = jnp.transpose(wide)[:8, :]


def rope_tables(places, head_size):
    half_size = head_size // 2
    frequency = THETA ** (-(jnp.arange(half_size).astype(F32) * 2.0 / head_size))
    angles = places.astype(F32)[:, None] * frequency[None, :]
    return (jnp.cos(angles), jnp.sin(angles))


def body(
    block_input,
    segments,
    positions,
    attention_gain,
    query_weight,
    key_weight,
    value_weight,
    query_gain,
    key_gain,
    output_weight,
    feedforward_gain,
    gate_weight,
    up_weight,
    down_weight,
    cotangent,
):
    tokens = block_input.shape[0]
    part = block_input.shape[1]
    head = query_gain.shape[0]
    cols = lax.axis_size("col")
    planes = lax.axis_size("dp")
    width = part * cols
    half = tokens // 2
    row = lax.axis_index("row")
    plane = lax.axis_index("dp")

    def mine_first(values):
        return jnp.where(row == 0, values, jnp.roll(values, half, axis=0))

    def natural(values):
        return jnp.where(row == 0, values, jnp.roll(values, half, axis=0))

    q_size = query_weight.shape[1] // cols
    units = gate_weight.shape[1] // cols
    shapes = [((half + 16 + part, part), BF16)] * cols
    first_in = exchange(
        kernel_call(
            pack_one_kernel,
            shapes,
            block_input,
            query_weight,
            key_weight,
            value_weight,
            attention_gain.reshape(1, part),
            feedforward_gain.reshape(1, part),
            placed=True,
            fetch=4, room=60),
    )
    (input_mine,) = kernel_call(join_first_kernel, [((half, width), BF16)], *first_in, room=10)
    gain_parts = jnp.concatenate([v[half : half + 16] for v in first_in], axis=1).astype(F32)
    gain_one = gain_parts[0] + gain_parts[1] + gain_parts[2]
    input_other = flip(input_mine, "row", 1)
    gate_in = kernel_call(
        pack_gate_kernel,
        [((part, units), BF16)] * (cols + 1),
        gate_weight,
        up_weight,
        placed=True,
        fetch=2, room=12)
    near_parts = exchange(gate_in[:cols])
    far_parts = [gate_in[cols]] + [flip(v, "dp", 1) for v in near_parts[1:]]
    inner_size = output_weight.shape[0]
    two_out = kernel_call(
        pack_two_kernel,
        [((inner_size, part), BF16)] * cols,
        output_weight,
        placed=True,
        fetch=1,
    )
    second_parts = exchange(two_out)
    cot_parts = spread(lax.dynamic_slice_in_dim(cotangent, row * half, half, 0))
    three_out = kernel_call(
        pack_three_kernel,
        [((units, part), BF16)] * cols,
        down_weight,
        placed=True,
        fetch=1,
    )
    down_parts = exchange(three_out)

    group = q_size // head
    segment_ids = mine_first(segments)
    places = mine_first(positions)
    index = mine_first(jnp.arange(tokens))

    cosine, sine_part = rope_tables(places, head)
    cos_lanes = jnp.concatenate([cosine] * (2 * group), axis=1)
    sin_lanes = jnp.concatenate([-sine_part, sine_part] * group, axis=1)
    head_gains = jnp.stack([jnp.tile(query_gain, group), jnp.tile(key_gain, group)])
    down = jnp.stack([index, segment_ids], axis=1)
    across = jnp.stack([index, segment_ids])
    common = (
        input_mine,
        input_other,
        *first_in,
        cos_lanes,
        sin_lanes,
        head_gains,
        down,
        across,
    )
    qkv, turned, context, logs = kernel_call(
        attend_kernel,
        [
            ((tokens, 2 * q_size), F32),
            ((tokens, 2 * q_size), BF16),
            ((tokens, q_size), BF16),
            ((tokens, q_size), F32),
        ],
        *common, room=26)

    context_parts = spread(context)
    (context_near,) = kernel_call(join_kernel, [((tokens, inner_size), BF16)], *context_parts, room=10)
    context_far = flip(context_near, "row", 1)
    (second_in,) = kernel_call(join_kernel, [((inner_size, width), BF16)], *second_parts, room=10)
    second_far = flip(second_in, "row", 1)
    (cot_mine,) = kernel_call(join_first_kernel, [((half, width), BF16)], *cot_parts, room=10)
    cot_other = flip(cot_mine, "row", 1)

    share = half // cols
    normed_two, first_block, first_share = kernel_call(
        project_kernel,
        [((tokens, width), BF16), ((half, part), F32), ((share, width), F32)],
        input_mine,
        input_other,
        context_near,
        context_far,
        second_in,
        second_far,
        *first_in,
        placed=True,
        scratch=[((half, width), F32)], room=24)
    gate_pre, up_pre, hidden = kernel_call(
        hidden_kernel,
        [((tokens, units), F32), ((tokens, units), F32), ((tokens, units), BF16)],
        normed_two,
        *near_parts,
        *far_parts,
        placed=True, room=24)
    rows = part // planes
    if planes == 4:
        down_dealt = kernel_call(
            down_grad_kernel,
            [((2, cols, rows, units), BF16)] * 2,
            cot_mine,
            cot_other,
            hidden,
            placed=True,
            scratch=[((part, units), BF16)], room=14)
    gate_grad, up_grad, two_mine, two_other = kernel_call(
        backward_kernel,
        [((tokens, units), BF16)] * 2 + [((half, width), BF16)] * 2,
        cot_mine,
        cot_other,
        gate_pre,
        up_pre,
        *down_parts,
        *near_parts,
        *far_parts,
        placed=True, room=30)

    two_came = flip(two_other, "row", 1)
    two_pieces = kernel_call(
        pack_tokens_kernel,
        [((share, width), BF16)] * cols,
        two_mine,
        two_came,
        placed=True,
        scratch=[((half, width), BF16)],
    )
    two_in = exchange(two_pieces)
    *first_pieces, feedforward_part = kernel_call(
        second_norm_kernel,
        [((share, width), BF16)] * cols + [((1, width), F32)],
        *two_in,
        first_share,
        cot_mine,
        *first_in,
        placed=True,
    )
    first_back = exchange(first_pieces)
    (first_half,) = kernel_call(
        join_tokens_kernel, [((half, width), BF16)], *first_back, placed=True
    )
    first_other = flip(first_half, "row", 1)

    def shifted(send, keep):
        came = flip(send, "dp", 1)
        rest = (keep[1].astype(F32) + came[1].astype(F32)).astype(BF16)
        return keep, came, flip(rest, "dp", 2)

    def scattered(split):
        return lax.psum_scatter(split, "dp", scatter_dimension=0, tiled=True)[0]

    if planes == 4:
        dealt = kernel_call(
            weight_grad_kernel,
            [((2, cols, rows, units), BF16)] * 4,
            normed_two,
            gate_grad,
            up_grad,
            placed=True,
            scratch=[((part, units), BF16)], room=20)
        dealt = list(down_dealt) + list(dealt)
        down_terms, gate_terms, up_terms = [
            shifted(dealt[2 * i], dealt[2 * i + 1])
            for i in range(3)
        ]
        feed_out = kernel_call(
            sum_feed_kernel,
            [((2 * rows, units), BF16)] * cols,
            *down_terms,
            *gate_terms,
            room=16,
        )
        up_out = kernel_call(
            sum_kernel, [((rows, units), BF16)] * cols, *up_terms, room=12
        )
    else:
        cot_all = jnp.concatenate([cot_mine, cot_other], axis=0)
        sums = [
            scattered(
                jnp.moveaxis(grad.astype(BF16).reshape(cols, planes, rows, units), 1, 0)
            )
            for grad in (
                matmul_tn(cot_all, hidden),
                matmul_tn(normed_two, gate_grad),
                matmul_tn(normed_two, up_grad),
            )
        ]
        feed_out = [jnp.concatenate([v[k] for v in sums[:2]], axis=0) for k in range(cols)]
        up_out = [sums[2][k] for k in range(cols)]
    feed_in = exchange(feed_out)
    down_share, gate_share = kernel_call(
        unpack_feed_kernel,
        [((rows, cols * units), F32)] * 2,
        *feed_in,
        placed=True,
        room=12,
    )

    up_in = exchange(up_out)
    (up_share,) = kernel_call(unpack_up_kernel, [((rows, cols * units), F32)], *up_in, placed=True)

    result_mine, result_other = kernel_call(
        result_kernel, [((half, width), BF16)] * 2, hidden, *down_parts, room=12)
    result_came = flip(result_other, "row", 1)
    result_pieces = kernel_call(
        pack_features_kernel, [((half, part), BF16)] * cols, result_mine, result_came
    )
    result_in = exchange(result_pieces)
    result_mine = (first_block + total(result_in)).astype(BF16)
    result_far = flip(result_mine, "row", 1)
    block_output = natural(jnp.concatenate([result_mine, result_far], axis=0))

    mixed_size = 3 * q_size
    if planes == 4:
        mixed_outs = [((2, cols, rows + 8, mixed_size), BF16)] * 2
    else:
        mixed_outs = [((cols, part, mixed_size), BF16), ((cols, 8, mixed_size), BF16)]
    one_mine, one_other, inner_part, mixed_first, mixed_second = kernel_call(
        attend_back_kernel,
        [((half, width), BF16), ((half, width), BF16), ((8, tokens), F32)] + mixed_outs,
        *common,
        qkv,
        turned,
        context,
        logs,
        first_half,
        first_other,
        second_in,
        feedforward_part,
        placed=True,
        scratch=[((part, mixed_size), BF16)], room=34)
    one_came = flip(one_other, "row", 1)
    inner_came = flip(inner_part[:, half:], "row", 1)
    one_pieces = kernel_call(
        pack_last_kernel,
        [((half + 16, part), BF16)] * cols,
        one_mine,
        one_came,
        inner_part,
        inner_came, room=10)
    one_in = exchange(one_pieces)
    one_grad = total([v[:half] for v in one_in])
    inner_one = jnp.sum(total([v[half:] for v in one_in])[:3], axis=0)[:, None]
    weighted_one = one_grad * gain_one[:part]
    own_input = input_mine.astype(F32)
    root_one = lax.rsqrt(jnp.mean(own_input * own_input, axis=1, keepdims=True) + EPSILON)
    normal_one = own_input[:, :part] * root_one
    input_mine_grad = first_half[:, :part].astype(F32) + root_one * (
        weighted_one - normal_one * inner_one
    )
    input_far_grad = flip(input_mine_grad, "row", 1)
    input_grad = natural(jnp.concatenate([input_mine_grad, input_far_grad], axis=0))

    if planes == 4:
        mixed_terms = shifted(mixed_first, mixed_second)
        last_out = kernel_call(sum_kernel, [((rows + 8, mixed_size), BF16)] * cols, *mixed_terms)
    else:
        lines = jnp.broadcast_to(mixed_second[:, None], (cols, planes, 8, mixed_size))
        blocks = mixed_first.reshape(cols, planes, rows, mixed_size)
        mixed_sum = scattered(jnp.moveaxis(jnp.concatenate([blocks, lines], axis=2), 1, 0))
        last_out = [mixed_sum[k] for k in range(cols)]
    last_in = exchange(last_out)
    query_share, key_share, value_share, output_share, gain_sums = kernel_call(
        unpack_last_kernel,
        [
            ((rows, cols * q_size), F32),
            ((rows, cols * head), F32),
            ((rows, cols * head), F32),
            ((rows, cols * q_size), F32),
            ((8, mixed_size), F32),
        ],
        *last_in,
        placed=True,
    )
    gain_came = flip(gain_sums, "row", 1)
    if planes == 4:
        attention_share, feedforward_share, query_gain_grad, key_gain_grad = [
            v.reshape(-1)
            for v in kernel_call(
                gain_kernel,
                [((1, rows), F32), ((1, rows), F32), ((1, head), F32), ((1, head), F32)],
                gain_sums,
                gain_came,
                placed=True,
            )
        ]
    else:
        gain_sums = gain_sums + gain_came
        attention_share = lax.dynamic_slice_in_dim(gain_sums[0], plane * rows, rows, 0)
        feedforward_share = lax.dynamic_slice_in_dim(gain_sums[1], plane * rows, rows, 0)
        query_gain_grad = gain_sums[0, 2 * q_size : 2 * q_size + head]
        key_gain_grad = gain_sums[0, 2 * q_size + head :]
    return (
        block_output,
        input_grad,
        attention_share,
        query_share,
        key_share,
        value_share,
        query_gain_grad,
        key_gain_grad,
        output_share.T,
        feedforward_share,
        gate_share,
        up_share,
        down_share.T,
    )


def solution(mesh):
    placed = (
        P("dp", "col"),
        P("dp"),
        P("dp"),
        P("col"),
        P("col", "row"),
        P("col", "row"),
        P("col", "row"),
        P(),
        P(),
        P("row", "col"),
        P("col"),
        P("col", "row"),
        P("col", "row"),
        P("row", "col"),
        P("dp", "col"),
    )


    return jax.shard_map(
        body,
        mesh=mesh,
        in_specs=placed,
        out_specs=(
            P("dp", "col"),
            P("dp", "col"),
            P(("col", "dp")),
            P(("col", "dp"), "row"),
            P(("col", "dp"), "row"),
            P(("col", "dp"), "row"),
            P(),
            P(),
            P("row", ("col", "dp")),
            P(("col", "dp")),
            P(("col", "dp"), "row"),
            P(("col", "dp"), "row"),
            P("row", ("col", "dp")),
        ),
        check_vma=False,
    )
```
